32 devices in a mesh: dp: 8 (over z, x), sp: 4 (over y, core).
Axes of the slice: x: 2, y: 2, z: 4, core: 2. Of those that a mesh axis runs over, the one named last changes fastest.
Arguments:
- hidden_in: bfloat16 [8, 1024, 512], P('dp', 'sp'), may hold values from -6 to 6
- cotangent: float32 [8, 1024, 512], P('dp', 'sp'), may hold values from -6 to 6
- lengths: int32 [8], P('dp'), may hold values from 256 to 1024, as said below
- master: float32 [6301696], P(('dp', 'sp'))
- moment_one: float32 [6301696], P(('dp', 'sp'))
- moment_two: float32 [6301696], P(('dp', 'sp'))
Outputs:
- output: float32 [8, 1024, 512], P('dp', 'sp')
- input_grad: float32 [8, 1024, 512], P('dp', 'sp')
- new_master: float32 [6301696], P(('dp', 'sp'))
- new_moment_one: float32 [6301696], P(('dp', 'sp'))
- new_moment_two: float32 [6301696], P(('dp', 'sp'))
- new_weights: bfloat16 [6301696], P(('dp', 'sp'))
- grad_norm: float32 [], replicated
- gains_grad: float32 [2, 2, 512], replicated
The draws below stay inside these ranges and needn't reach their ends.
Inputs may be any that keep to these rules, and one draw needn't show every extreme that they name: `lengths`: in every draw one sequence has all 1024 tokens real and another only 256.
All inputs are finite; a program needn't handle non-finite values.
Results may differ from the reference program's by a relative error of at most 0.017.
Values may be sent and summed in bfloat16 or wider, within the bound.
A program may use at most 192 MiB of HBM per device.

```python
import jax
import jax.numpy as jnp
from jax import lax

D = 512
HEADS = 8
HEAD_DIM = 64
FF = 1368
SEQ = 1024
STEP = 5
SEQS = 8
LAYER_PARAMS = 3150848
NPARAM = 6301696


def matrix_scale(places):
    within = places % LAYER_PARAMS
    bound_qkv = 3 * D * D
    bound_out = bound_qkv + D * D
    bound_gu = bound_out + 2 * D * FF
    bound_down = bound_gu + FF * D
    scale_rows = jnp.where(within < bound_qkv, D ** (-0.5), jnp.where(within < bound_out, 3.0 * D ** (-0.5), jnp.where(within < bound_gu, D ** (-0.5), FF ** (-0.5))))
    is_gain = within >= bound_down
    return (scale_rows.astype(jnp.float32), is_gain)


def draw_lengths(key, part):
    first_key, second_key, third_key = jax.random.split(key, 3)
    values = jax.random.randint(first_key, (SEQS,), SEQ // 4, SEQ + 1)
    longest = jax.random.randint(second_key, (), 0, SEQS)
    shortest = (longest + 1 + jax.random.randint(third_key, (), 0, SEQS - 1)) % SEQS
    places = jnp.arange(SEQS)
    values = jnp.where(places == longest, SEQ, values)
    values = jnp.where(places == shortest, SEQ // 4, values)
    return values.astype(jnp.int32)


def draw_master(key, part):
    places = jnp.arange(NPARAM)
    scale_rows, is_gain = matrix_scale(places)
    first_key, second_key = jax.random.split(key)
    standard = jax.random.normal(first_key, (NPARAM,), jnp.float32)
    gain_values = jax.random.uniform(second_key, (NPARAM,), jnp.float32, 0.6, 1.4)
    return jnp.where(is_gain, gain_values, standard * scale_rows)


def draw_moment_one(key, part):
    places = jnp.arange(NPARAM)
    scale_rows, is_gain = matrix_scale(places)
    typical = NPARAM ** (-0.5)
    factor = jnp.where(is_gain, 4.0, 1.0) * typical
    standard = jax.random.normal(key, (NPARAM,), jnp.float32)
    return standard * factor


def draw_moment_two(key, part):
    places = jnp.arange(NPARAM)
    scale_rows, is_gain = matrix_scale(places)
    typical = NPARAM ** (-0.5)
    factor = jnp.where(is_gain, 4.0, 1.0) * typical
    spread = 2.0 * jnp.exp(jax.random.uniform(key, (NPARAM,), jnp.float32, -0.6931472, 0.6931472))
    return spread * factor * factor


def shard_levels(stream_key, shape, cuts, low, top_value):
    loudness, own = 1.0, jax.random.fold_in(stream_key, 6)
    for axis_at, parts in cuts:
        steps = jnp.exp(jax.random.uniform(jax.random.fold_in(own, axis_at), (parts,), jnp.float32, low / len(cuts), top_value / len(cuts)))
        loudness = loudness * jnp.repeat(steps, shape[axis_at] // parts).reshape([-1 if axis == axis_at else 1 for axis in range(len(shape))])
    return loudness


def gaussian(own_key, extent, scale, limit, cuts=(), kind=jnp.bfloat16):
    result = scale * jax.random.normal(own_key, extent, jnp.float32)
    if cuts:
        result = result * shard_levels(own_key, extent, cuts, -0.22, 0.18)
    return jnp.clip(result, -limit, limit).astype(kind)


def setup_inputs(seed: int = 0) -> dict:
    seeds = jax.random.split(jax.random.key(seed), 7)
    hidden_in = gaussian(seeds[0], (SEQS, SEQ, D), 1.0, 6.0, ((0, 8), (1, 4)))
    cotangent = gaussian(seeds[1], (SEQS, SEQ, D), 1.0, 6.0, ((0, 8), (1, 4)), jnp.float32)
    lengths = draw_lengths(jax.random.fold_in(seeds[6], 71), 0)
    master = draw_master(jax.random.fold_in(seeds[6], 71), 0)
    moment_one = draw_moment_one(jax.random.fold_in(seeds[6], 71), 0)
    moment_two = draw_moment_two(jax.random.fold_in(seeds[6], 71), 0)
    return {"hidden_in": hidden_in, "cotangent": cotangent, "lengths": lengths, "master": master, "moment_one": moment_one, "moment_two": moment_two}


@jax.custom_vjp
def low(v):
    return lax.optimization_barrier(v.astype(jnp.bfloat16)).astype(jnp.float32)

@jax.custom_vjp
def low_back(v):
    return v

def low_keep(v):
    return (low(v), None)

def low_pass(kept, grad):
    return (grad,)

def back_keep(v):
    return (v, None)

def back_low(kept, grad):
    return (low(grad),)
low.defvjp(low_keep, low_pass)
low_back.defvjp(back_keep, back_low)
NORM_EPS = 1e-06
ADAM_EPS = 1e-08
LEARN_RATE = 0.02
DECAY_RATE = 0.01
HIGHEST = lax.Precision.HIGHEST

def rope_tables(positions):
    half_dim = HEAD_DIM // 2
    frequency = jnp.exp(-jnp.log(10000.0) * jnp.arange(half_dim).astype(jnp.float32) * 2.0 / HEAD_DIM)
    angles = positions.astype(jnp.float32)[:, None] * frequency[None, :]
    return (jnp.cos(angles), jnp.sin(angles))

def rotate(values, cosine_table, sine_table):
    half_dim = values.shape[-1] // 2
    first_half = values[..., :half_dim]
    second_half = values[..., half_dim:]
    cos_rows = cosine_table[:, None, :]
    sin_rows = sine_table[:, None, :]
    return jnp.concatenate([first_half * cos_rows - second_half * sin_rows, second_half * cos_rows + first_half * sin_rows], axis=-1)

def rms_norm(stream, gain):
    return stream * lax.rsqrt(lax.optimization_barrier(jnp.mean(stream * stream, axis=-1, keepdims=True)) + NORM_EPS) * gain

def layer_pieces(flat_weights, layer_index):
    shapes = [(D, 3 * D), (D, D), (D, 2 * FF), (FF, D), (2, D)]
    offset = layer_index * LAYER_PARAMS
    pieces = []
    for dims_pair in shapes:
        length_now = dims_pair[0] * dims_pair[1]
        pieces.append(flat_weights[offset:offset + length_now].reshape(dims_pair))
        offset = offset + length_now
    return pieces

def attend(packed_in):
    queries, key_rows, value_rows, length_now = packed_in
    raw_scores = low_back(jnp.einsum('qhd,khd->hqk', queries, key_rows, precision=HIGHEST))
    row_place = jnp.arange(SEQ)[:, None]
    col_place = jnp.arange(SEQ)[None, :]
    allowed = (col_place <= row_place) & (col_place < length_now)
    logits = jnp.where(allowed[None], raw_scores * HEAD_DIM ** (-0.5), -1000000000.0)
    weights_soft = low(jax.nn.softmax(logits, axis=-1))
    return jnp.einsum('hqk,khd->qhd', weights_soft, value_rows, precision=HIGHEST)

def forward(hidden, flat_master, lengths):
    weights = low(flat_master)
    seq_count = hidden.shape[0]
    cosine_table, sine_table = rope_tables(jnp.arange(SEQ))

    def attention_branch(stream, weight_qkv, weight_out):
        inputs_low = low(stream).reshape(-1, D)
        projected = low_back(jnp.dot(inputs_low, weight_qkv, precision=HIGHEST)).reshape(seq_count, SEQ, 3, HEADS, HEAD_DIM)
        queries = low_back(low(rotate(projected[:, :, 0], cosine_table, sine_table)))
        key_rows = low_back(low(rotate(projected[:, :, 1], cosine_table, sine_table)))
        value_rows = low_back(low(projected[:, :, 2]))
        context = lax.map(jax.checkpoint(attend), (queries, key_rows, value_rows, lengths))
        context = low_back(low(context)).reshape(-1, D)
        return low_back(jnp.dot(context, weight_out, precision=HIGHEST)).reshape(seq_count, SEQ, D)

    def ffn_branch(stream, weight_gu, weight_down):
        inputs_low = low(stream).reshape(-1, D)
        both_parts = low_back(jnp.dot(inputs_low, weight_gu, precision=HIGHEST))
        gate_part = both_parts[:, :FF]
        up_part = both_parts[:, FF:]
        units = low(jax.nn.silu(gate_part) * up_part)
        return low_back(jnp.dot(units, weight_down, precision=HIGHEST)).reshape(seq_count, SEQ, D)
    first_weights = layer_pieces(weights, 0)
    second_weights = layer_pieces(weights, 1)
    resid_one = hidden + attention_branch(hidden, first_weights[0], first_weights[1])
    stream_one = rms_norm(resid_one, first_weights[4][0])
    resid_two = stream_one + ffn_branch(stream_one, first_weights[2], first_weights[3])
    stream_two = rms_norm(resid_two, first_weights[4][1])
    stream_three = stream_two + attention_branch(rms_norm(stream_two, second_weights[4][0]), second_weights[0], second_weights[1])
    return stream_three + ffn_branch(rms_norm(stream_three, second_weights[4][1]), second_weights[2], second_weights[3])

def reference(hidden_in, cotangent, lengths, master, moment_one, moment_two):
    group_count = SEQS // 4
    hidden_groups = hidden_in.astype(jnp.float32).reshape(group_count, 4, SEQ, D)
    keep = (jnp.arange(SEQ)[None, :] < lengths[:, None]).astype(jnp.float32)
    upstream = (cotangent * keep[:, :, None]).reshape(group_count, 4, SEQ, D)
    length_groups = lengths.reshape(group_count, 4)

    def visit(carried, inputs_all):
        hidden_group, upstream_group, length_group = inputs_all
        output_group, pullback = jax.vjp(lambda hidden, params: forward(hidden, params, length_group), hidden_group, master)
        input_group, weight_grad = pullback(upstream_group)
        return (carried + weight_grad, (output_group, input_group))
    grad_flat, (outputs, input_grads) = lax.scan(visit, jnp.zeros(master.shape, jnp.float32), (hidden_groups, upstream, length_groups))
    gains_start = LAYER_PARAMS - 2 * D
    gains_grad = jnp.stack([grad_flat[gains_start:gains_start + 2 * D].reshape(2, D), grad_flat[LAYER_PARAMS + gains_start:LAYER_PARAMS + gains_start + 2 * D].reshape(2, D)])
    grad_norm = jnp.sqrt(jnp.sum(grad_flat * grad_flat))
    clipped = grad_flat * jnp.minimum(1.0, 1.0 / grad_norm)
    new_one = 0.5 * moment_one + 0.5 * clipped
    new_two = 0.5 * moment_two + 0.5 * clipped * clipped
    correction = 1.0 - 0.5 ** STEP
    new_master = master * (1.0 - LEARN_RATE * DECAY_RATE) - LEARN_RATE * (new_one / correction) / (jnp.sqrt(new_two / correction) + ADAM_EPS)
    output = outputs.reshape(SEQS, SEQ, D)
    input_grad = input_grads.reshape(SEQS, SEQ, D)
    return (output, input_grad, new_master, new_one, new_two, new_master.astype(jnp.bfloat16), grad_norm, gains_grad)
```

```python
import functools

import jax
import jax.numpy as jnp
from jax import lax
from jax.experimental import pallas as pl
from jax.experimental.pallas import tpu as pltpu
from jax.sharding import PartitionSpec as P

D = 512
HEADS = 8
HEAD_DIM = 64
FF = 1368
FFP = 1408
TILES = 11
STEP = 5
NORM_EPS = 1e-06
ADAM_EPS = 1e-08
LEARN_RATE = 0.02
DECAY_RATE = 0.01
LANES = 128
LAYER_ROWS = 24616
BASE_OUT = 6144
BASE_GU = 8192
BASE_DOWN = 19136
BASE_GAINS = 24608
GU_ROW = 2 * FF
PERIOD = 171
MESH = pl.DeviceIdType.MESH
MIB = 1 << 20
f32 = jnp.float32
bf16 = jnp.bfloat16


def mm(a, b):
    return lax.dot_general(a, b, (((1,), (0,)), ((), ())), preferred_element_type=f32)


def mm_nt(a, b):
    return lax.dot_general(a, b, (((1,), (1,)), ((), ())), preferred_element_type=f32)


def mm_tn(a, b):
    return lax.dot_general(a, b, (((0,), (0,)), ((), ())), preferred_element_type=f32)


def chunk_rows(rows):
    tiles = rows // 16
    best = max(d for d in range(1, 17) if tiles % d == 0)
    return best * 16


def vmem_spec():
    return pl.BlockSpec(memory_space=pltpu.VMEM)


def any_spec():
    return pl.BlockSpec(memory_space=pl.ANY)


def local_call(body, outs, ins, scratch=(), limit=60, flops=0):
    return pl.pallas_call(
        body,
        out_shape=[jax.ShapeDtypeStruct(s, d) for s, d in outs],
        in_specs=[vmem_spec()] * len(ins),
        out_specs=[vmem_spec()] * len(outs),
        scratch_shapes=list(scratch),
        compiler_params=pltpu.CompilerParams(vmem_limit_bytes=limit * MIB),
    )(*ins)


def coords():
    dp = lax.axis_index("dp")
    sp = lax.axis_index("sp")
    return lax.div(dp, 2), lax.rem(dp, 2), lax.div(sp, 2), lax.rem(sp, 2)


def place(z, x, y, c):
    return {"dp": z * 2 + x, "sp": y * 2 + c}


def remote(src, dst, send_sem, recv_sem, device):
    return pltpu.make_async_remote_copy(
        src_ref=src,
        dst_ref=dst,
        send_sem=send_sem,
        recv_sem=recv_sem,
        device_id=device,
        device_id_type=MESH,
    )


def order_at(tau, z):
    step = lax.div(tau + 1, 2)
    return z + jnp.where(lax.rem(tau, 2) == 1, -step, step)


def gather_weights(master_pad, zn, rows, share, zlo, zhi):
    nz = zhi - zlo
    half = rows // 2
    step = chunk_rows(rows)

    def body(x_ref, out_ref, own, send, recv, lsem):
        z, x, y, c = coords()
        bar = pltpu.get_barrier_semaphore()

        def hello(device):
            pl.semaphore_signal(bar, inc=1, device_id=device, device_id_type=MESH)

        hello(place(z, 1 - x, y, c))
        hello(place(z, x, 1 - y, c))
        hello(place(z, x, y, 1 - c))
        pl.when(z > 0)(lambda: hello(place(z - 1, x, y, c)))
        pl.when(z < zn - 1)(lambda: hello(place(z + 1, x, y, c)))

        shift = lax.rem(share * (((z * 2 + x) * 2 + y) * 2 + c), LANES)
        lane = lax.broadcasted_iota(jnp.int32, (step, LANES), 1)

        def align(i, carry):
            now = pltpu.roll(x_ref[pl.ds(8 + i * step, step), :], shift, 1)
            before = pltpu.roll(x_ref[pl.ds(7 + i * step, step), :], shift, 1)
            own[pl.ds(i * step, step), :] = jnp.where(lane >= shift, now, before).astype(bf16)
            return carry

        lax.fori_loop(0, rows // step, align, 0)
        pl.semaphore_wait(
            bar, 3 + (z > 0).astype(jnp.int32) + (z < zn - 1).astype(jnp.int32)
        )

        def slot(zp, xp, yp, cp):
            return (((zp - zlo) * 2 + xp) * 2 + yp) * 2 + cp

        def whole(zp, xp, yp):
            return out_ref.at[slot(zp, xp, yp, c)]

        def upper(zp, xp, yp):
            return out_ref.at[slot(zp, xp, yp, c), pl.ds(0, half)]

        def lower(zp, xp, yp):
            return out_ref.at[slot(zp, xp, yp, c), pl.ds(half, half)]

        to_x = place(z, 1 - x, y, c)
        to_y = place(z, x, 1 - y, c)
        to_c = place(z, x, y, 1 - c)

        def cp(ref, zp, s, r, device):
            return remote(ref, ref, send.at[zp - zlo, s], recv.at[zp - zlo, r], device)

        def right(zp):
            return cp(whole(zp, x, y), zp, 0, 0, place(z + 1, x, y, c))

        def left(zp):
            return cp(whole(zp, x, y), zp, 1, 0, place(z - 1, x, y, c))

        def first(zp):
            ref = whole(zp, x, y)
            return [cp(ref, zp, 2, 1, to_x), cp(ref, zp, 3, 2, to_y), cp(ref, zp, 4, 3, to_c)]

        def second_x(zp):
            return [
                cp(upper(zp, 1 - x, y), zp, 5, 4, to_y),
                cp(whole(zp, 1 - x, y), zp, 6, 6, to_c),
            ]

        def second_y(zp):
            return [
                cp(lower(zp, x, 1 - y), zp, 7, 5, to_x),
                cp(whole(zp, x, 1 - y), zp, 8, 7, to_c),
            ]

        def third_a(zp):
            return cp(upper(zp, 1 - x, 1 - y), zp, 9, 8, to_c)

        def third_b(zp):
            return cp(lower(zp, 1 - x, 1 - y), zp, 10, 9, to_c)

        def arrival(ref, zp, r):
            cp(ref, zp, 0, r, to_c).wait_recv()

        mine = (z >= zlo) & (z < zhi)

        @pl.when(mine)
        def _():
            keep = pltpu.make_async_copy(own, whole(z, x, y), lsem)
            keep.start()
            keep.wait()

        def valid(zp):
            return (zp >= zlo) & (zp < zhi)

        def stage_one(tau):
            zp = order_at(tau, z)

            @pl.when(valid(zp))
            def _():
                pl.when(tau > 0)(lambda: arrival(whole(zp, x, y), zp, 0))
                pl.when((zp <= z) & (z < zn - 1))(lambda: right(zp).start())
                pl.when((zp >= z) & (z > 0))(lambda: left(zp).start())
                for item in first(zp):
                    item.start()

        def stage_two(tau):
            zp = order_at(tau, z)

            @pl.when((tau >= 0) & valid(zp))
            def _():
                arrival(whole(zp, 1 - x, y), zp, 1)
                for item in second_x(zp):
                    item.start()
                arrival(whole(zp, x, 1 - y), zp, 2)
                for item in second_y(zp):
                    item.start()

        def stage_three(tau):
            zp = order_at(tau, z)

            @pl.when((tau >= 0) & valid(zp))
            def _():
                arrival(upper(zp, 1 - x, 1 - y), zp, 4)
                third_a(zp).start()
                arrival(lower(zp, 1 - x, 1 - y), zp, 5)
                third_b(zp).start()

        total = 2 * zn - 1

        def turn(tau, carry):
            pl.when(tau < total)(lambda: stage_one(tau))
            pl.when(tau - 1 < total)(lambda: stage_two(tau - 1))
            stage_three(tau - 2)
            return carry

        lax.fori_loop(0, total + 2, turn, 0)

        def finish(i, carry):
            zp = zlo + i
            pl.when((zp <= z) & (z < zn - 1))(lambda: right(zp).wait_send())
            pl.when((zp >= z) & (z > 0))(lambda: left(zp).wait_send())
            for item in first(zp) + second_x(zp) + second_y(zp) + [third_a(zp), third_b(zp)]:
                item.wait_send()
            far = 1 - c
            arrival(out_ref.at[slot(zp, x, y, far)], zp, 3)
            arrival(out_ref.at[slot(zp, 1 - x, y, far)], zp, 6)
            arrival(out_ref.at[slot(zp, x, 1 - y, far)], zp, 7)
            arrival(out_ref.at[slot(zp, 1 - x, 1 - y, far), pl.ds(0, half)], zp, 8)
            arrival(out_ref.at[slot(zp, 1 - x, 1 - y, far), pl.ds(half, half)], zp, 9)
            return carry

        lax.fori_loop(0, nz, finish, 0)

    return pl.pallas_call(
        body,
        out_shape=jax.ShapeDtypeStruct((nz * 8, rows, LANES), bf16),
        in_specs=[vmem_spec()],
        out_specs=any_spec(),
        scratch_shapes=[
            pltpu.VMEM((rows, LANES), bf16),
            pltpu.SemaphoreType.DMA((nz, 11)),
            pltpu.SemaphoreType.DMA((nz, 10)),
            pltpu.SemaphoreType.DMA,
        ],
        compiler_params=pltpu.CompilerParams(
            collective_id=1, has_side_effects=True, vmem_limit_bytes=40 * MIB
        ),
    )(master_pad)


def unpack_weights(slots, layer, rows, share):
    per_layer = slots.shape[0] // 2
    step = chunk_rows(rows)
    depth = LAYER_ROWS + rows

    def body(s_ref, qkv_ref, out_ref, gu_ref, down_ref, gains_ref, flat, gate_up):
        i = pl.program_id(0)
        start = lax.div(share * i, LANES)
        shift = lax.rem(share * i, LANES)
        edge = flat[pl.ds(start, 1), :]

        def fill(j, carry):
            flat[pl.ds(start + j * step, step), :] = s_ref[0, pl.ds(j * step, step), :].astype(f32)
            return carry

        lax.fori_loop(0, rows // step, fill, 0)

        @pl.when(shift > 0)
        def _():
            flat[pl.ds(start, 1), :] = flat[pl.ds(start, 1), :] + edge

        @pl.when(i == per_layer - 1)
        def _():
            for col in range(12):
                qkv_ref[:, 128 * col : 128 * col + 128] = flat[
                    pl.ds(col, D, stride=12), :
                ].astype(bf16)
            for col in range(4):
                out_ref[:, 128 * col : 128 * col + 128] = flat[
                    pl.ds(BASE_OUT + col, D, stride=4), :
                ].astype(bf16)
                down_ref[0:FF, 128 * col : 128 * col + 128] = flat[
                    pl.ds(BASE_DOWN + col, FF, stride=4), :
                ].astype(bf16)
                gains_ref[:, 128 * col : 128 * col + 128] = flat[
                    pl.ds(BASE_GAINS + col, 2, stride=4), :
                ]
            down_ref[FF:FFP, :] = jnp.zeros((FFP - FF, D), bf16)
            lane = lax.broadcasted_iota(jnp.int32, (64, LANES), 1)
            for r in range(8):
                for part in range(2):
                    for tile in range(TILES):
                        first = GU_ROW * r + FF * part + LANES * tile
                        q, s = first // LANES, first % LANES
                        value = flat[pl.ds(BASE_GU + q, 64, stride=PERIOD), :]
                        if s:
                            after = flat[pl.ds(BASE_GU + q + 1, 64, stride=PERIOD), :]
                            value = jnp.where(
                                lane < LANES - s,
                                pltpu.roll(value, LANES - s, 1),
                                pltpu.roll(after, LANES - s, 1),
                            )
                        if tile == TILES - 1:
                            value = jnp.where(lane < FF - LANES * tile, value, 0.0)
                        gate_up[2 * tile + part, pl.ds(r, 64, stride=8), :] = value
            for k in range(2 * TILES):
                gu_ref[:, 128 * k : 128 * k + 128] = gate_up[k].astype(bf16)

    shapes = [
        ((D, 3 * D), bf16),
        ((D, D), bf16),
        ((D, 2 * FFP), bf16),
        ((FFP, D), bf16),
        ((2, D), f32),
    ]
    return pl.pallas_call(
        body,
        grid=(per_layer,),
        out_shape=[jax.ShapeDtypeStruct(s, d) for s, d in shapes],
        in_specs=[pl.BlockSpec((1, rows, LANES), lambda i: (layer * per_layer + i, 0, 0))],
        out_specs=[pl.BlockSpec(s, lambda i: (0, 0)) for s, _ in shapes],
        scratch_shapes=[pltpu.VMEM((depth, LANES), f32), pltpu.VMEM((2 * TILES, D, LANES), f32)],
        compiler_params=pltpu.CompilerParams(vmem_limit_bytes=60 * MIB),
    )(slots)


def gate_up_segments(q):
    pieces = []
    place_now = LANES * q
    end = place_now + LANES
    while place_now < end:
        r, within = divmod(place_now, GU_ROW)
        part, unit = divmod(within, FF)
        tile, lane_src = divmod(unit, LANES)
        room = min(end - place_now, FF - unit, LANES - lane_src)
        lane_dst = place_now - LANES * q
        pieces.append((r, 2 * tile + part, lane_dst, lane_dst + room, (lane_dst - lane_src) % LANES))
        place_now += room
    return pieces


def weight_grads(a_low, e_lin, ctx, e_attn, b_low, e_both, units, e_ffn, gains, rows, share, per_layer):
    step = chunk_rows(rows)
    depth = LAYER_ROWS + rows

    def body(a_ref, lin_ref, ctx_ref, ea_ref, b_ref, both_ref, u_ref, ef_ref, g_ref, s_ref, flat, gate_up):
        i = pl.program_id(0)

        @pl.when(i == 0)
        def _():
            for t in range(6):
                value = mm_tn(a_ref[...], lin_ref[:, 256 * t : 256 * t + 256])
                for k in range(2):
                    flat[pl.ds(2 * t + k, D, stride=12), :] = value[:, 128 * k : 128 * k + 128]
            for t in range(2):
                value = mm_tn(ctx_ref[...], ea_ref[:, 256 * t : 256 * t + 256])
                for k in range(2):
                    flat[pl.ds(BASE_OUT + 2 * t + k, D, stride=4), :] = value[
                        :, 128 * k : 128 * k + 128
                    ]
                value = mm_tn(u_ref[...], ef_ref[:, 256 * t : 256 * t + 256])
                for k in range(2):
                    flat[pl.ds(BASE_DOWN + 2 * t + k, FF, stride=4), :] = value[
                        0:FF, 128 * k : 128 * k + 128
                    ]
            for t in range(TILES):
                value = mm_tn(b_ref[...], both_ref[:, 256 * t : 256 * t + 256])
                for k in range(2):
                    gate_up[2 * t + k] = value[:, 128 * k : 128 * k + 128]
            for col in range(4):
                flat[pl.ds(BASE_GAINS + col, 2, stride=4), :] = g_ref[:, 128 * col : 128 * col + 128]
            lane = lax.broadcasted_iota(jnp.int32, (64, LANES), 1)
            for q in range(PERIOD):
                value = None
                for r, k, low, high, turn in gate_up_segments(q):
                    piece = gate_up[k, pl.ds(r, 64, stride=8), :]
                    if turn:
                        piece = pltpu.roll(piece, turn, 1)
                    value = piece if value is None else jnp.where(lane < low, value, piece)
                flat[pl.ds(BASE_GU + q, 64, stride=PERIOD), :] = value
            flat[LAYER_ROWS:depth, :] = jnp.zeros((depth - LAYER_ROWS, LANES), f32)

        start = lax.div(share * i, LANES)

        def fill(j, carry):
            s_ref[0, pl.ds(j * step, step), :] = flat[pl.ds(start + j * step, step), :].astype(bf16)
            return carry

        lax.fori_loop(0, rows // step, fill, 0)

    ins = [a_low, e_lin, ctx, e_attn, b_low, e_both, units, e_ffn, gains]
    return pl.pallas_call(
        body,
        grid=(per_layer,),
        out_shape=jax.ShapeDtypeStruct((per_layer, rows, LANES), bf16),
        in_specs=[pl.BlockSpec(v.shape, lambda i: (0, 0)) for v in ins],
        out_specs=pl.BlockSpec((1, rows, LANES), lambda i: (i, 0, 0)),
        scratch_shapes=[pltpu.VMEM((depth, LANES), f32), pltpu.VMEM((2 * TILES, D, LANES), f32)],
        compiler_params=pltpu.CompilerParams(vmem_limit_bytes=60 * MIB),
    )(*ins)


def exchange_keys(kv):
    rows, width = kv.shape
    parts = 4
    piece = rows // parts

    def body(kv_ref, all_ref, send, recv, lsem):
        z, x, y, c = coords()
        bar = pltpu.get_barrier_semaphore()
        to_y = place(z, x, 1 - y, c)
        to_c = place(z, x, y, 1 - c)
        for device in (to_y, to_c):
            pl.semaphore_signal(bar, inc=1, device_id=device, device_id_type=MESH)
        pl.semaphore_wait(bar, 2)
        mine = y * 2 + c
        beyond = (1 - y) * 2 + c
        keep = pltpu.make_async_copy(kv_ref, all_ref.at[mine], lsem)
        keep.start()

        def part(ref, k):
            return ref.at[pl.ds(k * piece, piece)]

        own_y, own_c, pass_c = [], [], []
        for k in range(parts):
            src, dst = part(kv_ref, k), part(all_ref.at[mine], k)
            own_y.append(remote(src, dst, send.at[0, k], recv.at[0, k], to_y))
            own_c.append(remote(src, dst, send.at[1, k], recv.at[1, k], to_c))
            ref = part(all_ref.at[beyond], k)
            pass_c.append(remote(ref, ref, send.at[2, k], recv.at[2, k], to_c))
        for k in range(parts):
            own_y[k].start()
        for k in range(parts):
            own_c[k].start()
        for k in range(parts):
            own_y[k].wait_recv()
            pass_c[k].start()
        for k in range(parts):
            own_c[k].wait_recv()
            pass_c[k].wait_recv()
        for item in own_y + own_c + pass_c:
            item.wait_send()
        keep.wait()

    return pl.pallas_call(
        body,
        out_shape=jax.ShapeDtypeStruct((4, rows, width), kv.dtype),
        in_specs=[vmem_spec()],
        out_specs=vmem_spec(),
        scratch_shapes=[
            pltpu.SemaphoreType.DMA((3, parts)),
            pltpu.SemaphoreType.DMA((3, parts)),
            pltpu.SemaphoreType.DMA,
        ],
        compiler_params=pltpu.CompilerParams(
            collective_id=2, has_side_effects=True, vmem_limit_bytes=32 * MIB
        ),
    )(kv)


def collect_keys(dkv):
    blocks, rows, width = dkv.shape
    parts = 4
    piece = rows // parts

    def body(g_ref, sum_ref, from_c, pair, from_y, send, recv):
        z, x, y, c = coords()
        bar = pltpu.get_barrier_semaphore()
        to_y = place(z, x, 1 - y, c)
        to_c = place(z, x, y, 1 - c)
        for device in (to_y, to_c):
            pl.semaphore_signal(bar, inc=1, device_id=device, device_id_type=MESH)
        pl.semaphore_wait(bar, 2)
        mine = y * 2 + c
        beyond = (1 - y) * 2 + c

        def part(ref, k):
            return ref.at[pl.ds(k * piece, piece)]

        near, wide = [], []
        for h, row in ((0, 1 - y), (1, y)):
            src = g_ref.at[row * 2 + 1 - c]
            near.append(
                [
                    remote(part(src, k), part(from_c.at[h], k), send.at[h, k], recv.at[h, k], to_c)
                    for k in range(parts)
                ]
            )
        for k in range(parts):
            wide.append(remote(part(pair, k), part(from_y, k), send.at[2, k], recv.at[2, k], to_y))
        for group in near:
            for item in group:
                item.start()
        for k in range(parts):
            span = pl.ds(k * piece, piece)
            near[0][k].wait_recv()
            pair[span, :] = (
                from_c[0, span, :].astype(f32) + g_ref[beyond, span, :].astype(f32)
            ).astype(bf16)
            wide[k].start()
        for k in range(parts):
            span = pl.ds(k * piece, piece)
            near[1][k].wait_recv()
            wide[k].wait_recv()
            sum_ref[span, :] = (
                from_c[1, span, :].astype(f32)
                + g_ref[mine, span, :].astype(f32)
                + from_y[span, :].astype(f32)
            ).astype(bf16)
        for item in near[0] + near[1] + wide:
            item.wait_send()

    return pl.pallas_call(
        body,
        out_shape=jax.ShapeDtypeStruct((rows, width), bf16),
        in_specs=[vmem_spec()],
        out_specs=vmem_spec(),
        scratch_shapes=[
            pltpu.VMEM((2, rows, width), bf16),
            pltpu.VMEM((rows, width), bf16),
            pltpu.VMEM((rows, width), bf16),
            pltpu.SemaphoreType.DMA((3, parts)),
            pltpu.SemaphoreType.DMA((3, parts)),
        ],
        compiler_params=pltpu.CompilerParams(
            collective_id=3, has_side_effects=True, vmem_limit_bytes=32 * MIB
        ),
    )(dkv)


def half_swap(u):
    lane = lax.broadcasted_iota(jnp.int32, u.shape, 1)
    return jnp.where(lax.rem(lane, 64) < 32, pltpu.roll(u, 96, 1), pltpu.roll(u, 32, 1))


def project_heads(a_low, w_ref, cos_ref, sin_ref, q_ref, kv_ref):
    for t in range(6):
        lin = mm(a_low, w_ref[:, 256 * t : 256 * t + 256])
        for k in range(2):
            u = lin[:, 128 * k : 128 * k + 128]
            if t < 4:
                u = u * cos_ref[...] + half_swap(u) * sin_ref[...]
            col = 256 * t + 128 * k
            if col < D:
                q_ref[:, col : col + 128] = u.astype(bf16)
            else:
                kv_ref[:, col - D : col - D + 128] = u.astype(bf16)


def norm_factor(r):
    return lax.rsqrt(jnp.mean(r * r, axis=-1, keepdims=True) + NORM_EPS)


def norm_back(e, r, f, g):
    scaled = e * g
    gain = jnp.sum(e * r * f, axis=0, keepdims=True)
    grad = f * scaled - r * (f * f * f) * jnp.mean(scaled * r, axis=-1, keepdims=True)
    return grad, gain


def head_mask(rows, h):
    lane = lax.broadcasted_iota(jnp.int32, (rows, LANES), 1)
    return (lane >= 64) if h else (lane < 64)


def make_bias(bias, length):
    rows, cols = bias.shape
    first = lax.axis_index("sp") * rows
    row = lax.broadcasted_iota(jnp.int32, (rows, cols), 0) + first
    col = lax.broadcasted_iota(jnp.int32, (rows, cols), 1)
    bias[...] = jnp.where((col <= row) & (col < length), 0.0, -1e9)


def attend(q_ref, kv_ref, bias, p_ref, ctx_ref):
    rows = q_ref.shape[0]

    def pair(i, carry):
        span = pl.ds(pl.multiple_of(i * LANES, LANES), LANES)
        vspan = pl.ds(pl.multiple_of(D + i * LANES, LANES), LANES)
        keys = kv_ref[:, span]
        values = kv_ref[:, vspan]
        queries = q_ref[:, span]
        total = jnp.zeros((rows, LANES), f32)
        for h in range(2):
            qm = jnp.where(head_mask(rows, h), queries, jnp.zeros_like(queries))
            vm = jnp.where(head_mask(values.shape[0], h), values, jnp.zeros_like(values))
            logits = mm_nt(qm, keys) * HEAD_DIM ** (-0.5) + bias[...]
            top = jnp.max(logits, axis=-1, keepdims=True)
            soft = jnp.exp(logits - top)
            norm = 1.0 / jnp.sum(soft, axis=-1, keepdims=True)
            low = (soft * norm).astype(bf16)
            p_ref[2 * i + h] = low
            total = total + mm(low, vm)
        ctx_ref[:, span] = total.astype(bf16)
        return carry

    lax.fori_loop(0, HEADS // 2, pair, 0)


def attend_back(q_ref, kv_ref, p_ref, ectx_ref, eq_ref, dkv_ref):
    rows = q_ref.shape[0]
    cols = kv_ref.shape[0]

    def pair(i, carry):
        span = pl.ds(pl.multiple_of(i * LANES, LANES), LANES)
        vspan = pl.ds(pl.multiple_of(D + i * LANES, LANES), LANES)
        keys = kv_ref[:, span]
        values = kv_ref[:, vspan]
        queries = q_ref[:, span]
        grads = ectx_ref[:, span]
        dq = jnp.zeros((rows, LANES), f32)
        dk = jnp.zeros((LANES, cols), f32)
        dv = jnp.zeros((LANES, cols), f32)
        for h in range(2):
            mask = head_mask(rows, h)
            qm = jnp.where(mask, queries, jnp.zeros_like(queries))
            em = jnp.where(mask, grads, jnp.zeros_like(grads))
            km = jnp.where(head_mask(cols, h), keys, jnp.zeros_like(keys))
            low = p_ref[2 * i + h]
            soft = low.astype(f32)
            dp = mm_nt(em, values)
            center = jnp.sum(soft * dp, axis=-1, keepdims=True)
            raw = (soft * (dp - center) * HEAD_DIM ** (-0.5)).astype(bf16)
            dv = dv + mm_tn(em, low)
            dk = dk + mm_tn(qm, raw)
            dq = dq + mm(raw, km)
        eq_ref[:, span] = dq.astype(bf16)
        dkv_ref[:, span] = dk.T.astype(bf16)
        dkv_ref[:, vspan] = dv.T.astype(bf16)
        return carry

    lax.fori_loop(0, HEADS // 2, pair, 0)


def feed_forward(b_low, gu_ref, down_ref, both_ref, units_ref):
    for t in range(TILES):
        both = mm(b_low, gu_ref[:, 256 * t : 256 * t + 256])
        both_ref[:, 256 * t : 256 * t + 256] = both
        gate, up = both[:, :128], both[:, 128:]
        units_ref[:, 128 * t : 128 * t + 128] = (gate / (1.0 + jnp.exp(-gate)) * up).astype(bf16)
    return mm(units_ref[...], down_ref[...])


def feed_back(e_low, gu_ref, down_ref, both_ref, eboth_ref):
    for t in range(TILES):
        eu = mm_nt(e_low, down_ref[128 * t : 128 * t + 128, :])
        gate = both_ref[:, 256 * t : 256 * t + 128]
        up = both_ref[:, 256 * t + 128 : 256 * t + 256]
        sig = 1.0 / (1.0 + jnp.exp(-gate))
        eboth_ref[:, 256 * t : 256 * t + 128] = (eu * up * sig * (1.0 + gate * (1.0 - sig))).astype(bf16)
        eboth_ref[:, 256 * t + 128 : 256 * t + 256] = (eu * gate * sig).astype(bf16)
    return mm_nt(eboth_ref[...], gu_ref[...])


def stage_heads(hidden, w_qkv, cos, sin):
    rows = hidden.shape[0]

    def body(a_ref, w_ref, c_ref, s_ref, q_ref, kv_ref):
        project_heads(a_ref[...], w_ref, c_ref, s_ref, q_ref, kv_ref)

    return local_call(body, [((rows, D), bf16), ((rows, 2 * D), bf16)], [hidden, w_qkv, cos, sin])


def stage_first(length, hidden, q, kv, w_out, w_gu, w_down, gains, next_gains, w_qkv, cos, sin):
    rows = hidden.shape[0]
    cols = kv.shape[0]

    def body(
        l_ref, h_ref, q_ref, kv_ref, wo_ref, gu_ref, dn_ref, g_ref, ng_ref, wq_ref, c_ref, s_ref,
        p_ref, ctx_ref, r1_ref, b_ref, both_ref, units_ref, r2_ref, sec_ref, a1_ref, q1_ref, kv1_ref,
        bias,
    ):
        make_bias(bias, l_ref[0])
        attend(q_ref, kv_ref, bias, p_ref, ctx_ref)
        r1 = h_ref[...].astype(f32) + mm(ctx_ref[...], wo_ref[...])
        r1_ref[...] = r1
        first = r1 * norm_factor(r1) * g_ref[0:1, :]
        b_ref[...] = first.astype(bf16)
        r2 = first + feed_forward(b_ref[...], gu_ref, dn_ref, both_ref, units_ref)
        r2_ref[...] = r2
        second = r2 * norm_factor(r2) * g_ref[1:2, :]
        sec_ref[...] = second
        a1_ref[...] = (second * norm_factor(second) * ng_ref[0:1, :]).astype(bf16)
        project_heads(a1_ref[...], wq_ref, c_ref, s_ref, q1_ref, kv1_ref)

    outs = [
        ((HEADS, rows, cols), bf16),
        ((rows, D), bf16),
        ((rows, D), f32),
        ((rows, D), bf16),
        ((rows, 2 * FFP), f32),
        ((rows, FFP), bf16),
        ((rows, D), f32),
        ((rows, D), f32),
        ((rows, D), bf16),
        ((rows, D), bf16),
        ((rows, 2 * D), bf16),
    ]
    ins = [length, hidden, q, kv, w_out, w_gu, w_down, gains, next_gains, w_qkv, cos, sin]
    return pl.pallas_call(
        body,
        out_shape=[jax.ShapeDtypeStruct(s, d) for s, d in outs],
        in_specs=[pl.BlockSpec(memory_space=pltpu.SMEM)] + [vmem_spec()] * (len(ins) - 1),
        out_specs=[vmem_spec()] * len(outs),
        scratch_shapes=[pltpu.VMEM((rows, cols), f32)],
        compiler_params=pltpu.CompilerParams(vmem_limit_bytes=60 * MIB),
    )(*ins)


def stage_second(length, cotangent, second, q, kv, w_out, w_gu, w_down, gains):
    rows = q.shape[0]
    cols = kv.shape[0]

    def body(
        l_ref, cot_ref, sec_ref, q_ref, kv_ref, wo_ref, gu_ref, dn_ref, g_ref,
        o_ref, ctx_ref, b_ref, units_ref, eboth_ref, ef_ref, ea_ref, e3_ref, eq_ref, dkv_ref, gg_ref,
        bias, p_ref, both_ref, ectx_ref,
    ):
        length_now = l_ref[0]
        make_bias(bias, length_now)
        attend(q_ref, kv_ref, bias, p_ref, ctx_ref)
        third = sec_ref[...] + mm(ctx_ref[...], wo_ref[...])
        f4 = norm_factor(third)
        b_ref[...] = (third * f4 * g_ref[1:2, :]).astype(bf16)
        o_ref[...] = third + feed_forward(b_ref[...], gu_ref, dn_ref, both_ref, units_ref)
        place_now = lax.broadcasted_iota(jnp.int32, (rows, D), 0) + lax.axis_index("sp") * rows
        e_out = jnp.where(place_now < length_now, cot_ref[...], 0.0)
        ef_ref[...] = e_out.astype(bf16)
        e_b = feed_back(ef_ref[...], gu_ref, dn_ref, both_ref, eboth_ref)
        grad, gain = norm_back(e_b, third, f4, g_ref[1:2, :])
        gg_ref[...] = gain
        e3 = e_out + grad
        e3_ref[...] = e3
        ea_ref[...] = e3.astype(bf16)
        ectx_ref[...] = mm_nt(ea_ref[...], wo_ref[...]).astype(bf16)
        attend_back(q_ref, kv_ref, p_ref, ectx_ref, eq_ref, dkv_ref)

    outs = [
        ((rows, D), f32),
        ((rows, D), bf16),
        ((rows, D), bf16),
        ((rows, FFP), bf16),
        ((rows, 2 * FFP), bf16),
        ((rows, D), bf16),
        ((rows, D), bf16),
        ((rows, D), f32),
        ((rows, D), bf16),
        ((cols, 2 * D), bf16),
        ((1, D), f32),
    ]
    ins = [length, cotangent, second, q, kv, w_out, w_gu, w_down, gains]
    return pl.pallas_call(
        body,
        out_shape=[jax.ShapeDtypeStruct(s, d) for s, d in outs],
        in_specs=[pl.BlockSpec(memory_space=pltpu.SMEM)] + [vmem_spec()] * (len(ins) - 1),
        out_specs=[vmem_spec()] * len(outs),
        scratch_shapes=[
            pltpu.VMEM((rows, cols), f32),
            pltpu.VMEM((HEADS, rows, cols), bf16),
            pltpu.VMEM((rows, 2 * FFP), f32),
            pltpu.VMEM((rows, D), bf16),
        ],
        compiler_params=pltpu.CompilerParams(vmem_limit_bytes=60 * MIB),
    )(*ins)


def lin_grads(eq_ref, ekv_ref, cos_ref, sin_ref, lin_ref):
    for t in range(12):
        col = 128 * t
        src = eq_ref[:, col : col + 128] if t < 4 else ekv_ref[:, col - D : col - D + 128]
        if t < 8:
            w = src.astype(f32)
            src = (w * cos_ref[...] - half_swap(w) * sin_ref[...]).astype(bf16)
        lin_ref[:, col : col + 128] = src


def stage_back(
    e_q, e_kv, e3, second, next_gains, w_qkv, cos, sin,
    r1, r2, both, gains, w_gu, w_down, w_out, q, kv, p,
):
    rows = e_q.shape[0]
    cols = kv.shape[0]

    def body(
        eq_ref, ekv_ref, e3_ref, sec_ref, ng_ref, wq_ref, c_ref, s_ref,
        r1_ref, r2_ref, both_ref, g_ref, gu_ref, dn_ref, wo_ref, q_ref, kv_ref, p_ref,
        lin_ref, eboth_ref, ef_ref, ea_ref, e1_ref, eq0_ref, dkv_ref, gg_ref,
        ectx_ref,
    ):
        lin_grads(eq_ref, ekv_ref, c_ref, s_ref, lin_ref)
        e_a = mm_nt(lin_ref[...], wq_ref[...])
        second = sec_ref[...]
        grad, gain3 = norm_back(e_a, second, norm_factor(second), ng_ref[0:1, :])
        e2 = e3_ref[...] + grad
        r2 = r2_ref[...]
        er2, gain2 = norm_back(e2, r2, norm_factor(r2), g_ref[1:2, :])
        ef_ref[...] = er2.astype(bf16)
        e_first = er2 + feed_back(ef_ref[...], gu_ref, dn_ref, both_ref, eboth_ref)
        r1 = r1_ref[...]
        er1, gain1 = norm_back(e_first, r1, norm_factor(r1), g_ref[0:1, :])
        e1_ref[...] = er1
        ea_ref[...] = er1.astype(bf16)
        gg_ref[0:1, :] = gain1
        gg_ref[1:2, :] = gain2
        gg_ref[2:3, :] = gain3
        ectx_ref[...] = mm_nt(ea_ref[...], wo_ref[...]).astype(bf16)
        attend_back(q_ref, kv_ref, p_ref, ectx_ref, eq0_ref, dkv_ref)

    return local_call(
        body,
        [
            ((rows, 3 * D), bf16),
            ((rows, 2 * FFP), bf16),
            ((rows, D), bf16),
            ((rows, D), bf16),
            ((rows, D), f32),
            ((rows, D), bf16),
            ((cols, 2 * D), bf16),
            ((3, D), f32),
        ],
        [
            e_q, e_kv, e3, second, next_gains, w_qkv, cos, sin,
            r1, r2, both, gains, w_gu, w_down, w_out, q, kv, p,
        ],
        [pltpu.VMEM((rows, D), bf16)],
    )


def stage_end(e_q, e_kv, e1, w_qkv, cos, sin):
    rows = e_q.shape[0]

    def body(eq_ref, ekv_ref, e1_ref, wq_ref, c_ref, s_ref, lin_ref, o_ref):
        lin_grads(eq_ref, ekv_ref, c_ref, s_ref, lin_ref)
        o_ref[...] = e1_ref[...] + mm_nt(lin_ref[...], wq_ref[...])

    return local_call(
        body, [((rows, 3 * D), bf16), ((rows, D), f32)], [e_q, e_kv, e1, w_qkv, cos, sin]
    )


def reduce_and_update(slots_zero, slots_one, gains_part, master, one, two, zn, rows, share):
    half = rows // 2
    step = chunk_rows(rows)
    ndev = zn * 8
    per_layer = ndev // 2
    turns = rows // step

    def body(
        g0_ref, g1_ref, gp_ref, m_ref, one_ref, two_ref,
        nm_ref, n1_ref, n2_ref, gn_ref, gg_ref,
        acc, rc, rd, rx, ry, rz, fin, sq, sqs, gps, send, recv, lsem, ssem, rsem,
    ):
        z, x, y, c = coords()
        me = ((z * 2 + x) * 2 + y) * 2 + c
        bar = pltpu.get_barrier_semaphore()

        def peer(d):
            tgt = lax.rem(me + d, ndev)
            return {"dp": lax.div(tgt, 4), "sp": lax.rem(tgt, 4)}

        def hello(d, carry):
            pl.semaphore_signal(bar, inc=1, device_id=peer(d), device_id_type=MESH)
            return carry

        lax.fori_loop(1, ndev, hello, 0)

        to_x = place(z, 1 - x, y, c)
        to_y = place(z, x, 1 - y, c)
        to_c = place(z, x, y, 1 - c)
        spots = [(x, y), (1 - x, y), (x, 1 - y), (1 - x, 1 - y)]

        def slot(zp, rel, cp):
            xp, yp = spots[rel]
            return ((zp * 2 + xp) * 2 + yp) * 2 + cp

        def on_source(zp, rel, cp, act):
            index = slot(zp, rel, cp)

            @pl.when(index < per_layer)
            def _():
                act(g0_ref.at[index])

            @pl.when(index >= per_layer)
            def _():
                act(g1_ref.at[index - per_layer])

        def cp(src, dst, zp, s, r, device):
            return remote(src, dst, send.at[zp, s], recv.at[zp, r], device)

        def core_send(zp, rel, src):
            return cp(src, rc.at[zp, rel], zp, rel, rel, to_c)

        def load(zp, rel, src):
            return pltpu.make_async_copy(src, acc.at[zp, rel], lsem.at[zp, rel])

        def diag_a(zp):
            return cp(acc.at[zp, 3, pl.ds(0, half)], rd.at[zp, pl.ds(0, half)], zp, 4, 4, to_y)

        def diag_b(zp):
            return cp(acc.at[zp, 3, pl.ds(half, half)], rd.at[zp, pl.ds(half, half)], zp, 5, 5, to_x)

        def send_x(zp):
            return cp(acc.at[zp, 1], rx.at[zp], zp, 6, 6, to_x)

        def send_y(zp):
            return cp(acc.at[zp, 2], ry.at[zp], zp, 7, 7, to_y)

        def right(zp):
            return cp(acc.at[zp, 0], rz.at[zp, 0], zp, 8, 8, place(z + 1, x, y, c))

        def left(zp):
            return cp(acc.at[zp, 0], rz.at[zp, 1], zp, 8, 9, place(z - 1, x, y, c))

        def add_into(dst, low, high, *srcs):
            size = step if (high - low) % step == 0 else 16

            def one_step(i, carry):
                span = pl.ds(pl.multiple_of(low + i * size, 16), size)
                value = dst[span, :].astype(f32)
                for src in srcs:
                    value = value + src[span, :].astype(f32)
                dst[span, :] = value.astype(bf16)
                return carry

            lax.fori_loop(0, (high - low) // size, one_step, 0)

        def valid(k):
            zp = order_at(2 * zn - 2 - k, z)
            return zp, (k >= 0) & (k < 2 * zn - 1) & (zp >= 0) & (zp < zn)

        def stage_c(k):
            zp, ok = valid(k)

            @pl.when(ok)
            def _():
                for rel in (3, 1, 2, 0):
                    on_source(zp, rel, 1 - c, lambda src, rel=rel: core_send(zp, rel, src).start())
                    on_source(zp, rel, c, lambda src, rel=rel: load(zp, rel, src).start())

        def stage_one(k):
            zp, ok = valid(k)

            @pl.when(ok)
            def _():
                for rel in (3, 1, 2, 0):
                    core_send(zp, rel, g0_ref.at[0]).wait_recv()
                    load(zp, rel, g0_ref.at[0]).wait()
                    add_into(acc.at[zp, rel], 0, rows, rc.at[zp, rel])
                    if rel == 3:
                        diag_a(zp).start()
                        diag_b(zp).start()

        def stage_two(k):
            zp, ok = valid(k)

            @pl.when(ok)
            def _():
                diag_a(zp).wait_recv()
                add_into(acc.at[zp, 1], 0, half, rd.at[zp])
                send_x(zp).start()
                diag_b(zp).wait_recv()
                add_into(acc.at[zp, 2], half, rows, rd.at[zp])
                send_y(zp).start()

        def stage_three(k):
            zp, ok = valid(k)

            @pl.when(ok & (zp != z))
            def _():
                send_x(zp).wait_recv()
                send_y(zp).wait_recv()
                add_into(acc.at[zp, 0], 0, rows, rx.at[zp], ry.at[zp])

                @pl.when((zp > z) & (z > 0))
                def _():
                    right(zp).wait_recv()
                    add_into(acc.at[zp, 0], 0, rows, rz.at[zp, 0])

                @pl.when((zp < z) & (z < zn - 1))
                def _():
                    left(zp).wait_recv()
                    add_into(acc.at[zp, 0], 0, rows, rz.at[zp, 1])

                pl.when(zp > z)(lambda: right(zp).start())
                pl.when(zp < z)(lambda: left(zp).start())

        pl.semaphore_wait(bar, ndev - 1)

        def tell(src, dst, s):
            def go(d, carry):
                remote(src, dst.at[me], ssem.at[s], rsem.at[s], peer(d)).start()
                return carry

            lax.fori_loop(1, ndev, go, 0)

        def hear(dst, s):
            part = dst.at[pl.ds(0, ndev - 1)]
            both = remote(part, part, ssem.at[s], rsem.at[s], to_c)
            both.wait_send()
            both.wait_recv()

        for k in range(3):
            stage_c(k)
        tell(gp_ref, gps, 0)
        gps[me] = gp_ref[...]

        def turn(k, carry):
            stage_one(k)
            stage_c(k + 3)
            stage_two(k - 1)
            stage_three(k - 2)
            return carry

        lax.fori_loop(0, 2 * zn + 1, turn, 0)

        send_x(z).wait_recv()
        send_y(z).wait_recv()
        pl.when(z > 0)(lambda: right(z).wait_recv())
        pl.when(z < zn - 1)(lambda: left(z).wait_recv())

        def total(i, carry):
            span = pl.ds(pl.multiple_of(i * step, 16), step)
            value = (
                acc[z, 0, span, :].astype(f32)
                + rx[z, span, :].astype(f32)
                + ry[z, span, :].astype(f32)
            )
            value = value + jnp.where(z > 0, rz[z, 0, span, :].astype(f32), 0.0)
            value = value + jnp.where(z < zn - 1, rz[z, 1, span, :].astype(f32), 0.0)
            fin[span, :] = value
            return carry

        lax.fori_loop(0, turns, total, 0)
        fin[pl.ds(rows, 8), :] = jnp.zeros((8, LANES), f32)

        shift = lax.rem(share * me, LANES)
        back = lax.rem(LANES - shift, LANES)
        lane = lax.broadcasted_iota(jnp.int32, (step, LANES), 1)
        row = lax.broadcasted_iota(jnp.int32, (step, LANES), 0)

        def realign(i, carry):
            now = pltpu.roll(fin[pl.ds(i * step, step), :], back, 1)
            after = pltpu.roll(fin[pl.ds(i * step + 1, step), :], back, 1)
            value = jnp.where(lane < LANES - shift, now, after)
            value = jnp.where((row + i * step) * LANES + lane < share, value, 0.0)
            n1_ref[pl.ds(i * step, step), :] = value
            square = value * value
            return carry + jnp.sum(square.reshape(step // 8, 8, LANES), axis=0)

        sq[...] = lax.fori_loop(0, turns, realign, jnp.zeros((8, LANES), f32))
        tell(sq, sqs, 1)
        sqs[me] = sq[...]

        def finish(i, carry):
            for rel in range(4):
                core_send(i, rel, g0_ref.at[0]).wait_send()
            for item in (diag_a(i), diag_b(i), send_x(i), send_y(i)):
                item.wait_send()
            pl.when(i > z)(lambda: right(i).wait_send())
            pl.when(i < z)(lambda: left(i).wait_send())
            return carry

        lax.fori_loop(0, zn, finish, 0)
        hear(gps, 0)
        gg_ref[...] = lax.fori_loop(
            1, ndev, lambda i, s: s + gps[i], gps[0]
        )
        hear(sqs, 1)
        squares = lax.fori_loop(1, ndev, lambda i, s: s + sqs[i], sqs[0])
        norm = jnp.sqrt(jnp.sum(squares, keepdims=True))
        gn_ref[...] = jnp.broadcast_to(norm, (8, LANES))
        scale = jnp.minimum(1.0, 1.0 / norm)
        correction = 1.0 - 0.5**STEP

        def update(i, carry):
            span = pl.ds(pl.multiple_of(i * step, 16), step)
            clipped = n1_ref[span, :] * scale
            new_one = 0.5 * one_ref[span, :] + 0.5 * clipped
            new_two = 0.5 * two_ref[span, :] + 0.5 * clipped * clipped
            n1_ref[span, :] = new_one
            n2_ref[span, :] = new_two
            nm_ref[span, :] = m_ref[pl.ds(8 + i * step, step), :] * (
                1.0 - LEARN_RATE * DECAY_RATE
            ) - LEARN_RATE * (new_one / correction) / (jnp.sqrt(new_two / correction) + ADAM_EPS)
            return carry

        lax.fori_loop(0, turns, update, 0)

    flat = jax.ShapeDtypeStruct((rows, LANES), f32)
    return pl.pallas_call(
        body,
        out_shape=[
            flat,
            flat,
            flat,
            jax.ShapeDtypeStruct((8, LANES), f32),
            jax.ShapeDtypeStruct((16, LANES), f32),
        ],
        in_specs=[any_spec(), any_spec()] + [vmem_spec()] * 4,
        out_specs=[vmem_spec()] * 5,
        scratch_shapes=[
            pltpu.VMEM((zn, 4, rows, LANES), bf16),
            pltpu.VMEM((zn, 4, rows, LANES), bf16),
            pltpu.VMEM((zn, rows, LANES), bf16),
            pltpu.VMEM((zn, rows, LANES), bf16),
            pltpu.VMEM((zn, rows, LANES), bf16),
            pltpu.VMEM((zn, 2, rows, LANES), bf16),
            pltpu.VMEM((rows + 8, LANES), f32),
            pltpu.VMEM((8, LANES), f32),
            pltpu.VMEM((ndev, 8, LANES), f32),
            pltpu.VMEM((ndev, 16, LANES), f32),
            pltpu.SemaphoreType.DMA((zn, 9)),
            pltpu.SemaphoreType.DMA((zn, 10)),
            pltpu.SemaphoreType.DMA((zn, 4)),
            pltpu.SemaphoreType.DMA((2,)),
            pltpu.SemaphoreType.DMA((2,)),
        ],
        compiler_params=pltpu.CompilerParams(
            collective_id=4, has_side_effects=True, vmem_limit_bytes=60 * MIB
        ),
    )(slots_zero, slots_one, gains_part, master, one, two)


def rope_rows(rows):
    frequency = jnp.exp(
        -jnp.log(10000.0) * jnp.arange(HEAD_DIM // 2).astype(f32) * 2.0 / HEAD_DIM
    )
    positions = lax.axis_index("sp") * rows + jnp.arange(rows)
    angles = positions.astype(f32)[:, None] * frequency[None, :]
    cos = jnp.cos(angles)
    sin = jnp.sin(angles)
    return (
        jnp.concatenate([cos] * 4, axis=1),
        jnp.concatenate([-sin, sin, -sin, sin], axis=1),
    )


def step_shard(dp_size, sp_size, hidden_in, cotangent, lengths, master, moment_one, moment_two):
    share = master.shape[0]
    zn = dp_size // 2
    per_layer = dp_size * sp_size // 2
    rows = -(-(-(-share // LANES) + 1) // 32) * 32
    seqs, tokens, width = hidden_in.shape

    def pad(flat, lead):
        return jnp.pad(flat, (lead * LANES, rows * LANES - share)).reshape(rows + lead, LANES)

    master_pad = pad(master, 8)
    slots = gather_weights(master_pad, zn, rows, share, 0, zn)
    wq0, wo0, wg0, wd0, g0 = unpack_weights(slots, 0, rows, share)
    wq1, wo1, wg1, wd1, g1 = unpack_weights(slots, 1, rows, share)
    cos, sin = rope_rows(tokens)
    hidden = hidden_in.reshape(tokens, width)

    def join(kv):
        return exchange_keys(kv).reshape(4 * tokens, 2 * width)

    def collect(dkv):
        return collect_keys(dkv.reshape(4, tokens, 2 * width))

    q0, kv0 = stage_heads(hidden, wq0, cos, sin)
    kv0 = join(kv0)
    p0, ctx0, r1, b0, both0, units0, r2, second, a1, q1, kv1 = stage_first(
        lengths, hidden, q0, kv0, wo0, wg0, wd0, g0, g1, wq1, cos, sin
    )
    kv1 = join(kv1)
    output, ctx1, b1, units1, eboth1, ef1, ea1, e3, eq1, dkv1, gain4 = stage_second(
        lengths, cotangent.reshape(tokens, width), second, q1, kv1, wo1, wg1, wd1, g1
    )
    ekv1 = collect(dkv1)
    lin1, eboth0, ef0, ea0, e1, eq0, dkv0, gains3 = stage_back(
        eq1, ekv1, e3, second, g1, wq1, cos, sin, r1, r2, both0, g0, wg0, wd0, wo0, q0, kv0, p0
    )
    gains_one = jnp.concatenate([gains3[2:3], gain4], axis=0)
    grads_one = weight_grads(
        a1, lin1, ctx1, ea1, b1, eboth1, units1, ef1, gains_one, rows, share, per_layer
    )
    ekv0 = collect(dkv0)
    lin0, input_grad = stage_end(eq0, ekv0, e1, wq0, cos, sin)
    gains_zero = gains3[0:2]
    grads_zero = weight_grads(
        hidden, lin0, ctx0, ea0, b0, eboth0, units0, ef0, gains_zero, rows, share, per_layer
    )
    gains_part = jnp.concatenate([gains_zero, gains_one], axis=0).reshape(16, LANES)
    new_master, new_one, new_two, norm, gains = reduce_and_update(
        grads_zero, grads_one, gains_part, master_pad, pad(moment_one, 0), pad(moment_two, 0),
        zn, rows, share,
    )

    def flat(value):
        return value.reshape(-1)[:share]

    new_master = flat(new_master)
    return (
        output.reshape(hidden_in.shape),
        input_grad.reshape(hidden_in.shape),
        new_master,
        flat(new_one),
        flat(new_two),
        new_master.astype(bf16),
        norm[0, 0],
        gains.reshape(2, 2, width),
    )


def solution(mesh):
    in_specs = (
        P("dp", "sp", None),
        P("dp", "sp", None),
        P("dp"),
        P(("dp", "sp")),
        P(("dp", "sp")),
        P(("dp", "sp")),
    )
    out_specs = (
        P("dp", "sp", None),
        P("dp", "sp", None),
        P(("dp", "sp")),
        P(("dp", "sp")),
        P(("dp", "sp")),
        P(("dp", "sp")),
        P(),
        P(),
    )
    body = functools.partial(step_shard, mesh.shape["dp"], mesh.shape["sp"])
    return jax.shard_map(body, mesh=mesh, in_specs=in_specs, out_specs=out_specs, check_vma=False)
```

```python
import functools

import jax
import jax.numpy as jnp
from jax import lax
from jax.experimental import pallas as pl
from jax.experimental.pallas import tpu as pltpu
from jax.sharding import PartitionSpec as P

D = 512
HEADS = 8
HEAD_DIM = 64
FF = 1368
FFP = 1408
TILES = 11
STEP = 5
NORM_EPS = 1e-06
ADAM_EPS = 1e-08
LEARN_RATE = 0.02
DECAY_RATE = 0.01
LANES = 128
LAYER_ROWS = 24616
BASE_OUT = 6144
BASE_GU = 8192
BASE_DOWN = 19136
BASE_GAINS = 24608
GU_ROW = 2 * FF
PERIOD = 171
MESH = pl.DeviceIdType.MESH
MIB = 1 << 20
f32 = jnp.float32
bf16 = jnp.bfloat16


def mm(a, b):
    return lax.dot_general(a, b, (((1,), (0,)), ((), ())), preferred_element_type=f32)


def mm_nt(a, b):
    return lax.dot_general(a, b, (((1,), (1,)), ((), ())), preferred_element_type=f32)


def mm_tn(a, b):
    return lax.dot_general(a, b, (((0,), (0,)), ((), ())), preferred_element_type=f32)


def chunk_rows(rows):
    tiles = rows // 16
    best = max(d for d in range(1, 17) if tiles % d == 0)
    return best * 16


def vmem_spec():
    return pl.BlockSpec(memory_space=pltpu.VMEM)


def any_spec():
    return pl.BlockSpec(memory_space=pl.ANY)


def local_call(body, outs, ins, scratch=(), limit=60, flops=0):
    return pl.pallas_call(
        body,
        out_shape=[jax.ShapeDtypeStruct(s, d) for s, d in outs],
        in_specs=[vmem_spec()] * len(ins),
        out_specs=[vmem_spec()] * len(outs),
        scratch_shapes=list(scratch),
        compiler_params=pltpu.CompilerParams(vmem_limit_bytes=limit * MIB),
    )(*ins)


def coords():
    dp = lax.axis_index("dp")
    sp = lax.axis_index("sp")
    return lax.div(dp, 2), lax.rem(dp, 2), lax.div(sp, 2), lax.rem(sp, 2)


def place(z, x, y, c):
    return {"dp": z * 2 + x, "sp": y * 2 + c}


def remote(src, dst, send_sem, recv_sem, device):
    return pltpu.make_async_remote_copy(
        src_ref=src,
        dst_ref=dst,
        send_sem=send_sem,
        recv_sem=recv_sem,
        device_id=device,
        device_id_type=MESH,
    )


def order_at(tau, z):
    step = lax.div(tau + 1, 2)
    return z + jnp.where(lax.rem(tau, 2) == 1, -step, step)


class Gather:
    def __init__(self, out_ref, own, send, recv, zn, rows, zlo, zhi):
        self.out_ref, self.own, self.send, self.recv = out_ref, own, send, recv
        self.zn, self.half, self.zlo, self.zhi = zn, rows // 2, zlo, zhi
        self.z, self.x, self.y, self.c = coords()
        z, x, y, c = self.z, self.x, self.y, self.c
        self.to_x = place(z, 1 - x, y, c)
        self.to_y = place(z, x, 1 - y, c)
        self.to_c = place(z, x, y, 1 - c)
        self.turns = 2 * zn + 1

    def slot(self, zp, xp, yp, cp):
        return (((zp - self.zlo) * 2 + xp) * 2 + yp) * 2 + cp

    def whole(self, zp, xp, yp):
        return self.out_ref.at[self.slot(zp, xp, yp, self.c)]

    def upper(self, zp, xp, yp):
        return self.out_ref.at[self.slot(zp, xp, yp, self.c), pl.ds(0, self.half)]

    def lower(self, zp, xp, yp):
        return self.out_ref.at[self.slot(zp, xp, yp, self.c), pl.ds(self.half, self.half)]

    def cp(self, ref, zp, s, r, device):
        i = zp - self.zlo
        return remote(ref, ref, self.send.at[i, s], self.recv.at[i, r], device)

    def right(self, zp):
        return self.cp(self.whole(zp, self.x, self.y), zp, 0, 0, place(self.z + 1, self.x, self.y, self.c))

    def left(self, zp):
        return self.cp(self.whole(zp, self.x, self.y), zp, 1, 0, place(self.z - 1, self.x, self.y, self.c))

    def first(self, zp):
        ref = self.whole(zp, self.x, self.y)
        return [
            self.cp(ref, zp, 2, 1, self.to_x),
            self.cp(ref, zp, 3, 2, self.to_y),
            self.cp(ref, zp, 4, 3, self.to_c),
        ]

    def second_x(self, zp):
        return [
            self.cp(self.upper(zp, 1 - self.x, self.y), zp, 5, 4, self.to_y),
            self.cp(self.whole(zp, 1 - self.x, self.y), zp, 6, 6, self.to_c),
        ]

    def second_y(self, zp):
        return [
            self.cp(self.lower(zp, self.x, 1 - self.y), zp, 7, 5, self.to_x),
            self.cp(self.whole(zp, self.x, 1 - self.y), zp, 8, 7, self.to_c),
        ]

    def third_a(self, zp):
        return self.cp(self.upper(zp, 1 - self.x, 1 - self.y), zp, 9, 8, self.to_c)

    def third_b(self, zp):
        return self.cp(self.lower(zp, 1 - self.x, 1 - self.y), zp, 10, 9, self.to_c)

    def arrival(self, ref, zp, r):
        self.cp(ref, zp, 0, r, self.to_c).wait_recv()

    def keep(self, lsem):
        @pl.when((self.z >= self.zlo) & (self.z < self.zhi))
        def _():
            copy = pltpu.make_async_copy(self.own, self.whole(self.z, self.x, self.y), lsem)
            copy.start()
            copy.wait()

    def valid(self, tau):
        zp = order_at(tau, self.z)
        ok = (tau >= 0) & (tau < 2 * self.zn - 1) & (zp >= self.zlo) & (zp < self.zhi)
        return zp, ok

    def turn(self, tau):
        z, x, y = self.z, self.x, self.y
        zp, ok = self.valid(tau)

        @pl.when(ok)
        def _():
            pl.when(tau > 0)(lambda: self.arrival(self.whole(zp, x, y), zp, 0))
            pl.when((zp <= z) & (z < self.zn - 1))(lambda: self.right(zp).start())
            pl.when((zp >= z) & (z > 0))(lambda: self.left(zp).start())
            for item in self.first(zp):
                item.start()

        zq, ok_two = self.valid(tau - 1)

        @pl.when(ok_two)
        def _():
            self.arrival(self.whole(zq, 1 - x, y), zq, 1)
            for item in self.second_x(zq):
                item.start()
            self.arrival(self.whole(zq, x, 1 - y), zq, 2)
            for item in self.second_y(zq):
                item.start()

        zr, ok_three = self.valid(tau - 2)

        @pl.when(ok_three)
        def _():
            self.arrival(self.upper(zr, 1 - x, 1 - y), zr, 4)
            self.third_a(zr).start()
            self.arrival(self.lower(zr, 1 - x, 1 - y), zr, 5)
            self.third_b(zr).start()

    def pump(self, low, high):
        def one(tau, carry):
            self.turn(tau)
            return carry

        lax.fori_loop(low, high, one, 0)

    def arrived(self):
        x, y, far = self.x, self.y, 1 - self.c
        half = self.half

        def one(i, carry):
            zp = self.zlo + i
            ref = self.out_ref
            self.arrival(ref.at[self.slot(zp, x, y, far)], zp, 3)
            self.arrival(ref.at[self.slot(zp, 1 - x, y, far)], zp, 6)
            self.arrival(ref.at[self.slot(zp, x, 1 - y, far)], zp, 7)
            self.arrival(ref.at[self.slot(zp, 1 - x, 1 - y, far), pl.ds(0, half)], zp, 8)
            self.arrival(ref.at[self.slot(zp, 1 - x, 1 - y, far), pl.ds(half, half)], zp, 9)
            return carry

        lax.fori_loop(0, self.zhi - self.zlo, one, 0)

    def sent(self):
        z = self.z

        def one(i, carry):
            zp = self.zlo + i
            pl.when((zp <= z) & (z < self.zn - 1))(lambda: self.right(zp).wait_send())
            pl.when((zp >= z) & (z > 0))(lambda: self.left(zp).wait_send())
            for item in self.first(zp) + self.second_x(zp) + self.second_y(zp):
                item.wait_send()
            self.third_a(zp).wait_send()
            self.third_b(zp).wait_send()
            return carry

        lax.fori_loop(0, self.zhi - self.zlo, one, 0)


class KeyExchange:
    def __init__(self, kv_ref, all_ref, send, recv, lsem, parts):
        z, x, y, c = coords()
        rows = kv_ref.shape[0]
        piece = rows // parts
        to_y = place(z, x, 1 - y, c)
        to_c = place(z, x, y, 1 - c)
        mine = y * 2 + c
        beyond = (1 - y) * 2 + c
        self.parts = parts

        def part(row, k):
            return all_ref.at[pl.ds(pl.multiple_of(row * rows, rows) + k * piece, piece)]

        self.keep = pltpu.make_async_copy(
            kv_ref, all_ref.at[pl.ds(pl.multiple_of(mine * rows, rows), rows)], lsem
        )
        self.own_y, self.own_c, self.pass_c = [], [], []
        for k in range(parts):
            src, dst = kv_ref.at[pl.ds(k * piece, piece)], part(mine, k)
            self.own_y.append(remote(src, dst, send.at[0, k], recv.at[0, k], to_y))
            self.own_c.append(remote(src, dst, send.at[1, k], recv.at[1, k], to_c))
            ref = part(beyond, k)
            self.pass_c.append(remote(ref, ref, send.at[2, k], recv.at[2, k], to_c))

    def start(self):
        self.keep.start()
        for item in self.own_y + self.own_c:
            item.start()

    def forward(self):
        for k in range(self.parts):
            self.own_y[k].wait_recv()
            self.pass_c[k].start()

    def finish(self):
        for k in range(self.parts):
            self.own_c[k].wait_recv()
            self.pass_c[k].wait_recv()
        for item in self.own_y + self.own_c + self.pass_c:
            item.wait_send()
        self.keep.wait()


def fill_flat(slots, flat, rows, share, low, high):
    step = chunk_rows(rows)

    def one(i, carry):
        start = lax.div(share * i, LANES)
        shift = lax.rem(share * i, LANES)
        edge = flat[pl.ds(start, 1), :]

        def fill(j, inner):
            flat[pl.ds(start + j * step, step), :] = slots[i, pl.ds(j * step, step), :].astype(f32)
            return inner

        lax.fori_loop(0, rows // step, fill, 0)

        @pl.when(shift > 0)
        def _():
            flat[pl.ds(start, 1), :] = flat[pl.ds(start, 1), :] + edge

        return carry

    lax.fori_loop(low, high, one, 0)


def take_qkv(flat, qkv_ref, low, high):
    for col in range(low, high):
        qkv_ref[:, 128 * col : 128 * col + 128] = flat[pl.ds(col, D, stride=12), :].astype(bf16)


def take_out(flat, out_ref, gains_ref):
    for col in range(4):
        span = slice(128 * col, 128 * col + 128)
        out_ref[:, span] = flat[pl.ds(BASE_OUT + col, D, stride=4), :].astype(bf16)
        gains_ref[:, span] = flat[pl.ds(BASE_GAINS + col, 2, stride=4), :]


def take_down(flat, down_ref):
    for col in range(4):
        span = slice(128 * col, 128 * col + 128)
        down_ref[0:FF, span] = flat[pl.ds(BASE_DOWN + col, FF, stride=4), :].astype(bf16)
    down_ref[FF:FFP, :] = jnp.zeros((FFP - FF, D), bf16)


def take_gate_up(flat, gate_up, r):
    lane = lax.broadcasted_iota(jnp.int32, (64, LANES), 1)
    for part in range(2):
        for tile in range(TILES):
            first = GU_ROW * r + FF * part + LANES * tile
            q, s = first // LANES, first % LANES
            value = flat[pl.ds(BASE_GU + q, 64, stride=PERIOD), :]
            if s:
                after = flat[pl.ds(BASE_GU + q + 1, 64, stride=PERIOD), :]
                value = jnp.where(
                    lane < LANES - s,
                    pltpu.roll(value, LANES - s, 1),
                    pltpu.roll(after, LANES - s, 1),
                )
            if tile == TILES - 1:
                value = jnp.where(lane < FF - LANES * tile, value, 0.0)
            gate_up[2 * tile + part, pl.ds(r, 64, stride=8), :] = value


def place_gate_up(gate_up, gu_ref):
    for k in range(2 * TILES):
        gu_ref[:, 128 * k : 128 * k + 128] = gate_up[k].astype(bf16)


def gate_up_segments(q):
    pieces = []
    place_now = LANES * q
    end = place_now + LANES
    while place_now < end:
        r, within = divmod(place_now, GU_ROW)
        part, unit = divmod(within, FF)
        tile, lane_src = divmod(unit, LANES)
        room = min(end - place_now, FF - unit, LANES - lane_src)
        lane_dst = place_now - LANES * q
        pieces.append((r, 2 * tile + part, lane_dst, lane_dst + room, (lane_dst - lane_src) % LANES))
        place_now += room
    return pieces


def weight_grads(a_low, e_lin, ctx, e_attn, b_low, e_both, units, e_ffn, gains, rows, share, per_layer):
    step = chunk_rows(rows)
    depth = LAYER_ROWS + rows

    def body(a_ref, lin_ref, ctx_ref, ea_ref, b_ref, both_ref, u_ref, ef_ref, g_ref, s_ref, flat, gate_up):
        i = pl.program_id(0)

        @pl.when(i == 0)
        def _():
            for t in range(6):
                value = mm_tn(a_ref[...], lin_ref[:, 256 * t : 256 * t + 256])
                for k in range(2):
                    flat[pl.ds(2 * t + k, D, stride=12), :] = value[:, 128 * k : 128 * k + 128]
            for t in range(2):
                value = mm_tn(ctx_ref[...], ea_ref[:, 256 * t : 256 * t + 256])
                for k in range(2):
                    flat[pl.ds(BASE_OUT + 2 * t + k, D, stride=4), :] = value[
                        :, 128 * k : 128 * k + 128
                    ]
                value = mm_tn(u_ref[...], ef_ref[:, 256 * t : 256 * t + 256])
                for k in range(2):
                    flat[pl.ds(BASE_DOWN + 2 * t + k, FF, stride=4), :] = value[
                        0:FF, 128 * k : 128 * k + 128
                    ]
            for t in range(TILES):
                value = mm_tn(b_ref[...], both_ref[:, 256 * t : 256 * t + 256])
                for k in range(2):
                    gate_up[2 * t + k] = value[:, 128 * k : 128 * k + 128]
            for col in range(4):
                flat[pl.ds(BASE_GAINS + col, 2, stride=4), :] = g_ref[:, 128 * col : 128 * col + 128]
            lane = lax.broadcasted_iota(jnp.int32, (64, LANES), 1)
            for q in range(PERIOD):
                value = None
                for r, k, low, high, turn in gate_up_segments(q):
                    piece = gate_up[k, pl.ds(r, 64, stride=8), :]
                    if turn:
                        piece = pltpu.roll(piece, turn, 1)
                    value = piece if value is None else jnp.where(lane < low, value, piece)
                flat[pl.ds(BASE_GU + q, 64, stride=PERIOD), :] = value
            flat[LAYER_ROWS:depth, :] = jnp.zeros((depth - LAYER_ROWS, LANES), f32)

        start = lax.div(share * i, LANES)

        def fill(j, carry):
            s_ref[0, pl.ds(j * step, step), :] = flat[pl.ds(start + j * step, step), :].astype(bf16)
            return carry

        lax.fori_loop(0, rows // step, fill, 0)

    ins = [a_low, e_lin, ctx, e_attn, b_low, e_both, units, e_ffn, gains]
    return pl.pallas_call(
        body,
        grid=(per_layer,),
        out_shape=jax.ShapeDtypeStruct((per_layer, rows, LANES), bf16),
        in_specs=[pl.BlockSpec(v.shape, lambda i: (0, 0)) for v in ins],
        out_specs=pl.BlockSpec((1, rows, LANES), lambda i: (i, 0, 0)),
        scratch_shapes=[pltpu.VMEM((depth, LANES), f32), pltpu.VMEM((2 * TILES, D, LANES), f32)],
        compiler_params=pltpu.CompilerParams(vmem_limit_bytes=60 * MIB),
    )(*ins)


def exchange_keys(kv):
    rows, width = kv.shape
    parts = 4
    piece = rows // parts

    def body(kv_ref, all_ref, send, recv, lsem):
        z, x, y, c = coords()
        bar = pltpu.get_barrier_semaphore()
        to_y = place(z, x, 1 - y, c)
        to_c = place(z, x, y, 1 - c)
        for device in (to_y, to_c):
            pl.semaphore_signal(bar, inc=1, device_id=device, device_id_type=MESH)
        pl.semaphore_wait(bar, 2)
        mine = y * 2 + c
        beyond = (1 - y) * 2 + c
        keep = pltpu.make_async_copy(kv_ref, all_ref.at[mine], lsem)
        keep.start()

        def part(ref, k):
            return ref.at[pl.ds(k * piece, piece)]

        own_y, own_c, pass_c = [], [], []
        for k in range(parts):
            src, dst = part(kv_ref, k), part(all_ref.at[mine], k)
            own_y.append(remote(src, dst, send.at[0, k], recv.at[0, k], to_y))
            own_c.append(remote(src, dst, send.at[1, k], recv.at[1, k], to_c))
            ref = part(all_ref.at[beyond], k)
            pass_c.append(remote(ref, ref, send.at[2, k], recv.at[2, k], to_c))
        for k in range(parts):
            own_y[k].start()
        for k in range(parts):
            own_c[k].start()
        for k in range(parts):
            own_y[k].wait_recv()
            pass_c[k].start()
        for k in range(parts):
            own_c[k].wait_recv()
            pass_c[k].wait_recv()
        for item in own_y + own_c + pass_c:
            item.wait_send()
        keep.wait()

    return pl.pallas_call(
        body,
        out_shape=jax.ShapeDtypeStruct((4, rows, width), kv.dtype),
        in_specs=[vmem_spec()],
        out_specs=vmem_spec(),
        scratch_shapes=[
            pltpu.SemaphoreType.DMA((3, parts)),
            pltpu.SemaphoreType.DMA((3, parts)),
            pltpu.SemaphoreType.DMA,
        ],
        compiler_params=pltpu.CompilerParams(
            collective_id=2, has_side_effects=True, vmem_limit_bytes=32 * MIB
        ),
    )(kv)


def collect_keys(dkv):
    blocks, rows, width = dkv.shape
    parts = 4
    piece = rows // parts

    def body(g_ref, sum_ref, from_c, pair, from_y, send, recv):
        z, x, y, c = coords()
        bar = pltpu.get_barrier_semaphore()
        to_y = place(z, x, 1 - y, c)
        to_c = place(z, x, y, 1 - c)
        for device in (to_y, to_c):
            pl.semaphore_signal(bar, inc=1, device_id=device, device_id_type=MESH)
        pl.semaphore_wait(bar, 2)
        mine = y * 2 + c
        beyond = (1 - y) * 2 + c

        def part(ref, k):
            return ref.at[pl.ds(k * piece, piece)]

        near, wide = [], []
        for h, row in ((0, 1 - y), (1, y)):
            src = g_ref.at[row * 2 + 1 - c]
            near.append(
                [
                    remote(part(src, k), part(from_c.at[h], k), send.at[h, k], recv.at[h, k], to_c)
                    for k in range(parts)
                ]
            )
        for k in range(parts):
            wide.append(remote(part(pair, k), part(from_y, k), send.at[2, k], recv.at[2, k], to_y))
        for group in near:
            for item in group:
                item.start()
        for k in range(parts):
            span = pl.ds(k * piece, piece)
            near[0][k].wait_recv()
            pair[span, :] = (
                from_c[0, span, :].astype(f32) + g_ref[beyond, span, :].astype(f32)
            ).astype(bf16)
            wide[k].start()
        for k in range(parts):
            span = pl.ds(k * piece, piece)
            near[1][k].wait_recv()
            wide[k].wait_recv()
            sum_ref[span, :] = (
                from_c[1, span, :].astype(f32)
                + g_ref[mine, span, :].astype(f32)
                + from_y[span, :].astype(f32)
            ).astype(bf16)
        for item in near[0] + near[1] + wide:
            item.wait_send()

    return pl.pallas_call(
        body,
        out_shape=jax.ShapeDtypeStruct((rows, width), bf16),
        in_specs=[vmem_spec()],
        out_specs=vmem_spec(),
        scratch_shapes=[
            pltpu.VMEM((2, rows, width), bf16),
            pltpu.VMEM((rows, width), bf16),
            pltpu.VMEM((rows, width), bf16),
            pltpu.SemaphoreType.DMA((3, parts)),
            pltpu.SemaphoreType.DMA((3, parts)),
        ],
        compiler_params=pltpu.CompilerParams(
            collective_id=3, has_side_effects=True, vmem_limit_bytes=32 * MIB
        ),
    )(dkv)


def half_swap(u):
    lane = lax.broadcasted_iota(jnp.int32, u.shape, 1)
    return jnp.where(lax.rem(lane, 64) < 32, pltpu.roll(u, 96, 1), pltpu.roll(u, 32, 1))


def project_heads(a_low, w_ref, cos_ref, sin_ref, q_ref, kv_ref):
    for t in range(6):
        lin = mm(a_low, w_ref[:, 256 * t : 256 * t + 256])
        for k in range(2):
            u = lin[:, 128 * k : 128 * k + 128]
            if t < 4:
                u = u * cos_ref[...] + half_swap(u) * sin_ref[...]
            col = 256 * t + 128 * k
            if col < D:
                q_ref[:, col : col + 128] = u.astype(bf16)
            else:
                kv_ref[:, col - D : col - D + 128] = u.astype(bf16)


def norm_factor(r):
    return lax.rsqrt(jnp.mean(r * r, axis=-1, keepdims=True) + NORM_EPS)


def norm_back(e, r, f, g):
    scaled = e * g
    gain = jnp.sum(e * r * f, axis=0, keepdims=True)
    grad = f * scaled - r * (f * f * f) * jnp.mean(scaled * r, axis=-1, keepdims=True)
    return grad, gain


def head_mask(rows, h):
    lane = lax.broadcasted_iota(jnp.int32, (rows, LANES), 1)
    return (lane >= 64) if h else (lane < 64)


def make_bias(bias, length):
    rows, cols = bias.shape
    first = lax.axis_index("sp") * rows
    row = lax.broadcasted_iota(jnp.int32, (rows, cols), 0) + first
    col = lax.broadcasted_iota(jnp.int32, (rows, cols), 1)
    bias[...] = jnp.where((col <= row) & (col < length), 0.0, -1e9)


def attend(q_ref, kv_ref, bias, p_ref, ctx_ref):
    rows = q_ref.shape[0]

    def pair(i, carry):
        span = pl.ds(pl.multiple_of(i * LANES, LANES), LANES)
        vspan = pl.ds(pl.multiple_of(D + i * LANES, LANES), LANES)
        keys = kv_ref[:, span]
        values = kv_ref[:, vspan]
        queries = q_ref[:, span]
        total = jnp.zeros((rows, LANES), f32)
        for h in range(2):
            qm = jnp.where(head_mask(rows, h), queries, jnp.zeros_like(queries))
            vm = jnp.where(head_mask(values.shape[0], h), values, jnp.zeros_like(values))
            logits = mm_nt(qm, keys) * HEAD_DIM ** (-0.5) + bias[...]
            top = jnp.max(logits, axis=-1, keepdims=True)
            soft = jnp.exp(logits - top)
            norm = 1.0 / jnp.sum(soft, axis=-1, keepdims=True)
            low = (soft * norm).astype(bf16)
            p_ref[2 * i + h] = low
            total = total + mm(low, vm)
        ctx_ref[:, span] = total.astype(bf16)
        return carry

    lax.fori_loop(0, HEADS // 2, pair, 0)


def attend_back(q_ref, kv_ref, p_ref, ectx_ref, eq_ref, dkv_ref):
    rows = q_ref.shape[0]
    cols = kv_ref.shape[0]

    def pair(i, carry):
        span = pl.ds(pl.multiple_of(i * LANES, LANES), LANES)
        vspan = pl.ds(pl.multiple_of(D + i * LANES, LANES), LANES)
        keys = kv_ref[:, span]
        values = kv_ref[:, vspan]
        queries = q_ref[:, span]
        grads = ectx_ref[:, span]
        dq = jnp.zeros((rows, LANES), f32)
        dk = jnp.zeros((LANES, cols), f32)
        dv = jnp.zeros((LANES, cols), f32)
        for h in range(2):
            mask = head_mask(rows, h)
            qm = jnp.where(mask, queries, jnp.zeros_like(queries))
            em = jnp.where(mask, grads, jnp.zeros_like(grads))
            km = jnp.where(head_mask(cols, h), keys, jnp.zeros_like(keys))
            low = p_ref[2 * i + h]
            soft = low.astype(f32)
            dp = mm_nt(em, values)
            center = jnp.sum(soft * dp, axis=-1, keepdims=True)
            raw = (soft * (dp - center) * HEAD_DIM ** (-0.5)).astype(bf16)
            dv = dv + mm_tn(em, low)
            dk = dk + mm_tn(qm, raw)
            dq = dq + mm(raw, km)
        eq_ref[:, span] = dq.astype(bf16)
        dkv_ref[:, span] = dk.T.astype(bf16)
        dkv_ref[:, vspan] = dv.T.astype(bf16)
        return carry

    lax.fori_loop(0, HEADS // 2, pair, 0)


def feed_forward(b_low, gu_ref, down_ref, both_ref, units_ref):
    for t in range(TILES):
        both = mm(b_low, gu_ref[:, 256 * t : 256 * t + 256])
        both_ref[:, 256 * t : 256 * t + 256] = both
        gate, up = both[:, :128], both[:, 128:]
        units_ref[:, 128 * t : 128 * t + 128] = (gate / (1.0 + jnp.exp(-gate)) * up).astype(bf16)
    return mm(units_ref[...], down_ref[...])


def feed_back(e_low, gu_ref, down_ref, both_ref, eboth_ref):
    for t in range(TILES):
        eu = mm_nt(e_low, down_ref[128 * t : 128 * t + 128, :])
        gate = both_ref[:, 256 * t : 256 * t + 128]
        up = both_ref[:, 256 * t + 128 : 256 * t + 256]
        sig = 1.0 / (1.0 + jnp.exp(-gate))
        eboth_ref[:, 256 * t : 256 * t + 128] = (eu * up * sig * (1.0 + gate * (1.0 - sig))).astype(bf16)
        eboth_ref[:, 256 * t + 128 : 256 * t + 256] = (eu * gate * sig).astype(bf16)
    return mm_nt(eboth_ref[...], gu_ref[...])


def stage_head(master_pad, hidden, cos, sin, zn, rows, share):
    tokens = hidden.shape[0]
    step = chunk_rows(rows)
    per_layer = zn * 4
    half_zn = zn // 2
    depth = LAYER_ROWS + rows
    parts = 4

    def body(
        x_ref, h_ref, c_ref, s_ref,
        wq0, wo0, wg0, wd0, g0, wq1, wo1, wg1, wd1, g1, q_ref, all_ref,
        own, slots0, slots1, flat, gate_up, kv, send0, recv0, send1, recv1, ksend, krecv, lsem,
    ):
        z, x, y, c = coords()
        bar = pltpu.get_barrier_semaphore()

        def hello(device):
            pl.semaphore_signal(bar, inc=1, device_id=device, device_id_type=MESH)

        hello(place(z, 1 - x, y, c))
        hello(place(z, x, 1 - y, c))
        hello(place(z, x, y, 1 - c))
        pl.when(z > 0)(lambda: hello(place(z - 1, x, y, c)))
        pl.when(z < zn - 1)(lambda: hello(place(z + 1, x, y, c)))

        shift = lax.rem(share * (((z * 2 + x) * 2 + y) * 2 + c), LANES)
        lane = lax.broadcasted_iota(jnp.int32, (step, LANES), 1)

        def align(i, carry):
            now = pltpu.roll(x_ref[pl.ds(8 + i * step, step), :], shift, 1)
            before = pltpu.roll(x_ref[pl.ds(7 + i * step, step), :], shift, 1)
            own[pl.ds(i * step, step), :] = jnp.where(lane >= shift, now, before).astype(bf16)
            return carry

        lax.fori_loop(0, rows // step, align, 0)
        pl.semaphore_wait(
            bar, 3 + (z > 0).astype(jnp.int32) + (z < zn - 1).astype(jnp.int32)
        )
        zero = Gather(slots0, own, send0, recv0, zn, rows, 0, half_zn)
        one = Gather(slots1, own, send1, recv1, zn, rows, half_zn, zn)
        exchange = KeyExchange(kv, all_ref, ksend, krecv, lsem.at[1], parts)
        zero.keep(lsem.at[0])
        one.keep(lsem.at[0])
        zero.turn(0)
        one.turn(0)
        zero.pump(1, zero.turns)
        zero.arrived()

        sites = 9
        calls = []

        def pump():
            k = len(calls)
            calls.append(k)
            total = one.turns - 1
            one.pump(1 + total * k // sites, 1 + total * (k + 1) // sites)

        fill_flat(slots0, flat, rows, share, 0, per_layer)
        pump()
        take_qkv(flat, wq0, 0, 12)
        pump()
        project_heads(h_ref[...], wq0, c_ref, s_ref, q_ref, kv)
        exchange.start()
        pump()
        take_out(flat, wo0, g0)
        take_down(flat, wd0)
        pump()
        for r in range(8):
            take_gate_up(flat, gate_up, r)
            if r % 2 == 1:
                pump()
        place_gate_up(gate_up, wg0)
        exchange.forward()
        pump()
        one.arrived()
        fill_flat(slots1, flat, rows, share, 0, per_layer)
        take_qkv(flat, wq1, 0, 12)
        take_out(flat, wo1, g1)
        take_down(flat, wd1)
        for r in range(8):
            take_gate_up(flat, gate_up, r)
        place_gate_up(gate_up, wg1)
        exchange.finish()
        zero.sent()
        one.sent()

    layer = [((D, 3 * D), bf16), ((D, D), bf16), ((D, 2 * FFP), bf16), ((FFP, D), bf16), ((2, D), f32)]
    outs = layer + layer + [((tokens, D), bf16), ((4 * tokens, 2 * D), bf16)]
    ins = [master_pad, hidden, cos, sin]
    return pl.pallas_call(
        body,
        out_shape=[jax.ShapeDtypeStruct(s, d) for s, d in outs],
        in_specs=[vmem_spec()] * len(ins),
        out_specs=[vmem_spec()] * len(outs),
        scratch_shapes=[
            pltpu.VMEM((rows, LANES), bf16),
            pltpu.VMEM((per_layer, rows, LANES), bf16),
            pltpu.VMEM((per_layer, rows, LANES), bf16),
            pltpu.VMEM((depth, LANES), f32),
            pltpu.VMEM((2 * TILES, D, LANES), f32),
            pltpu.VMEM((tokens, 2 * D), bf16),
            pltpu.SemaphoreType.DMA((half_zn, 11)),
            pltpu.SemaphoreType.DMA((half_zn, 10)),
            pltpu.SemaphoreType.DMA((half_zn, 11)),
            pltpu.SemaphoreType.DMA((half_zn, 10)),
            pltpu.SemaphoreType.DMA((3, parts)),
            pltpu.SemaphoreType.DMA((3, parts)),
            pltpu.SemaphoreType.DMA((2,)),
        ],
        compiler_params=pltpu.CompilerParams(
            collective_id=1, has_side_effects=True, vmem_limit_bytes=60 * MIB
        ),
    )(*ins)


def stage_first(length, hidden, q, kv, w_out, w_gu, w_down, gains, next_gains, w_qkv, cos, sin):
    rows = hidden.shape[0]
    cols = kv.shape[0]

    def body(
        l_ref, h_ref, q_ref, kv_ref, wo_ref, gu_ref, dn_ref, g_ref, ng_ref, wq_ref, c_ref, s_ref,
        p_ref, ctx_ref, r1_ref, b_ref, both_ref, units_ref, r2_ref, sec_ref, a1_ref, q1_ref, kv1_ref,
        bias,
    ):
        make_bias(bias, l_ref[0])
        attend(q_ref, kv_ref, bias, p_ref, ctx_ref)
        r1 = h_ref[...].astype(f32) + mm(ctx_ref[...], wo_ref[...])
        r1_ref[...] = r1
        first = r1 * norm_factor(r1) * g_ref[0:1, :]
        b_ref[...] = first.astype(bf16)
        r2 = first + feed_forward(b_ref[...], gu_ref, dn_ref, both_ref, units_ref)
        r2_ref[...] = r2
        second = r2 * norm_factor(r2) * g_ref[1:2, :]
        sec_ref[...] = second
        a1_ref[...] = (second * norm_factor(second) * ng_ref[0:1, :]).astype(bf16)
        project_heads(a1_ref[...], wq_ref, c_ref, s_ref, q1_ref, kv1_ref)

    outs = [
        ((HEADS, rows, cols), bf16),
        ((rows, D), bf16),
        ((rows, D), f32),
        ((rows, D), bf16),
        ((rows, 2 * FFP), f32),
        ((rows, FFP), bf16),
        ((rows, D), f32),
        ((rows, D), f32),
        ((rows, D), bf16),
        ((rows, D), bf16),
        ((rows, 2 * D), bf16),
    ]
    ins = [length, hidden, q, kv, w_out, w_gu, w_down, gains, next_gains, w_qkv, cos, sin]
    return pl.pallas_call(
        body,
        out_shape=[jax.ShapeDtypeStruct(s, d) for s, d in outs],
        in_specs=[pl.BlockSpec(memory_space=pltpu.SMEM)] + [vmem_spec()] * (len(ins) - 1),
        out_specs=[vmem_spec()] * len(outs),
        scratch_shapes=[pltpu.VMEM((rows, cols), f32)],
        compiler_params=pltpu.CompilerParams(vmem_limit_bytes=60 * MIB),
    )(*ins)


def stage_second(length, cotangent, second, q, kv, w_out, w_gu, w_down, gains):
    rows = q.shape[0]
    cols = kv.shape[0]

    def body(
        l_ref, cot_ref, sec_ref, q_ref, kv_ref, wo_ref, gu_ref, dn_ref, g_ref,
        o_ref, ctx_ref, b_ref, units_ref, eboth_ref, ef_ref, ea_ref, e3_ref, eq_ref, dkv_ref, gg_ref,
        bias, p_ref, both_ref, ectx_ref,
    ):
        length_now = l_ref[0]
        make_bias(bias, length_now)
        attend(q_ref, kv_ref, bias, p_ref, ctx_ref)
        third = sec_ref[...] + mm(ctx_ref[...], wo_ref[...])
        f4 = norm_factor(third)
        b_ref[...] = (third * f4 * g_ref[1:2, :]).astype(bf16)
        o_ref[...] = third + feed_forward(b_ref[...], gu_ref, dn_ref, both_ref, units_ref)
        place_now = lax.broadcasted_iota(jnp.int32, (rows, D), 0) + lax.axis_index("sp") * rows
        e_out = jnp.where(place_now < length_now, cot_ref[...], 0.0)
        ef_ref[...] = e_out.astype(bf16)
        e_b = feed_back(ef_ref[...], gu_ref, dn_ref, both_ref, eboth_ref)
        grad, gain = norm_back(e_b, third, f4, g_ref[1:2, :])
        gg_ref[...] = gain
        e3 = e_out + grad
        e3_ref[...] = e3
        ea_ref[...] = e3.astype(bf16)
        ectx_ref[...] = mm_nt(ea_ref[...], wo_ref[...]).astype(bf16)
        attend_back(q_ref, kv_ref, p_ref, ectx_ref, eq_ref, dkv_ref)

    outs = [
        ((rows, D), f32),
        ((rows, D), bf16),
        ((rows, D), bf16),
        ((rows, FFP), bf16),
        ((rows, 2 * FFP), bf16),
        ((rows, D), bf16),
        ((rows, D), bf16),
        ((rows, D), f32),
        ((rows, D), bf16),
        ((cols, 2 * D), bf16),
        ((1, D), f32),
    ]
    ins = [length, cotangent, second, q, kv, w_out, w_gu, w_down, gains]
    return pl.pallas_call(
        body,
        out_shape=[jax.ShapeDtypeStruct(s, d) for s, d in outs],
        in_specs=[pl.BlockSpec(memory_space=pltpu.SMEM)] + [vmem_spec()] * (len(ins) - 1),
        out_specs=[vmem_spec()] * len(outs),
        scratch_shapes=[
            pltpu.VMEM((rows, cols), f32),
            pltpu.VMEM((HEADS, rows, cols), bf16),
            pltpu.VMEM((rows, 2 * FFP), f32),
            pltpu.VMEM((rows, D), bf16),
        ],
        compiler_params=pltpu.CompilerParams(vmem_limit_bytes=60 * MIB),
    )(*ins)


def lin_grads(eq_ref, ekv_ref, cos_ref, sin_ref, lin_ref):
    for t in range(12):
        col = 128 * t
        src = eq_ref[:, col : col + 128] if t < 4 else ekv_ref[:, col - D : col - D + 128]
        if t < 8:
            w = src.astype(f32)
            src = (w * cos_ref[...] - half_swap(w) * sin_ref[...]).astype(bf16)
        lin_ref[:, col : col + 128] = src


def stage_back(
    e_q, e_kv, e3, second, next_gains, w_qkv, cos, sin,
    r1, r2, both, gains, w_gu, w_down, w_out, q, kv, p,
):
    rows = e_q.shape[0]
    cols = kv.shape[0]

    def body(
        eq_ref, ekv_ref, e3_ref, sec_ref, ng_ref, wq_ref, c_ref, s_ref,
        r1_ref, r2_ref, both_ref, g_ref, gu_ref, dn_ref, wo_ref, q_ref, kv_ref, p_ref,
        lin_ref, eboth_ref, ef_ref, ea_ref, e1_ref, eq0_ref, dkv_ref, gg_ref,
        ectx_ref,
    ):
        lin_grads(eq_ref, ekv_ref, c_ref, s_ref, lin_ref)
        e_a = mm_nt(lin_ref[...], wq_ref[...])
        second = sec_ref[...]
        grad, gain3 = norm_back(e_a, second, norm_factor(second), ng_ref[0:1, :])
        e2 = e3_ref[...] + grad
        r2 = r2_ref[...]
        er2, gain2 = norm_back(e2, r2, norm_factor(r2), g_ref[1:2, :])
        ef_ref[...] = er2.astype(bf16)
        e_first = er2 + feed_back(ef_ref[...], gu_ref, dn_ref, both_ref, eboth_ref)
        r1 = r1_ref[...]
        er1, gain1 = norm_back(e_first, r1, norm_factor(r1), g_ref[0:1, :])
        e1_ref[...] = er1
        ea_ref[...] = er1.astype(bf16)
        gg_ref[0:1, :] = gain1
        gg_ref[1:2, :] = gain2
        gg_ref[2:3, :] = gain3
        ectx_ref[...] = mm_nt(ea_ref[...], wo_ref[...]).astype(bf16)
        attend_back(q_ref, kv_ref, p_ref, ectx_ref, eq0_ref, dkv_ref)

    return local_call(
        body,
        [
            ((rows, 3 * D), bf16),
            ((rows, 2 * FFP), bf16),
            ((rows, D), bf16),
            ((rows, D), bf16),
            ((rows, D), f32),
            ((rows, D), bf16),
            ((cols, 2 * D), bf16),
            ((3, D), f32),
        ],
        [
            e_q, e_kv, e3, second, next_gains, w_qkv, cos, sin,
            r1, r2, both, gains, w_gu, w_down, w_out, q, kv, p,
        ],
        [pltpu.VMEM((rows, D), bf16)],
    )


def stage_end(e_q, e_kv, e1, w_qkv, cos, sin):
    rows = e_q.shape[0]

    def body(eq_ref, ekv_ref, e1_ref, wq_ref, c_ref, s_ref, lin_ref, o_ref):
        lin_grads(eq_ref, ekv_ref, c_ref, s_ref, lin_ref)
        o_ref[...] = e1_ref[...] + mm_nt(lin_ref[...], wq_ref[...])

    return local_call(
        body, [((rows, 3 * D), bf16), ((rows, D), f32)], [e_q, e_kv, e1, w_qkv, cos, sin]
    )


def reduce_and_update(slots_zero, slots_one, gains_part, master, one, two, zn, rows, share):
    half = rows // 2
    step = chunk_rows(rows)
    ndev = zn * 8
    per_layer = ndev // 2
    turns = rows // step

    def body(
        g0_ref, g1_ref, gp_ref, m_ref, one_ref, two_ref,
        nm_ref, n1_ref, n2_ref, gn_ref, gg_ref,
        acc, rc, rd, rx, ry, rz, fin, sq, sqs, gps, send, recv, lsem, ssem, rsem,
    ):
        z, x, y, c = coords()
        me = ((z * 2 + x) * 2 + y) * 2 + c
        bar = pltpu.get_barrier_semaphore()

        def peer(d):
            tgt = lax.rem(me + d, ndev)
            return {"dp": lax.div(tgt, 4), "sp": lax.rem(tgt, 4)}

        def hello(d, carry):
            pl.semaphore_signal(bar, inc=1, device_id=peer(d), device_id_type=MESH)
            return carry

        lax.fori_loop(1, ndev, hello, 0)

        to_x = place(z, 1 - x, y, c)
        to_y = place(z, x, 1 - y, c)
        to_c = place(z, x, y, 1 - c)
        spots = [(x, y), (1 - x, y), (x, 1 - y), (1 - x, 1 - y)]

        def slot(zp, rel, cp):
            xp, yp = spots[rel]
            return ((zp * 2 + xp) * 2 + yp) * 2 + cp

        def on_source(zp, rel, cp, act):
            index = slot(zp, rel, cp)

            @pl.when(index < per_layer)
            def _():
                act(g0_ref.at[index])

            @pl.when(index >= per_layer)
            def _():
                act(g1_ref.at[index - per_layer])

        def cp(src, dst, zp, s, r, device):
            return remote(src, dst, send.at[zp, s], recv.at[zp, r], device)

        def core_send(zp, rel, src):
            return cp(src, rc.at[zp, rel], zp, rel, rel, to_c)

        def load(zp, rel, src):
            return pltpu.make_async_copy(src, acc.at[zp, rel], lsem.at[zp, rel])

        def diag_a(zp):
            return cp(acc.at[zp, 3, pl.ds(0, half)], rd.at[zp, pl.ds(0, half)], zp, 4, 4, to_y)

        def diag_b(zp):
            return cp(acc.at[zp, 3, pl.ds(half, half)], rd.at[zp, pl.ds(half, half)], zp, 5, 5, to_x)

        def send_x(zp):
            return cp(acc.at[zp, 1], rx.at[zp], zp, 6, 6, to_x)

        def send_y(zp):
            return cp(acc.at[zp, 2], ry.at[zp], zp, 7, 7, to_y)

        def right(zp):
            return cp(acc.at[zp, 0], rz.at[zp, 0], zp, 8, 8, place(z + 1, x, y, c))

        def left(zp):
            return cp(acc.at[zp, 0], rz.at[zp, 1], zp, 8, 9, place(z - 1, x, y, c))

        def add_into(dst, low, high, *srcs):
            size = step if (high - low) % step == 0 else 16

            def one_step(i, carry):
                span = pl.ds(pl.multiple_of(low + i * size, 16), size)
                value = dst[span, :].astype(f32)
                for src in srcs:
                    value = value + src[span, :].astype(f32)
                dst[span, :] = value.astype(bf16)
                return carry

            lax.fori_loop(0, (high - low) // size, one_step, 0)

        def valid(k):
            zp = order_at(2 * zn - 2 - k, z)
            return zp, (k >= 0) & (k < 2 * zn - 1) & (zp >= 0) & (zp < zn)

        def stage_c(k):
            zp, ok = valid(k)

            @pl.when(ok)
            def _():
                for rel in (3, 1, 2, 0):
                    on_source(zp, rel, 1 - c, lambda src, rel=rel: core_send(zp, rel, src).start())
                    on_source(zp, rel, c, lambda src, rel=rel: load(zp, rel, src).start())

        def stage_one(k):
            zp, ok = valid(k)

            @pl.when(ok)
            def _():
                for rel in (3, 1, 2, 0):
                    core_send(zp, rel, g0_ref.at[0]).wait_recv()
                    load(zp, rel, g0_ref.at[0]).wait()
                    add_into(acc.at[zp, rel], 0, rows, rc.at[zp, rel])
                    if rel == 3:
                        diag_a(zp).start()
                        diag_b(zp).start()

        def stage_two(k):
            zp, ok = valid(k)

            @pl.when(ok)
            def _():
                diag_a(zp).wait_recv()
                add_into(acc.at[zp, 1], 0, half, rd.at[zp])
                send_x(zp).start()
                diag_b(zp).wait_recv()
                add_into(acc.at[zp, 2], half, rows, rd.at[zp])
                send_y(zp).start()

        def stage_three(k):
            zp, ok = valid(k)

            @pl.when(ok & (zp != z))
            def _():
                send_x(zp).wait_recv()
                send_y(zp).wait_recv()
                add_into(acc.at[zp, 0], 0, rows, rx.at[zp], ry.at[zp])

                @pl.when((zp > z) & (z > 0))
                def _():
                    right(zp).wait_recv()
                    add_into(acc.at[zp, 0], 0, rows, rz.at[zp, 0])

                @pl.when((zp < z) & (z < zn - 1))
                def _():
                    left(zp).wait_recv()
                    add_into(acc.at[zp, 0], 0, rows, rz.at[zp, 1])

                pl.when(zp > z)(lambda: right(zp).start())
                pl.when(zp < z)(lambda: left(zp).start())

        pl.semaphore_wait(bar, ndev - 1)

        def tell(src, dst, s):
            def go(d, carry):
                remote(src, dst.at[me], ssem.at[s], rsem.at[s], peer(d)).start()
                return carry

            lax.fori_loop(1, ndev, go, 0)

        def hear(dst, s):
            part = dst.at[pl.ds(0, ndev - 1)]
            both = remote(part, part, ssem.at[s], rsem.at[s], to_c)
            both.wait_send()
            both.wait_recv()

        for k in range(3):
            stage_c(k)
        tell(gp_ref, gps, 0)
        gps[me] = gp_ref[...]

        def turn(k, carry):
            stage_one(k)
            stage_c(k + 3)
            stage_two(k - 1)
            stage_three(k - 2)
            return carry

        lax.fori_loop(0, 2 * zn + 1, turn, 0)

        send_x(z).wait_recv()
        send_y(z).wait_recv()
        pl.when(z > 0)(lambda: right(z).wait_recv())
        pl.when(z < zn - 1)(lambda: left(z).wait_recv())

        def total(i, carry):
            span = pl.ds(pl.multiple_of(i * step, 16), step)
            value = (
                acc[z, 0, span, :].astype(f32)
                + rx[z, span, :].astype(f32)
                + ry[z, span, :].astype(f32)
            )
            value = value + jnp.where(z > 0, rz[z, 0, span, :].astype(f32), 0.0)
            value = value + jnp.where(z < zn - 1, rz[z, 1, span, :].astype(f32), 0.0)
            fin[span, :] = value
            return carry

        lax.fori_loop(0, turns, total, 0)
        fin[pl.ds(rows, 8), :] = jnp.zeros((8, LANES), f32)

        shift = lax.rem(share * me, LANES)
        back = lax.rem(LANES - shift, LANES)
        lane = lax.broadcasted_iota(jnp.int32, (step, LANES), 1)
        row = lax.broadcasted_iota(jnp.int32, (step, LANES), 0)

        def realign(i, carry):
            now = pltpu.roll(fin[pl.ds(i * step, step), :], back, 1)
            after = pltpu.roll(fin[pl.ds(i * step + 1, step), :], back, 1)
            value = jnp.where(lane < LANES - shift, now, after)
            value = jnp.where((row + i * step) * LANES + lane < share, value, 0.0)
            n1_ref[pl.ds(i * step, step), :] = value
            square = value * value
            return carry + jnp.sum(square.reshape(step // 8, 8, LANES), axis=0)

        sq[...] = lax.fori_loop(0, turns, realign, jnp.zeros((8, LANES), f32))
        tell(sq, sqs, 1)
        sqs[me] = sq[...]

        def finish(i, carry):
            for rel in range(4):
                core_send(i, rel, g0_ref.at[0]).wait_send()
            for item in (diag_a(i), diag_b(i), send_x(i), send_y(i)):
                item.wait_send()
            pl.when(i > z)(lambda: right(i).wait_send())
            pl.when(i < z)(lambda: left(i).wait_send())
            return carry

        lax.fori_loop(0, zn, finish, 0)
        hear(gps, 0)
        gg_ref[...] = lax.fori_loop(
            1, ndev, lambda i, s: s + gps[i], gps[0]
        )
        hear(sqs, 1)
        squares = lax.fori_loop(1, ndev, lambda i, s: s + sqs[i], sqs[0])
        norm = jnp.sqrt(jnp.sum(squares, keepdims=True))
        gn_ref[...] = jnp.broadcast_to(norm, (8, LANES))
        scale = jnp.minimum(1.0, 1.0 / norm)
        correction = 1.0 - 0.5**STEP

        def update(i, carry):
            span = pl.ds(pl.multiple_of(i * step, 16), step)
            clipped = n1_ref[span, :] * scale
            new_one = 0.5 * one_ref[span, :] + 0.5 * clipped
            new_two = 0.5 * two_ref[span, :] + 0.5 * clipped * clipped
            n1_ref[span, :] = new_one
            n2_ref[span, :] = new_two
            nm_ref[span, :] = m_ref[pl.ds(8 + i * step, step), :] * (
                1.0 - LEARN_RATE * DECAY_RATE
            ) - LEARN_RATE * (new_one / correction) / (jnp.sqrt(new_two / correction) + ADAM_EPS)
            return carry

        lax.fori_loop(0, turns, update, 0)

    flat = jax.ShapeDtypeStruct((rows, LANES), f32)
    return pl.pallas_call(
        body,
        out_shape=[
            flat,
            flat,
            flat,
            jax.ShapeDtypeStruct((8, LANES), f32),
            jax.ShapeDtypeStruct((16, LANES), f32),
        ],
        in_specs=[any_spec(), any_spec()] + [vmem_spec()] * 4,
        out_specs=[vmem_spec()] * 5,
        scratch_shapes=[
            pltpu.VMEM((zn, 4, rows, LANES), bf16),
            pltpu.VMEM((zn, 4, rows, LANES), bf16),
            pltpu.VMEM((zn, rows, LANES), bf16),
            pltpu.VMEM((zn, rows, LANES), bf16),
            pltpu.VMEM((zn, rows, LANES), bf16),
            pltpu.VMEM((zn, 2, rows, LANES), bf16),
            pltpu.VMEM((rows + 8, LANES), f32),
            pltpu.VMEM((8, LANES), f32),
            pltpu.VMEM((ndev, 8, LANES), f32),
            pltpu.VMEM((ndev, 16, LANES), f32),
            pltpu.SemaphoreType.DMA((zn, 9)),
            pltpu.SemaphoreType.DMA((zn, 10)),
            pltpu.SemaphoreType.DMA((zn, 4)),
            pltpu.SemaphoreType.DMA((2,)),
            pltpu.SemaphoreType.DMA((2,)),
        ],
        compiler_params=pltpu.CompilerParams(
            collective_id=4, has_side_effects=True, vmem_limit_bytes=60 * MIB
        ),
    )(slots_zero, slots_one, gains_part, master, one, two)


def rope_rows(rows):
    frequency = jnp.exp(
        -jnp.log(10000.0) * jnp.arange(HEAD_DIM // 2).astype(f32) * 2.0 / HEAD_DIM
    )
    positions = lax.axis_index("sp") * rows + jnp.arange(rows)
    angles = positions.astype(f32)[:, None] * frequency[None, :]
    cos = jnp.cos(angles)
    sin = jnp.sin(angles)
    return (
        jnp.concatenate([cos] * 4, axis=1),
        jnp.concatenate([-sin, sin, -sin, sin], axis=1),
    )


def step_shard(dp_size, sp_size, hidden_in, cotangent, lengths, master, moment_one, moment_two):
    share = master.shape[0]
    zn = dp_size // 2
    per_layer = dp_size * sp_size // 2
    rows = -(-(-(-share // LANES) + 1) // 32) * 32
    seqs, tokens, width = hidden_in.shape

    def pad(flat, lead):
        return jnp.pad(flat, (lead * LANES, rows * LANES - share)).reshape(rows + lead, LANES)

    master_pad = pad(master, 8)
    cos, sin = rope_rows(tokens)
    hidden = hidden_in.reshape(tokens, width)

    def join(kv):
        return exchange_keys(kv).reshape(4 * tokens, 2 * width)

    def collect(dkv):
        return collect_keys(dkv.reshape(4, tokens, 2 * width))

    wq0, wo0, wg0, wd0, g0, wq1, wo1, wg1, wd1, g1, q0, kv0 = stage_head(
        master_pad, hidden, cos, sin, zn, rows, share
    )
    p0, ctx0, r1, b0, both0, units0, r2, second, a1, q1, kv1 = stage_first(
        lengths, hidden, q0, kv0, wo0, wg0, wd0, g0, g1, wq1, cos, sin
    )
    kv1 = join(kv1)
    output, ctx1, b1, units1, eboth1, ef1, ea1, e3, eq1, dkv1, gain4 = stage_second(
        lengths, cotangent.reshape(tokens, width), second, q1, kv1, wo1, wg1, wd1, g1
    )
    ekv1 = collect(dkv1)
    lin1, eboth0, ef0, ea0, e1, eq0, dkv0, gains3 = stage_back(
        eq1, ekv1, e3, second, g1, wq1, cos, sin, r1, r2, both0, g0, wg0, wd0, wo0, q0, kv0, p0
    )
    gains_one = jnp.concatenate([gains3[2:3], gain4], axis=0)
    grads_one = weight_grads(
        a1, lin1, ctx1, ea1, b1, eboth1, units1, ef1, gains_one, rows, share, per_layer
    )
    ekv0 = collect(dkv0)
    lin0, input_grad = stage_end(eq0, ekv0, e1, wq0, cos, sin)
    gains_zero = gains3[0:2]
    grads_zero = weight_grads(
        hidden, lin0, ctx0, ea0, b0, eboth0, units0, ef0, gains_zero, rows, share, per_layer
    )
    gains_part = jnp.concatenate([gains_zero, gains_one], axis=0).reshape(16, LANES)
    new_master, new_one, new_two, norm, gains = reduce_and_update(
        grads_zero, grads_one, gains_part, master_pad, pad(moment_one, 0), pad(moment_two, 0),
        zn, rows, share,
    )

    def flat(value):
        return value.reshape(-1)[:share]

    new_master = flat(new_master)
    return (
        output.reshape(hidden_in.shape),
        input_grad.reshape(hidden_in.shape),
        new_master,
        flat(new_one),
        flat(new_two),
        new_master.astype(bf16),
        norm[0, 0],
        gains.reshape(2, 2, width),
    )


def solution(mesh):
    in_specs = (
        P("dp", "sp", None),
        P("dp", "sp", None),
        P("dp"),
        P(("dp", "sp")),
        P(("dp", "sp")),
        P(("dp", "sp")),
    )
    out_specs = (
        P("dp", "sp", None),
        P("dp", "sp", None),
        P(("dp", "sp")),
        P(("dp", "sp")),
        P(("dp", "sp")),
        P(("dp", "sp")),
        P(),
        P(),
    )
    body = functools.partial(step_shard, mesh.shape["dp"], mesh.shape["sp"])
    return jax.shard_map(body, mesh=mesh, in_specs=in_specs, out_specs=out_specs, check_vma=False)
```

```python
import functools

import jax
import jax.numpy as jnp
from jax import lax
from jax.experimental import pallas as pl
from jax.experimental.pallas import tpu as pltpu
from jax.sharding import PartitionSpec as P

D = 512
HEADS = 8
HEAD_DIM = 64
FF = 1368
FFP = 1408
TILES = 11
STEP = 5
NORM_EPS = 1e-06
ADAM_EPS = 1e-08
LEARN_RATE = 0.02
DECAY_RATE = 0.01
LANES = 128
LAYER_ROWS = 24616
BASE_OUT = 6144
BASE_GU = 8192
BASE_DOWN = 19136
BASE_GAINS = 24608
GU_ROW = 2 * FF
PERIOD = 171
MESH = pl.DeviceIdType.MESH
MIB = 1 << 20
f32 = jnp.float32
bf16 = jnp.bfloat16


def mm(a, b):
    return lax.dot_general(a, b, (((1,), (0,)), ((), ())), preferred_element_type=f32)


def mm_nt(a, b):
    return lax.dot_general(a, b, (((1,), (1,)), ((), ())), preferred_element_type=f32)


def mm_tn(a, b):
    return lax.dot_general(a, b, (((0,), (0,)), ((), ())), preferred_element_type=f32)


def chunk_rows(rows):
    tiles = rows // 16
    best = max(d for d in range(1, 17) if tiles % d == 0)
    return best * 16


def vmem_spec():
    return pl.BlockSpec(memory_space=pltpu.VMEM)


def any_spec():
    return pl.BlockSpec(memory_space=pl.ANY)


def local_call(body, outs, ins, scratch=(), limit=60, flops=0):
    return pl.pallas_call(
        body,
        out_shape=[jax.ShapeDtypeStruct(s, d) for s, d in outs],
        in_specs=[vmem_spec()] * len(ins),
        out_specs=[vmem_spec()] * len(outs),
        scratch_shapes=list(scratch),
        compiler_params=pltpu.CompilerParams(vmem_limit_bytes=limit * MIB),
    )(*ins)


def coords():
    dp = lax.axis_index("dp")
    sp = lax.axis_index("sp")
    return lax.div(dp, 2), lax.rem(dp, 2), lax.div(sp, 2), lax.rem(sp, 2)


def place(z, x, y, c):
    return {"dp": z * 2 + x, "sp": y * 2 + c}


def remote(src, dst, send_sem, recv_sem, device):
    return pltpu.make_async_remote_copy(
        src_ref=src,
        dst_ref=dst,
        send_sem=send_sem,
        recv_sem=recv_sem,
        device_id=device,
        device_id_type=MESH,
    )


def order_at(tau, z):
    step = lax.div(tau + 1, 2)
    return z + jnp.where(lax.rem(tau, 2) == 1, -step, step)


class Gather:
    lag = 1

    def __init__(self, slots, send, recv, zn, rows):
        self.slots, self.send, self.recv, self.zn = slots, send, recv, zn
        self.parts = 2 if rows > 1000 else 1
        self.size = rows // self.parts
        self.half = self.size // 32 * 16
        self.steps = zn * self.parts
        self.turns = self.steps + 2 * self.lag
        self.z, self.x, self.y, self.c = coords()
        z, x, y, c = self.z, self.x, self.y, self.c
        self.to_x = place(z, 1 - x, y, c)
        self.to_y = place(z, x, 1 - y, c)
        self.to_c = place(z, x, y, 1 - c)
        self.ahead = z >= zn // 2

    def until(self, zp):
        return zp * self.parts + 2 * self.lag if zp < self.zn else self.turns

    def at(self, k):
        return lax.div(k, self.parts), lax.rem(k, self.parts) * self.size

    def ref(self, k, xp, yp, low=0, size=None):
        zp, base = self.at(k)
        span = pl.ds(pl.multiple_of(base + low, 16), self.size if size is None else size)
        return self.slots.at[zp, self.c, xp * 2 + yp, span]

    def cp(self, ref, k, s, r, device):
        return remote(ref, ref, self.send.at[k, s], self.recv.at[k, r], device)

    def right(self, k):
        return self.cp(self.ref(k, self.x, self.y), k, 0, 0, place(self.z + 1, self.x, self.y, self.c))

    def left(self, k):
        return self.cp(self.ref(k, self.x, self.y), k, 1, 0, place(self.z - 1, self.x, self.y, self.c))

    def over_x(self, k):
        return self.cp(self.ref(k, self.x, self.y), k, 2, 1, self.to_x)

    def over_y(self, k):
        return self.cp(self.ref(k, self.x, self.y), k, 3, 2, self.to_y)

    def upper(self, k):
        return self.cp(self.ref(k, 1 - self.x, self.y, 0, self.half), k, 4, 3, self.to_y)

    def lower(self, k):
        ref = self.ref(k, self.x, 1 - self.y, self.half, self.size - self.half)
        return self.cp(ref, k, 5, 4, self.to_x)

    def over_c(self, k, c):
        zp, base = self.at(k)
        ref = self.slots.at[zp, c, :, pl.ds(pl.multiple_of(base, 16), self.size)]
        return self.cp(ref, k, 6, 5, self.to_c)

    def arrival(self, ref, k, r):
        self.cp(ref, k, 0, r, self.to_c).wait_recv()

    def issue(self, k):
        zp, base = self.at(k)
        z = self.z
        pl.when((zp <= z) & (z < self.zn - 1))(lambda: self.right(k).start())
        pl.when((zp >= z) & (z > 0))(lambda: self.left(k).start())
        self.over_x(k).start()
        self.over_y(k).start()

    def begin(self):
        @pl.when(self.ahead)
        def _():
            for j in range(self.parts):
                self.issue(self.z * self.parts + j)

    def turn(self, k):
        z, x, y = self.z, self.x, self.y
        zp, base = self.at(k)

        @pl.when((k < self.steps) & ((zp != z) | (z < self.zn // 2)))
        def _():
            pl.when(zp != z)(lambda: self.arrival(self.ref(k, x, y), k, 0))
            self.issue(k)

        q = k - self.lag

        @pl.when((q >= 0) & (q < self.steps))
        def _():
            self.arrival(self.ref(q, 1 - x, y), q, 1)
            self.upper(q).start()
            self.arrival(self.ref(q, x, 1 - y), q, 2)
            self.lower(q).start()

        r = k - 2 * self.lag

        @pl.when((r >= 0) & (r < self.steps))
        def _():
            self.arrival(self.ref(r, 1 - x, 1 - y, 0, self.half), r, 3)
            self.arrival(self.ref(r, 1 - x, 1 - y, self.half, self.size - self.half), r, 4)
            self.over_c(r, self.c).start()

    def pump(self, low, high):
        def one(k, carry):
            self.turn(k)
            return carry

        if high > low:
            lax.fori_loop(low, high, one, 0)

    def arrived(self, low, high):
        def one(k, carry):
            self.over_c(k, 1 - self.c).wait_recv()
            return carry

        lax.fori_loop(low * self.parts, high * self.parts, one, 0)

    def sent(self):
        z = self.z

        def one(k, carry):
            zp, base = self.at(k)
            pl.when((zp <= z) & (z < self.zn - 1))(lambda: self.right(k).wait_send())
            pl.when((zp >= z) & (z > 0))(lambda: self.left(k).wait_send())
            for item in (self.over_x(k), self.over_y(k), self.upper(k), self.lower(k)):
                item.wait_send()
            self.over_c(k, self.c).wait_send()
            return carry

        lax.fori_loop(0, self.steps, one, 0)


class KeyExchange:
    def __init__(self, kv_ref, all_ref, send, recv, lsem, parts):
        z, x, y, c = coords()
        rows = kv_ref.shape[0]
        piece = rows // parts
        to_y = place(z, x, 1 - y, c)
        to_c = place(z, x, y, 1 - c)
        mine = y * 2 + c
        beyond = (1 - y) * 2 + c
        self.parts = parts

        def part(row, k):
            return all_ref.at[pl.ds(pl.multiple_of(row * rows, rows) + k * piece, piece)]

        self.keep = pltpu.make_async_copy(
            kv_ref, all_ref.at[pl.ds(pl.multiple_of(mine * rows, rows), rows)], lsem
        )
        self.own_y, self.own_c, self.pass_c = [], [], []
        for k in range(parts):
            src, dst = kv_ref.at[pl.ds(k * piece, piece)], part(mine, k)
            self.own_y.append(remote(src, dst, send.at[0, k], recv.at[0, k], to_y))
            self.own_c.append(remote(src, dst, send.at[1, k], recv.at[1, k], to_c))
            ref = part(beyond, k)
            self.pass_c.append(remote(ref, ref, send.at[2, k], recv.at[2, k], to_c))

    def start(self):
        self.keep.start()
        for item in self.own_y + self.own_c:
            item.start()

    def forward(self):
        for k in range(self.parts):
            self.own_y[k].wait_recv()
            self.pass_c[k].start()

    def finish(self):
        for k in range(self.parts):
            self.own_c[k].wait_recv()
            self.pass_c[k].wait_recv()
        for item in self.own_y + self.own_c + self.pass_c:
            item.wait_send()
        self.keep.wait()


REGIONS = {"qkv": (0, BASE_OUT), "out": (BASE_OUT, BASE_GU), "gu": (BASE_GU, BASE_DOWN), "down": (BASE_DOWN, LAYER_ROWS)}
GROUPS = ((0, 6), (6, TILES))


def fill_flat(slots, flat, layer, name, rows, share):
    low, high = REGIONS[name]
    step = chunk_rows(rows)
    per_layer = LAYER_ROWS * LANES // share

    def one(i, carry):
        start = lax.div(share * i, LANES) - low + rows
        shift = lax.rem(share * i, LANES)
        index = i + layer * per_layer
        z, x = lax.div(index, 8), lax.rem(lax.div(index, 4), 2)
        y, c = lax.rem(lax.div(index, 2), 2), lax.rem(index, 2)
        edge = flat[pl.ds(start, 1), :]

        def fill(j, inner):
            flat[pl.ds(start + j * step, step), :] = slots[
                z, c, x * 2 + y, pl.ds(j * step, step), :
            ].astype(f32)
            return inner

        lax.fori_loop(0, rows // step, fill, 0)

        @pl.when(shift > 0)
        def _():
            flat[pl.ds(start, 1), :] = flat[pl.ds(start, 1), :] + edge

        return carry

    lax.fori_loop(low * LANES // share, (high * LANES - 1) // share + 1, one, 0)


def take_qkv(flat, top, qkv_ref):
    for col in range(12):
        qkv_ref[:, 128 * col : 128 * col + 128] = flat[pl.ds(top + col, D, stride=12), :].astype(bf16)


def take_out(flat, top, out_ref):
    for col in range(4):
        span = slice(128 * col, 128 * col + 128)
        out_ref[:, span] = flat[pl.ds(top + col, D, stride=4), :].astype(bf16)


def take_down(flat, top, down_ref, gains_ref):
    base = top + BASE_GAINS - BASE_DOWN
    for col in range(4):
        span = slice(128 * col, 128 * col + 128)
        down_ref[0:FF, span] = flat[pl.ds(top + col, FF, stride=4), :].astype(bf16)
        gains_ref[:, span] = flat[pl.ds(base + col, 2, stride=4), :]
    down_ref[FF:FFP, :] = jnp.zeros((FFP - FF, D), bf16)


def take_gate_up(flat, top, gate_up, gu_ref, group):
    lane = lax.broadcasted_iota(jnp.int32, (64, LANES), 1)
    low, high = group
    for r in range(8):
        for part in range(2):
            for tile in range(low, high):
                first = GU_ROW * r + FF * part + LANES * tile
                q, s = first // LANES, first % LANES
                value = flat[pl.ds(top + q, 64, stride=PERIOD), :]
                if s:
                    after = flat[pl.ds(top + q + 1, 64, stride=PERIOD), :]
                    value = jnp.where(
                        lane < LANES - s,
                        pltpu.roll(value, LANES - s, 1),
                        pltpu.roll(after, LANES - s, 1),
                    )
                if tile == TILES - 1:
                    value = jnp.where(lane < FF - LANES * tile, value, 0.0)
                gate_up[2 * (tile - low) + part, pl.ds(r, 64, stride=8), :] = value
    for k in range(2 * (high - low)):
        span = slice(256 * low + 128 * k, 256 * low + 128 * k + 128)
        gu_ref[:, span] = gate_up[k].astype(bf16)


def gate_up_segments(q):
    pieces = []
    place_now = LANES * q
    end = place_now + LANES
    while place_now < end:
        r, within = divmod(place_now, GU_ROW)
        part, unit = divmod(within, FF)
        tile, lane_src = divmod(unit, LANES)
        room = min(end - place_now, FF - unit, LANES - lane_src)
        lane_dst = place_now - LANES * q
        pieces.append((r, 2 * tile + part, lane_dst, lane_dst + room, (lane_dst - lane_src) % LANES))
        place_now += room
    return pieces


def gate_up_rows(tile):
    out = []
    for q in range(PERIOD):
        pieces = gate_up_segments(q)
        if max(k // 2 for _, k, _, _, _ in pieces) == tile:
            out.append((q, pieces))
    return out


def grad_qkv(flat, a_low, lin_ref):
    for t in range(6):
        value = mm_tn(a_low, lin_ref[:, 256 * t : 256 * t + 256])
        for k in range(2):
            flat[pl.ds(2 * t + k, D, stride=12), :] = value[:, 128 * k : 128 * k + 128]


def grad_out(flat, ctx, ea):
    for t in range(2):
        value = mm_tn(ctx, ea[:, 256 * t : 256 * t + 256])
        for k in range(2):
            flat[pl.ds(BASE_OUT + 2 * t + k, D, stride=4), :] = value[:, 128 * k : 128 * k + 128]


def grad_down(flat, units, ef):
    for t in range(2):
        value = mm_tn(units, ef[:, 256 * t : 256 * t + 256])
        for k in range(2):
            start = BASE_DOWN - BASE_GU + 2 * t + k
            flat[pl.ds(start, FF, stride=4), :] = value[0:FF, 128 * k : 128 * k + 128]


def grad_gate_up(flat, ring, t, b_low, eboth_ref):
    def at(tile):
        return 2 if tile == 0 else tile % 2

    value = mm_tn(b_low, eboth_ref[:, 256 * t : 256 * t + 256])
    for k in range(2):
        ring[2 * at(t) + k] = value[:, 128 * k : 128 * k + 128]
    lane = lax.broadcasted_iota(jnp.int32, (64, LANES), 1)
    for q, pieces in gate_up_rows(t):
        total = None
        for r, k, low, high, turn in pieces:
            piece = ring[2 * at(k // 2) + k % 2, pl.ds(r, 64, stride=8), :]
            if turn:
                piece = pltpu.roll(piece, turn, 1)
            total = piece if total is None else jnp.where(lane < low, total, piece)
        flat[pl.ds(q, 64, stride=PERIOD), :] = total


def grad_gains(flat, first, second):
    base = BASE_GAINS - BASE_GU
    for col in range(4):
        flat[pl.ds(base + col, 1), :] = first[:, 128 * col : 128 * col + 128]
        flat[pl.ds(base + 4 + col, 1), :] = second[:, 128 * col : 128 * col + 128]
    flat[LAYER_ROWS - BASE_GU :, :] = jnp.zeros((flat.shape[0] - LAYER_ROWS + BASE_GU, LANES), f32)


def flat_rows(rows):
    return LAYER_ROWS - BASE_GU + rows


def split_slot(share):
    return BASE_GU * LANES // share + 1


def carry_edge(flat, rows):
    flat[BASE_GU : BASE_GU + rows, :] = flat[0:rows, :]


def emit_slots(flat, base, stage, out_ref, sem, rows, share, low, high):
    step = chunk_rows(rows)

    def put(i):
        k = lax.rem(i, 2)
        return pltpu.make_async_copy(stage.at[k], out_ref.at[i], sem.at[k])

    def one(i, carry):
        pl.when(i >= low + 2)(lambda: put(i - 2).wait())
        start = lax.div(share * i, LANES) - base
        k = lax.rem(i, 2)

        def fill(j, inner):
            stage[k, pl.ds(j * step, step), :] = flat[pl.ds(start + j * step, step), :].astype(bf16)
            return inner

        lax.fori_loop(0, rows // step, fill, 0)
        put(i).start()
        return carry

    lax.fori_loop(low, high, one, 0)
    put(high - 2).wait()
    put(high - 1).wait()


class KeySum:
    def __init__(self, part_ref, sum_ref, from_c, pair, from_y, send, recv):
        z, x, y, c = coords()
        self.part, self.sum_ref = part_ref, sum_ref
        self.from_c, self.pair, self.from_y = from_c, pair, from_y
        self.send, self.recv = send, recv
        self.rows = pair.shape[1]
        self.y, self.c = y, c
        self.to_y = place(z, x, 1 - y, c)
        self.to_c = place(z, x, y, 1 - c)

    def block(self, i, yp, cp):
        start = pl.multiple_of((yp * 2 + cp) * self.rows, self.rows)
        return self.part.at[i, pl.ds(start, self.rows)]

    def near(self, i, h):
        yp = self.y if h else 1 - self.y
        return remote(
            self.block(i, yp, 1 - self.c), self.from_c.at[h, i],
            self.send.at[i, h], self.recv.at[i, h], self.to_c,
        )

    def wide(self, i):
        return remote(
            self.pair.at[i], self.from_y.at[i], self.send.at[i, 2], self.recv.at[i, 2], self.to_y
        )

    def start(self, i):
        self.near(i, 0).start()
        self.near(i, 1).start()

    def middle(self, i):
        self.near(i, 0).wait_recv()
        self.pair[i] = (
            self.from_c[0, i].astype(f32) + self.block(i, 1 - self.y, self.c)[...].astype(f32)
        ).astype(bf16)
        self.wide(i).start()

    def end(self, i):
        self.near(i, 1).wait_recv()
        self.wide(i).wait_recv()
        total = (
            self.from_c[1, i].astype(f32)
            + self.block(i, self.y, self.c)[...].astype(f32)
            + self.from_y[i].astype(f32)
        ).astype(bf16)
        self.sum_ref[:, LANES * i : LANES * i + LANES] = total[:, :LANES]
        self.sum_ref[:, D + LANES * i : D + LANES * i + LANES] = total[:, LANES:]

    def sent(self):
        for i in range(HEADS // 2):
            self.near(i, 0).wait_send()
            self.near(i, 1).wait_send()
            self.wide(i).wait_send()


def key_sum_scratch(rows):
    pairs = HEADS // 2
    return [
        pltpu.VMEM((pairs, 4 * rows, 2 * LANES), bf16),
        pltpu.VMEM((2, pairs, rows, 2 * LANES), bf16),
        pltpu.VMEM((pairs, rows, 2 * LANES), bf16),
        pltpu.VMEM((pairs, rows, 2 * LANES), bf16),
        pltpu.SemaphoreType.DMA((pairs, 3)),
        pltpu.SemaphoreType.DMA((pairs, 3)),
    ]


def half_swap(u):
    lane = lax.broadcasted_iota(jnp.int32, u.shape, 1)
    return jnp.where(lax.rem(lane, 64) < 32, pltpu.roll(u, 96, 1), pltpu.roll(u, 32, 1))


def project_heads(a_low, w_ref, cos_ref, sin_ref, q_ref, kv_ref, tiles=range(6)):
    for t in tiles:
        lin = mm(a_low, w_ref[:, 256 * t : 256 * t + 256])
        for k in range(2):
            u = lin[:, 128 * k : 128 * k + 128]
            if t < 4:
                u = u * cos_ref[...] + half_swap(u) * sin_ref[...]
            col = 256 * t + 128 * k
            if col < D:
                q_ref[:, col : col + 128] = u.astype(bf16)
            else:
                kv_ref[:, col - D : col - D + 128] = u.astype(bf16)


def norm_factor(r):
    return lax.rsqrt(jnp.mean(r * r, axis=-1, keepdims=True) + NORM_EPS)


def norm_back(e, r, f, g):
    scaled = e * g
    gain = jnp.sum(e * r * f, axis=0, keepdims=True)
    grad = f * scaled - r * (f * f * f) * jnp.mean(scaled * r, axis=-1, keepdims=True)
    return grad, gain


def head_mask(rows, h):
    lane = lax.broadcasted_iota(jnp.int32, (rows, LANES), 1)
    return (lane >= 64) if h else (lane < 64)


def make_bias(bias, length):
    rows, cols = bias.shape
    first = lax.axis_index("sp") * rows
    row = lax.broadcasted_iota(jnp.int32, (rows, cols), 0) + first
    col = lax.broadcasted_iota(jnp.int32, (rows, cols), 1)
    bias[...] = jnp.where((col <= row) & (col < length), 0.0, -1e9)


def attend(i, q_ref, kv_ref, bias, p_ref, ctx_ref):
    rows = q_ref.shape[0]
    span = slice(LANES * i, LANES * i + LANES)
    keys = kv_ref[:, span]
    values = kv_ref[:, D + LANES * i : D + LANES * i + LANES]
    queries = q_ref[:, span]
    total = jnp.zeros((rows, LANES), f32)
    for h in range(2):
        qm = jnp.where(head_mask(rows, h), queries, jnp.zeros_like(queries))
        vm = jnp.where(head_mask(values.shape[0], h), values, jnp.zeros_like(values))
        logits = mm_nt(qm, keys) * HEAD_DIM ** (-0.5) + bias[...]
        top = jnp.max(logits, axis=-1, keepdims=True)
        soft = jnp.exp(logits - top)
        norm = 1.0 / jnp.sum(soft, axis=-1, keepdims=True)
        low = (soft * norm).astype(bf16)
        p_ref[2 * i + h] = low
        total = total + mm(low, vm)
    ctx_ref[:, span] = total.astype(bf16)


def attend_back(i, q_ref, kv_ref, p_ref, ectx_ref, eq_ref, dkv_ref):
    rows = q_ref.shape[0]
    cols = kv_ref.shape[0]
    span = slice(LANES * i, LANES * i + LANES)
    keys = kv_ref[:, span]
    values = kv_ref[:, D + LANES * i : D + LANES * i + LANES]
    queries = q_ref[:, span]
    grads = ectx_ref[:, span]
    dq = jnp.zeros((rows, LANES), f32)
    dk = jnp.zeros((LANES, cols), f32)
    dv = jnp.zeros((LANES, cols), f32)
    for h in range(2):
        mask = head_mask(rows, h)
        qm = jnp.where(mask, queries, jnp.zeros_like(queries))
        em = jnp.where(mask, grads, jnp.zeros_like(grads))
        km = jnp.where(head_mask(cols, h), keys, jnp.zeros_like(keys))
        low = p_ref[2 * i + h]
        soft = low.astype(f32)
        dp = mm_nt(em, values)
        center = jnp.sum(soft * dp, axis=-1, keepdims=True)
        raw = (soft * (dp - center) * HEAD_DIM ** (-0.5)).astype(bf16)
        dv = dv + mm_tn(em, low)
        dk = dk + mm_tn(qm, raw)
        dq = dq + mm(raw, km)
    eq_ref[:, span] = dq.astype(bf16)
    dkv_ref[i, :, :LANES] = dk.T.astype(bf16)
    dkv_ref[i, :, LANES:] = dv.T.astype(bf16)


def feed_forward(b_low, gu_ref, down_ref, both_ref, units_ref):
    for t in range(TILES):
        both = mm(b_low, gu_ref[:, 256 * t : 256 * t + 256])
        both_ref[:, 256 * t : 256 * t + 256] = both
        gate, up = both[:, :128], both[:, 128:]
        units_ref[:, 128 * t : 128 * t + 128] = (gate / (1.0 + jnp.exp(-gate)) * up).astype(bf16)
    return mm(units_ref[...], down_ref[...])


def feed_back(e_low, gu_ref, down_ref, both_ref, eboth_ref, pump=None):
    for t in range(TILES):
        if pump is not None and t % 4 == 3:
            pump()
        eu = mm_nt(e_low, down_ref[128 * t : 128 * t + 128, :])
        gate = both_ref[:, 256 * t : 256 * t + 128]
        up = both_ref[:, 256 * t + 128 : 256 * t + 256]
        sig = 1.0 / (1.0 + jnp.exp(-gate))
        eboth_ref[:, 256 * t : 256 * t + 128] = (eu * up * sig * (1.0 + gate * (1.0 - sig))).astype(bf16)
        eboth_ref[:, 256 * t + 128 : 256 * t + 256] = (eu * gate * sig).astype(bf16)
    return mm_nt(eboth_ref[...], gu_ref[...])


def stage_head(length, master_pad, hidden, cos, sin, zn, rows_slot, share):
    rows = hidden.shape[0]
    cols = 4 * rows
    step = chunk_rows(rows_slot)
    half_zn = zn // 2
    first_zp = -(-BASE_OUT * LANES // (8 * share))
    parts = 4
    gather_steps = zn * (2 if rows_slot > 1000 else 1)
    top = rows_slot

    def body(
        l_ref, x_ref, h_ref, c_ref, s_ref,
        g0, g1, q0, ctx_ref, r1_ref, b_ref, units_ref, r2_ref, sec_ref, a1_ref, q1,
        wq0_any, wo0_any, wg0_any, wd0_any, wq1_any, wo1_any, wg1_any, wd1_any,
        kv0_any, kv1_any, p_any, both_any,
        wq0, wo0, wg0, wd0, wq1, wo1, wg1, wd1, all0, all1, p_ref, both_ref,
        slots, flat, gate_up, kv0, kv1, bias, send, recv,
        ksend0, krecv0, ksend1, krecv1, lsem, osem,
    ):
        z, x, y, c = coords()
        bar = pltpu.get_barrier_semaphore()

        def hello(device):
            pl.semaphore_signal(bar, inc=1, device_id=device, device_id_type=MESH)

        hello(place(z, 1 - x, y, c))
        hello(place(z, x, 1 - y, c))
        hello(place(z, x, y, 1 - c))
        pl.when(z > 0)(lambda: hello(place(z - 1, x, y, c)))
        pl.when(z < zn - 1)(lambda: hello(place(z + 1, x, y, c)))

        shift = lax.rem(share * (((z * 2 + x) * 2 + y) * 2 + c), LANES)
        lane = lax.broadcasted_iota(jnp.int32, (step, LANES), 1)

        def align(i, carry):
            now = pltpu.roll(x_ref[pl.ds(8 + i * step, step), :], shift, 1)
            before = pltpu.roll(x_ref[pl.ds(7 + i * step, step), :], shift, 1)
            slots[z, c, x * 2 + y, pl.ds(i * step, step), :] = jnp.where(
                lane >= shift, now, before
            ).astype(bf16)
            return carry

        lax.fori_loop(0, rows_slot // step, align, 0)
        pl.semaphore_wait(
            bar, 3 + (z > 0).astype(jnp.int32) + (z < zn - 1).astype(jnp.int32)
        )
        gather = Gather(slots, send, recv, zn, rows_slot)
        done = [0]

        def pump(until):
            gather.pump(done[0], until)
            done[0] = max(done[0], until)

        def between(low, high, k, n):
            pump(low + (high - low) * k // n)

        saves = [
            pltpu.make_async_copy(src, dst, osem.at[i])
            for i, (src, dst) in enumerate(
                [
                    (wq0, wq0_any), (wo0, wo0_any), (wg0, wg0_any), (wd0, wd0_any),
                    (wq1, wq1_any), (wo1, wo1_any), (wg1, wg1_any), (wd1, wd1_any),
                    (all0, kv0_any), (all1, kv1_any), (p_ref, p_any), (both_ref, both_any),
                ]
            )
        ]

        def fill(layer, name):
            fill_flat(slots, flat, layer, name, rows_slot, share)

        gather.begin()
        make_bias(bias, l_ref[0])
        pump(gather.until(first_zp))
        gather.arrived(0, first_zp)
        fill(0, "qkv")
        take_qkv(flat, top, wq0)
        exchange0 = KeyExchange(kv0, all0, ksend0, krecv0, lsem.at[0], parts)
        project_heads(h_ref[...], wq0, c_ref, s_ref, q0, kv0, range(2, 6))
        exchange0.start()
        saves[0].start()
        low, high = gather.until(first_zp), gather.until(half_zn)
        between(low, high, 1, 2)
        project_heads(h_ref[...], wq0, c_ref, s_ref, q0, kv0, range(2))
        exchange0.forward()
        pump(high)
        exchange0.finish()
        saves[8].start()
        low, high = high, gather.until(half_zn + first_zp)
        for i in range(HEADS // 2):
            attend(i, q0, all0, bias, p_ref, ctx_ref)
            if i == 1:
                between(low, high, 1, 2)
        saves[10].start()
        gather.arrived(first_zp, half_zn)
        fill(0, "out")
        take_out(flat, top, wo0)
        saves[1].start()
        fill(0, "down")
        take_down(flat, top, wd0, g0)
        saves[3].start()
        pump(high)
        fill(0, "gu")
        for group in GROUPS:
            take_gate_up(flat, top, gate_up, wg0, group)
        saves[2].start()
        low, high = high, gather.until(zn)
        between(low, high, 1, 3)
        r1 = h_ref[...].astype(f32) + mm(ctx_ref[...], wo0[...])
        r1_ref[...] = r1
        first = r1 * norm_factor(r1) * g0[0:1, :]
        b_ref[...] = first.astype(bf16)
        r2 = first + feed_forward(b_ref[...], wg0, wd0, both_ref, units_ref)
        saves[11].start()
        r2_ref[...] = r2
        second = r2 * norm_factor(r2) * g0[1:2, :]
        sec_ref[...] = second
        between(low, high, 2, 3)
        gather.arrived(half_zn, half_zn + first_zp)
        fill(1, "qkv")
        take_qkv(flat, top, wq1)
        saves[4].start()
        pump(high)
        gather.arrived(half_zn + first_zp, zn)
        fill(1, "down")
        take_down(flat, top, wd1, g1)
        saves[7].start()
        a1_ref[...] = (second * norm_factor(second) * g1[0:1, :]).astype(bf16)
        exchange1 = KeyExchange(kv1, all1, ksend1, krecv1, lsem.at[1], parts)
        project_heads(a1_ref[...], wq1, c_ref, s_ref, q1, kv1, range(2, 6))
        exchange1.start()
        project_heads(a1_ref[...], wq1, c_ref, s_ref, q1, kv1, range(2))
        fill(1, "out")
        take_out(flat, top, wo1)
        saves[5].start()
        fill(1, "gu")
        take_gate_up(flat, top, gate_up, wg1, GROUPS[0])
        exchange1.forward()
        take_gate_up(flat, top, gate_up, wg1, GROUPS[1])
        saves[6].start()
        exchange1.finish()
        saves[9].start()
        gather.sent()
        for item in saves:
            item.wait()

    layer = [((D, 3 * D), bf16), ((D, D), bf16), ((D, 2 * FFP), bf16), ((FFP, D), bf16)]
    kept = layer + layer + [
        ((cols, 2 * D), bf16),
        ((cols, 2 * D), bf16),
        ((HEADS, rows, cols), bf16),
        ((rows, 2 * FFP), f32),
    ]
    low_rows, full_rows = ((rows, D), bf16), ((rows, D), f32)
    outs = [
        ((2, D), f32),
        ((2, D), f32),
        low_rows,
        low_rows,
        full_rows,
        low_rows,
        ((rows, FFP), bf16),
        full_rows,
        full_rows,
        low_rows,
        low_rows,
    ]
    ins = [length, master_pad, hidden, cos, sin]
    longest = max(high - low for low, high in REGIONS.values())
    kv_scratch = pltpu.VMEM((rows, 2 * D), bf16)
    return pl.pallas_call(
        body,
        out_shape=[jax.ShapeDtypeStruct(s, d) for s, d in outs + kept],
        in_specs=[pl.BlockSpec(memory_space=pltpu.SMEM)] + [vmem_spec()] * (len(ins) - 1),
        out_specs=[vmem_spec()] * len(outs) + [any_spec()] * len(kept),
        scratch_shapes=[pltpu.VMEM(s, d) for s, d in kept]
        + [
            pltpu.VMEM((zn, 2, 4, rows_slot, LANES), bf16),
            pltpu.VMEM((longest + 2 * rows_slot, LANES), f32),
            pltpu.VMEM((12, D, LANES), f32),
            kv_scratch,
            kv_scratch,
            pltpu.VMEM((rows, cols), f32),
            pltpu.SemaphoreType.DMA((gather_steps, 7)),
            pltpu.SemaphoreType.DMA((gather_steps, 6)),
            pltpu.SemaphoreType.DMA((3, parts)),
            pltpu.SemaphoreType.DMA((3, parts)),
            pltpu.SemaphoreType.DMA((3, parts)),
            pltpu.SemaphoreType.DMA((3, parts)),
            pltpu.SemaphoreType.DMA((2,)),
            pltpu.SemaphoreType.DMA((12,)),
        ],
        compiler_params=pltpu.CompilerParams(
            collective_id=1, has_side_effects=True, vmem_limit_bytes=62 * MIB
        ),
    )(*ins)


class Loads:
    def __init__(self, pairs, sem):
        self.items = [pltpu.make_async_copy(src, dst, sem.at[i]) for i, (src, dst) in enumerate(pairs)]
        for item in self.items:
            item.start()

    def wait(self, *which):
        for i in which:
            self.items[i].wait()


def meet(devices):
    bar = pltpu.get_barrier_semaphore()
    for device in devices:
        pl.semaphore_signal(bar, inc=1, device_id=device, device_id_type=MESH)
    pl.semaphore_wait(bar, len(devices))


def stage_second(
    length, cotangent, second, q, kv, w_out, w_gu, w_down, w_qkv, gains, a1, cos, sin, share, rows_slot
):
    rows = q.shape[0]
    cols = kv.shape[0]
    per_layer = LAYER_ROWS * LANES // share
    middle = split_slot(share)

    def body(
        l_ref, cot_ref, sec_ref, q_ref, g_ref, a_ref, c_ref, s_ref, kv_any, wo_any, gu_any, dn_any, wq_any,
        o_ref, e2_ref, gg_ref, slots_ref,
        kv_ref, wo_ref, gu_ref, dn_ref, wq_ref, lsem, eq_ref, lin_ref,
        bias, p_ref, ctx_ref, b_ref, both_ref, units_ref, eboth_ref, ef_ref, ea_ref, ectx_ref,
        ekv_ref, flat, ring, stage, esem,
        dkv_ref, from_c, pair, from_y, send, recv,
    ):
        loads = Loads(
            [
                (kv_any, kv_ref), (wo_any, wo_ref), (gu_any, gu_ref), (dn_any, dn_ref), (wq_any, wq_ref)
            ],
            lsem,
        )
        z, x, y, c = coords()
        meet([place(z, x, 1 - y, c), place(z, x, y, 1 - c)])
        total = KeySum(dkv_ref, ekv_ref, from_c, pair, from_y, send, recv)
        length_now = l_ref[0]
        make_bias(bias, length_now)
        loads.wait(0)
        for i in range(HEADS // 2):
            attend(i, q_ref, kv_ref, bias, p_ref, ctx_ref)
        loads.wait(1, 2, 3)
        third = sec_ref[...] + mm(ctx_ref[...], wo_ref[...])
        f4 = norm_factor(third)
        b_ref[...] = (third * f4 * g_ref[1:2, :]).astype(bf16)
        o_ref[...] = third + feed_forward(b_ref[...], gu_ref, dn_ref, both_ref, units_ref)
        place_now = lax.broadcasted_iota(jnp.int32, (rows, D), 0) + lax.axis_index("sp") * rows
        e_out = jnp.where(place_now < length_now, cot_ref[...], 0.0)
        ef_ref[...] = e_out.astype(bf16)
        e_b = feed_back(ef_ref[...], gu_ref, dn_ref, both_ref, eboth_ref)
        grad, gain = norm_back(e_b, third, f4, g_ref[1:2, :])
        gg_ref[1:2, :] = gain
        e3 = e_out + grad
        e2_ref[...] = e3
        ea_ref[...] = e3.astype(bf16)
        ectx_ref[...] = mm_nt(ea_ref[...], wo_ref[...]).astype(bf16)
        for i in range(HEADS // 2):
            attend_back(i, q_ref, kv_ref, p_ref, ectx_ref, eq_ref, dkv_ref)
            total.start(i)
            if i >= 1:
                total.middle(i - 1)
        for t in range(TILES):
            grad_gate_up(flat, ring, t, b_ref[...], eboth_ref)
            if t == 0:
                total.middle(3)
            if t in (1, 4, 7, 10):
                total.end((t - 1) // 3)
        lin_grads(eq_ref, ekv_ref, c_ref, s_ref, lin_ref)
        grad_down(flat, units_ref[...], ef_ref[...])
        loads.wait(4)
        second = sec_ref[...]
        grad, gain = norm_back(
            mm_nt(lin_ref[...], wq_ref[...]), second, norm_factor(second), g_ref[0:1, :]
        )
        gg_ref[0:1, :] = gain
        e2_ref[...] = e2_ref[...] + grad
        grad_gains(flat, gg_ref[0:1, :], gg_ref[1:2, :])
        emit_slots(flat, BASE_GU, stage, slots_ref, esem, rows_slot, share, middle, per_layer)
        carry_edge(flat, rows_slot)
        grad_out(flat, ctx_ref[...], ea_ref[...])
        grad_qkv(flat, a_ref[...], lin_ref)
        emit_slots(flat, 0, stage, slots_ref, esem, rows_slot, share, 0, middle)
        total.sent()

    outs = [
        ((rows, D), f32),
        ((rows, D), f32),
        ((2, D), f32),
        ((per_layer, rows_slot, LANES), bf16),
    ]
    ins = [length, cotangent, second, q, gains, a1, cos, sin, kv, w_out, w_gu, w_down, w_qkv]
    return pl.pallas_call(
        body,
        out_shape=[jax.ShapeDtypeStruct(s, d) for s, d in outs],
        in_specs=[pl.BlockSpec(memory_space=pltpu.SMEM)] + [vmem_spec()] * 7 + [any_spec()] * 5,
        out_specs=[vmem_spec()] * 3 + [any_spec()],
        scratch_shapes=[
            pltpu.VMEM((cols, 2 * D), bf16),
            pltpu.VMEM((D, D), bf16),
            pltpu.VMEM((D, 2 * FFP), bf16),
            pltpu.VMEM((FFP, D), bf16),
            pltpu.VMEM((D, 3 * D), bf16),
            pltpu.SemaphoreType.DMA((5,)),
            pltpu.VMEM((rows, D), bf16),
            pltpu.VMEM((rows, 3 * D), bf16),
            pltpu.VMEM((rows, cols), f32),
            pltpu.VMEM((HEADS, rows, cols), bf16),
            pltpu.VMEM((rows, D), bf16),
            pltpu.VMEM((rows, D), bf16),
            pltpu.VMEM((rows, 2 * FFP), f32),
            pltpu.VMEM((rows, FFP), bf16),
            pltpu.VMEM((rows, 2 * FFP), bf16),
            pltpu.VMEM((rows, D), bf16),
            pltpu.VMEM((rows, D), bf16),
            pltpu.VMEM((rows, D), bf16),
            pltpu.VMEM((rows, 2 * D), bf16),
            pltpu.VMEM((flat_rows(rows_slot), LANES), f32),
            pltpu.VMEM((6, D, LANES), f32),
            pltpu.VMEM((2, rows_slot, LANES), bf16),
            pltpu.SemaphoreType.DMA((2,)),
        ]
        + key_sum_scratch(rows),
        compiler_params=pltpu.CompilerParams(
            collective_id=3, has_side_effects=True, vmem_limit_bytes=60 * MIB
        ),
    )(*ins)


def lin_grads(eq_ref, ekv_ref, cos_ref, sin_ref, lin_ref):
    for t in range(12):
        col = 128 * t
        src = eq_ref[:, col : col + 128] if t < 4 else ekv_ref[:, col - D : col - D + 128]
        if t < 8:
            w = src.astype(f32)
            src = (w * cos_ref[...] - half_swap(w) * sin_ref[...]).astype(bf16)
        lin_ref[:, col : col + 128] = src


def pieces_of(rows):
    return 7 if rows % 224 == 0 and rows > 1000 else 1


class Reduce:
    def __init__(self, src, bufs, fin, send, recv, lsem, zn, rows, zlo, zhi, lag=2, ahead=4):
        self.src, self.fin = src, fin
        self.acc, self.rc, self.rd, self.rx, self.ry, self.rz = bufs
        self.send, self.recv, self.lsem = send, recv, lsem
        self.zn, self.zlo, self.zhi = zn, zlo, zhi
        self.parts = pieces_of(rows)
        self.size = rows // self.parts
        self.half = self.size // 32 * 16
        self.steps = (zhi - zlo) * self.parts
        self.lag, self.ahead = lag, ahead
        self.turns = self.steps + 3 * lag
        self.z, self.x, self.y, self.c = coords()
        z, x, y, c = self.z, self.x, self.y, self.c
        self.to_x = place(z, 1 - x, y, c)
        self.to_y = place(z, x, 1 - y, c)
        self.to_c = place(z, x, y, 1 - c)
        self.spots = [(x, y), (1 - x, y), (x, 1 - y), (1 - x, 1 - y)]

    def at(self, k):
        zp = self.zhi - 1 - lax.div(k, self.parts)
        base = pl.multiple_of(lax.rem(k, self.parts) * self.size, 16)
        return zp, zp - self.zlo, base

    def cp(self, src, dst, k, s, r, device):
        return remote(src, dst, self.send.at[k, s], self.recv.at[k, r], device)

    def source(self, k, rel, cp):
        zp, loc, base = self.at(k)
        xp, yp = self.spots[rel]
        return self.src.at[((loc * 2 + xp) * 2 + yp) * 2 + cp, pl.ds(base, self.size)]

    def span(self, k, low=0, size=None):
        zp, loc, base = self.at(k)
        return loc, pl.ds(pl.multiple_of(base + low, 16), self.size if size is None else size)

    def core(self, k, rel):
        loc, span = self.span(k)
        return self.cp(
            self.source(k, rel, 1 - self.c), self.rc.at[loc, rel, span], k, rel, rel, self.to_c
        )

    def load(self, k, rel):
        loc, span = self.span(k)
        return pltpu.make_async_copy(
            self.source(k, rel, self.c), self.acc.at[loc, rel, span], self.lsem.at[k, rel]
        )

    def diag_a(self, k):
        loc, span = self.span(k, 0, self.half)
        return self.cp(self.acc.at[loc, 3, span], self.rd.at[loc, span], k, 4, 4, self.to_y)

    def diag_b(self, k):
        loc, span = self.span(k, self.half, self.size - self.half)
        return self.cp(self.acc.at[loc, 3, span], self.rd.at[loc, span], k, 5, 5, self.to_x)

    def send_x(self, k):
        loc, span = self.span(k)
        return self.cp(self.acc.at[loc, 1, span], self.rx.at[loc, span], k, 6, 6, self.to_x)

    def send_y(self, k):
        loc, span = self.span(k)
        return self.cp(self.acc.at[loc, 2, span], self.ry.at[loc, span], k, 7, 7, self.to_y)

    def right(self, k):
        loc, span = self.span(k)
        return self.cp(
            self.acc.at[loc, 0, span], self.rz.at[loc, 0, span], k, 8, 8,
            place(self.z + 1, self.x, self.y, self.c),
        )

    def left(self, k):
        loc, span = self.span(k)
        return self.cp(
            self.acc.at[loc, 0, span], self.rz.at[loc, 1, span], k, 8, 9,
            place(self.z - 1, self.x, self.y, self.c),
        )

    def add(self, loc, rel, span, *srcs):
        value = self.acc[loc, rel, span, :].astype(f32)
        for src in srcs:
            value = value + src.astype(f32)
        self.acc[loc, rel, span, :] = value.astype(bf16)

    def ok(self, k):
        return (k >= 0) & (k < self.steps)

    def stage_core(self, k):
        @pl.when(self.ok(k))
        def _():
            for rel in (3, 1, 2, 0):
                self.core(k, rel).start()
                self.load(k, rel).start()

    def stage_one(self, k):
        @pl.when(self.ok(k))
        def _():
            loc, span = self.span(k)
            for rel in (3, 1, 2, 0):
                self.core(k, rel).wait_recv()
                self.load(k, rel).wait()
                self.add(loc, rel, span, self.rc[loc, rel, span, :])
                if rel == 3:
                    self.diag_a(k).start()
                    self.diag_b(k).start()

    def stage_two(self, k):
        @pl.when(self.ok(k))
        def _():
            self.diag_a(k).wait_recv()
            loc, span = self.span(k, 0, self.half)
            self.add(loc, 1, span, self.rd[loc, span, :])
            self.send_x(k).start()
            self.diag_b(k).wait_recv()
            loc, span = self.span(k, self.half, self.size - self.half)
            self.add(loc, 2, span, self.rd[loc, span, :])
            self.send_y(k).start()

    def stage_three(self, k):
        zp, loc, base = self.at(k)
        z = self.z

        @pl.when(self.ok(k))
        def _():
            loc, span = self.span(k)
            self.send_x(k).wait_recv()
            self.send_y(k).wait_recv()

            @pl.when(zp == z)
            def _():
                self.fin[pl.ds(base, self.size), :] = (
                    self.acc[loc, 0, span, :].astype(f32)
                    + self.rx[loc, span, :].astype(f32)
                    + self.ry[loc, span, :].astype(f32)
                )

            @pl.when(zp != z)
            def _():
                self.add(loc, 0, span, self.rx[loc, span, :], self.ry[loc, span, :])

            pl.when((zp > z) & (z == 0))(lambda: self.right(k).start())
            pl.when((zp < z) & (z == self.zn - 1))(lambda: self.left(k).start())

    def stage_four(self, k):
        zp, loc, base = self.at(k)
        z = self.z

        @pl.when(self.ok(k))
        def _():
            loc, span = self.span(k)

            @pl.when((zp > z) & (z > 0))
            def _():
                self.right(k).wait_recv()
                self.add(loc, 0, span, self.rz[loc, 0, span, :])
                self.right(k).start()

            @pl.when((zp < z) & (z < self.zn - 1))
            def _():
                self.left(k).wait_recv()
                self.add(loc, 0, span, self.rz[loc, 1, span, :])
                self.left(k).start()

            whole = pl.ds(base, self.size)

            @pl.when((zp == z) & (z > 0))
            def _():
                self.right(k).wait_recv()
                self.fin[whole, :] = self.fin[whole, :] + self.rz[loc, 0, span, :].astype(f32)

            @pl.when((zp == z) & (z < self.zn - 1))
            def _():
                self.left(k).wait_recv()
                self.fin[whole, :] = self.fin[whole, :] + self.rz[loc, 1, span, :].astype(f32)

    def begin(self):
        for k in range(min(self.ahead, self.steps)):
            self.stage_core(k)

    def pump(self, low, high):
        def one(k, carry):
            self.stage_one(k)
            self.stage_core(k + self.ahead)
            self.stage_two(k - self.lag)
            self.stage_three(k - 2 * self.lag)
            self.stage_four(k - 3 * self.lag)
            return carry

        lax.fori_loop(low, high, one, 0)

    def sent(self):
        def one(k, carry):
            zp, loc, base = self.at(k)
            for rel in range(4):
                self.core(k, rel).wait_send()
            for item in (self.diag_a(k), self.diag_b(k), self.send_x(k), self.send_y(k)):
                item.wait_send()
            pl.when(zp > self.z)(lambda: self.right(k).wait_send())
            pl.when(zp < self.z)(lambda: self.left(k).wait_send())
            return carry

        lax.fori_loop(0, self.steps, one, 0)


class Pumps:
    def __init__(self, stream, first, sites):
        self.stream, self.first, self.sites, self.done = stream, first, sites, 0

    def __call__(self):
        self.to(self.done + 1)

    def to(self, site):
        total = self.stream.turns - self.first
        low = self.first + total * self.done // self.sites
        high = self.first + total * site // self.sites
        self.done = site
        if high > low:
            self.stream.pump(low, high)

    def rest(self):
        self.to(self.sites)


def stage_last(
    e2, r1, r2, gains, hidden, q, ctx, b_low, units, cos, sin, gains_one, master, one, two,
    slots_one, p, both, kv, w_gu, w_down, w_out, w_qkv, zn, rows_slot, share,
):
    rows = e2.shape[0]
    cols = kv.shape[0]
    ndev = zn * 8
    per_layer = ndev // 2
    half_zn = zn // 2
    step = chunk_rows(rows_slot)
    turns = rows_slot // step
    middle = split_slot(share)
    steps = half_zn * pieces_of(rows_slot)

    def body(
        e2_ref, r1_ref, r2_ref, g_ref, h_ref, q_ref, ctx_ref, b_ref, units_ref, c_ref, s_ref, g1_ref,
        m_ref, one_ref, two_ref,
        s1_any, p_any, both_any, kv_any, gu_any, dn_any, wo_any, wq_any,
        ig_ref, nm_ref, n1_ref, n2_ref, gn_ref, gg_ref, s0_any,
        p_ref, both_ref, kv_ref, gu_ref, dn_ref, wo_ref, wq_ref, load_sem,
        eboth_ref, ef_ref, ea_ref, ectx_ref, eq_ref, ekv_ref, lin_ref,
        flat, ring, stage, esem,
        acc, rc, rd, rx, ry, rz, fin, gp_ref, sq, sqs, gps,
        send1, recv1, lsem1, send0, recv0, lsem0, ssem, rsem, free,
        dkv_ref, from_c, pair, from_y, ksend, krecv,
    ):
        z, x, y, c = coords()
        me = ((z * 2 + x) * 2 + y) * 2 + c
        bar = pltpu.get_barrier_semaphore()

        def peer(d):
            tgt = lax.rem(me + d, ndev)
            return {"dp": lax.div(tgt, 4), "sp": lax.rem(tgt, 4)}

        def hello(d, carry):
            pl.semaphore_signal(bar, inc=1, device_id=peer(d), device_id_type=MESH)
            return carry

        lax.fori_loop(1, ndev, hello, 0)
        loads = Loads(
            [
                (gu_any, gu_ref), (dn_any, dn_ref), (both_any, both_ref), (wo_any, wo_ref),
                (kv_any, kv_ref), (p_any, p_ref), (wq_any, wq_ref),
            ],
            load_sem,
        )
        bufs = (acc, rc, rd, rx, ry, rz)
        late = Reduce(s1_any, bufs, fin, send1, recv1, lsem1, zn, rows_slot, half_zn, zn)
        early = Reduce(s0_any, bufs, fin, send0, recv0, lsem0, zn, rows_slot, 0, half_zn)
        total = KeySum(dkv_ref, ekv_ref, from_c, pair, from_y, ksend, krecv)
        pl.semaphore_wait(bar, ndev - 1)
        late.begin()
        pump = Pumps(late, 0, 16)

        r2 = r2_ref[...]
        er2, gain = norm_back(e2_ref[...], r2, norm_factor(r2), g_ref[1:2, :])
        gp_ref[4:8, :] = gain.reshape(4, LANES)
        gp_ref[8:16, :] = g1_ref[...].reshape(8, LANES)
        gg_rows = [None, gain]
        ef_ref[...] = er2.astype(bf16)
        loads.wait(0, 1, 2)
        pump()
        e_first = er2 + feed_back(ef_ref[...], gu_ref, dn_ref, both_ref, eboth_ref, pump)
        r1 = r1_ref[...]
        er1, gain = norm_back(e_first, r1, norm_factor(r1), g_ref[0:1, :])
        gp_ref[0:4, :] = gain.reshape(4, LANES)
        gg_rows[0] = gain
        ig_ref[...] = er1
        ea_ref[...] = er1.astype(bf16)

        def tell(src, dst, s):
            def go(d, carry):
                remote(src, dst.at[me], ssem.at[s], rsem.at[s], peer(d)).start()
                return carry

            lax.fori_loop(1, ndev, go, 0)

        def hear(dst, s):
            part = dst.at[pl.ds(0, ndev - 1)]
            both = remote(part, part, ssem.at[s], rsem.at[s], total.to_c)
            both.wait_send()
            both.wait_recv()

        tell(gp_ref, gps, 0)
        gps[me] = gp_ref[...]
        loads.wait(3, 4, 5)
        pump()
        ectx_ref[...] = mm_nt(ea_ref[...], wo_ref[...]).astype(bf16)
        for i in range(HEADS // 2):
            attend_back(i, q_ref, kv_ref, p_ref, ectx_ref, eq_ref, dkv_ref)
            total.start(i)
            if i >= 1:
                total.middle(i - 1)
            pump()
        for t in range(TILES):
            grad_gate_up(flat, ring, t, b_ref[...], eboth_ref)
            if t == 0:
                total.middle(3)
            if t in (1, 4, 7, 10):
                total.end((t - 1) // 3)
                pump()
        grad_down(flat, units_ref[...], ef_ref[...])
        pump()
        grad_gains(flat, gg_rows[0], gg_rows[1])
        emit_slots(flat, BASE_GU, stage, s0_any, esem, rows_slot, share, middle, per_layer)
        pump()
        lin_grads(eq_ref, ekv_ref, c_ref, s_ref, lin_ref)
        loads.wait(6)
        ig_ref[...] = ig_ref[...] + mm_nt(lin_ref[...], wq_ref[...])
        pump()
        carry_edge(flat, rows_slot)
        grad_out(flat, ctx_ref[...], ea_ref[...])
        grad_qkv(flat, h_ref[...], lin_ref)
        emit_slots(flat, 0, stage, s0_any, esem, rows_slot, share, 0, middle)
        pump.rest()
        late.sent()

        def near(act):
            for device in (late.to_x, late.to_y, late.to_c):
                act(device)
            pl.when(z > 0)(lambda: act(place(z - 1, x, y, c)))
            pl.when(z < zn - 1)(lambda: act(place(z + 1, x, y, c)))

        near(lambda d: pl.semaphore_signal(free, inc=1, device_id=d, device_id_type=MESH))
        pl.semaphore_wait(free, 3 + (z > 0).astype(jnp.int32) + (z < zn - 1).astype(jnp.int32))
        early.begin()
        early.pump(0, early.turns)

        fin[pl.ds(rows_slot, 8), :] = jnp.zeros((8, LANES), f32)
        shift = lax.rem(share * me, LANES)
        back = lax.rem(LANES - shift, LANES)
        lane = lax.broadcasted_iota(jnp.int32, (step, LANES), 1)
        row = lax.broadcasted_iota(jnp.int32, (step, LANES), 0)

        def realign(i, carry):
            now = pltpu.roll(fin[pl.ds(i * step, step), :], back, 1)
            after = pltpu.roll(fin[pl.ds(i * step + 1, step), :], back, 1)
            value = jnp.where(lane < LANES - shift, now, after)
            value = jnp.where((row + i * step) * LANES + lane < share, value, 0.0)
            n1_ref[pl.ds(i * step, step), :] = value
            square = value * value
            return carry + jnp.sum(square.reshape(step // 8, 8, LANES), axis=0)

        sq[...] = lax.fori_loop(0, turns, realign, jnp.zeros((8, LANES), f32))
        tell(sq, sqs, 1)
        sqs[me] = sq[...]
        early.sent()
        total.sent()
        hear(gps, 0)
        gg_ref[...] = lax.fori_loop(1, ndev, lambda i, s: s + gps[i], gps[0])
        hear(sqs, 1)
        squares = lax.fori_loop(1, ndev, lambda i, s: s + sqs[i], sqs[0])
        norm = jnp.sqrt(jnp.sum(squares, keepdims=True))
        gn_ref[...] = jnp.broadcast_to(norm, (8, LANES))
        scale = jnp.minimum(1.0, 1.0 / norm)
        correction = 1.0 - 0.5**STEP

        def update(i, carry):
            span = pl.ds(pl.multiple_of(i * step, 16), step)
            clipped = n1_ref[span, :] * scale
            new_one = 0.5 * one_ref[span, :] + 0.5 * clipped
            new_two = 0.5 * two_ref[span, :] + 0.5 * clipped * clipped
            n1_ref[span, :] = new_one
            n2_ref[span, :] = new_two
            nm_ref[span, :] = m_ref[pl.ds(8 + i * step, step), :] * (
                1.0 - LEARN_RATE * DECAY_RATE
            ) - LEARN_RATE * (new_one / correction) / (jnp.sqrt(new_two / correction) + ADAM_EPS)
            return carry

        lax.fori_loop(0, turns, update, 0)

    slot_flat = ((rows_slot, LANES), f32)
    outs = [
        ((rows, D), f32),
        slot_flat,
        slot_flat,
        slot_flat,
        ((8, LANES), f32),
        ((16, LANES), f32),
        ((per_layer, rows_slot, LANES), bf16),
    ]
    small = [e2, r1, r2, gains, hidden, q, ctx, b_low, units, cos, sin, gains_one, master, one, two]
    large = [slots_one, p, both, kv, w_gu, w_down, w_out, w_qkv]
    act = pltpu.VMEM((rows, D), bf16)
    return pl.pallas_call(
        body,
        out_shape=[jax.ShapeDtypeStruct(s, d) for s, d in outs],
        in_specs=[vmem_spec()] * len(small) + [any_spec()] * len(large),
        out_specs=[vmem_spec()] * 6 + [any_spec()],
        scratch_shapes=[
            pltpu.VMEM(p.shape, bf16),
            pltpu.VMEM(both.shape, f32),
            pltpu.VMEM(kv.shape, bf16),
            pltpu.VMEM(w_gu.shape, bf16),
            pltpu.VMEM(w_down.shape, bf16),
            pltpu.VMEM(w_out.shape, bf16),
            pltpu.VMEM(w_qkv.shape, bf16),
            pltpu.SemaphoreType.DMA((7,)),
            pltpu.VMEM((rows, 2 * FFP), bf16),
            act,
            act,
            act,
            act,
            pltpu.VMEM((rows, 2 * D), bf16),
            pltpu.VMEM((rows, 3 * D), bf16),
            pltpu.VMEM((flat_rows(rows_slot), LANES), f32),
            pltpu.VMEM((6, D, LANES), f32),
            pltpu.VMEM((2, rows_slot, LANES), bf16),
            pltpu.SemaphoreType.DMA((2,)),
            pltpu.VMEM((half_zn, 4, rows_slot, LANES), bf16),
            pltpu.VMEM((half_zn, 4, rows_slot, LANES), bf16),
            pltpu.VMEM((half_zn, rows_slot, LANES), bf16),
            pltpu.VMEM((half_zn, rows_slot, LANES), bf16),
            pltpu.VMEM((half_zn, rows_slot, LANES), bf16),
            pltpu.VMEM((half_zn, 2, rows_slot, LANES), bf16),
            pltpu.VMEM((rows_slot + 8, LANES), f32),
            pltpu.VMEM((16, LANES), f32),
            pltpu.VMEM((8, LANES), f32),
            pltpu.VMEM((ndev, 8, LANES), f32),
            pltpu.VMEM((ndev, 16, LANES), f32),
            pltpu.SemaphoreType.DMA((steps, 9)),
            pltpu.SemaphoreType.DMA((steps, 10)),
            pltpu.SemaphoreType.DMA((steps, 4)),
            pltpu.SemaphoreType.DMA((steps, 9)),
            pltpu.SemaphoreType.DMA((steps, 10)),
            pltpu.SemaphoreType.DMA((steps, 4)),
            pltpu.SemaphoreType.DMA((2,)),
            pltpu.SemaphoreType.DMA((2,)),
            pltpu.SemaphoreType.REGULAR,
        ]
        + key_sum_scratch(rows),
        compiler_params=pltpu.CompilerParams(
            collective_id=4, has_side_effects=True, vmem_limit_bytes=62 * MIB
        ),
    )(*small, *large)


def rope_rows(rows):
    frequency = jnp.exp(
        -jnp.log(10000.0) * jnp.arange(HEAD_DIM // 2).astype(f32) * 2.0 / HEAD_DIM
    )
    positions = lax.axis_index("sp") * rows + jnp.arange(rows)
    angles = positions.astype(f32)[:, None] * frequency[None, :]
    cos = jnp.cos(angles)
    sin = jnp.sin(angles)
    return (
        jnp.concatenate([cos] * 4, axis=1),
        jnp.concatenate([-sin, sin, -sin, sin], axis=1),
    )


def step_shard(dp_size, sp_size, hidden_in, cotangent, lengths, master, moment_one, moment_two):
    share = master.shape[0]
    zn = dp_size // 2
    per_layer = dp_size * sp_size // 2
    rows = -(-(-(-share // LANES) + 1) // 32) * 32
    seqs, tokens, width = hidden_in.shape

    def pad(flat, lead):
        return jnp.pad(flat, (lead * LANES, rows * LANES - share)).reshape(rows + lead, LANES)

    master_pad = pad(master, 8)
    cos, sin = rope_rows(tokens)
    hidden = hidden_in.reshape(tokens, width)

    (
        g0, g1, q0, ctx0, r1, b0, units0, r2, second, a1, q1,
        wq0, wo0, wg0, wd0, wq1, wo1, wg1, wd1, kv0, kv1, p0, both0,
    ) = stage_head(lengths, master_pad, hidden, cos, sin, zn, rows, share)
    output, e2, gains_one, slots_one = stage_second(
        lengths, cotangent.reshape(tokens, width), second, q1, kv1, wo1, wg1, wd1, wq1, g1, a1,
        cos, sin, share, rows,
    )
    input_grad, new_master, new_one, new_two, norm, gains, _ = stage_last(
        e2, r1, r2, g0, hidden, q0, ctx0, b0, units0, cos, sin, gains_one,
        master_pad, pad(moment_one, 0), pad(moment_two, 0),
        slots_one, p0, both0, kv0, wg0, wd0, wo0, wq0, zn, rows, share,
    )

    def flat(value):
        return value.reshape(-1)[:share]

    new_master = flat(new_master)
    return (
        output.reshape(hidden_in.shape),
        input_grad.reshape(hidden_in.shape),
        new_master,
        flat(new_one),
        flat(new_two),
        new_master.astype(bf16),
        norm[0, 0],
        gains.reshape(2, 2, width),
    )


def solution(mesh):
    in_specs = (
        P("dp", "sp", None),
        P("dp", "sp", None),
        P("dp"),
        P(("dp", "sp")),
        P(("dp", "sp")),
        P(("dp", "sp")),
    )
    out_specs = (
        P("dp", "sp", None),
        P("dp", "sp", None),
        P(("dp", "sp")),
        P(("dp", "sp")),
        P(("dp", "sp")),
        P(("dp", "sp")),
        P(),
        P(),
    )
    body = functools.partial(step_shard, mesh.shape["dp"], mesh.shape["sp"])
    return jax.shard_map(body, mesh=mesh, in_specs=in_specs, out_specs=out_specs, check_vma=False)
```

```python
import functools

import jax
import jax.numpy as jnp
from jax import lax
from jax.experimental import pallas as pl
from jax.experimental.pallas import tpu as pltpu
from jax.sharding import PartitionSpec as P

D = 512
HEADS = 8
HEAD_DIM = 64
FF = 1368
FFP = 1408
TILES = 11
STEP = 5
NORM_EPS = 1e-06
ADAM_EPS = 1e-08
LEARN_RATE = 0.02
DECAY_RATE = 0.01
LANES = 128
LAYER_ROWS = 24616
BASE_OUT = 6144
BASE_GU = 8192
BASE_DOWN = 19136
BASE_GAINS = 24608
GU_ROW = 2 * FF
PERIOD = 171
MESH = pl.DeviceIdType.MESH
MIB = 1 << 20
f32 = jnp.float32
bf16 = jnp.bfloat16


def mm(a, b):
    return lax.dot_general(a, b, (((1,), (0,)), ((), ())), preferred_element_type=f32)


def mm_nt(a, b):
    return lax.dot_general(a, b, (((1,), (1,)), ((), ())), preferred_element_type=f32)


def mm_tn(a, b):
    return lax.dot_general(a, b, (((0,), (0,)), ((), ())), preferred_element_type=f32)


def chunk_rows(rows):
    tiles = rows // 16
    best = max(d for d in range(1, 17) if tiles % d == 0)
    return best * 16


def vmem_spec():
    return pl.BlockSpec(memory_space=pltpu.VMEM)


def any_spec():
    return pl.BlockSpec(memory_space=pl.ANY)


def local_call(body, outs, ins, scratch=(), limit=60, flops=0):
    return pl.pallas_call(
        body,
        out_shape=[jax.ShapeDtypeStruct(s, d) for s, d in outs],
        in_specs=[vmem_spec()] * len(ins),
        out_specs=[vmem_spec()] * len(outs),
        scratch_shapes=list(scratch),
        compiler_params=pltpu.CompilerParams(vmem_limit_bytes=limit * MIB),
    )(*ins)


def coords():
    dp = lax.axis_index("dp")
    sp = lax.axis_index("sp")
    return lax.div(dp, 2), lax.rem(dp, 2), lax.div(sp, 2), lax.rem(sp, 2)


def place(z, x, y, c):
    return {"dp": z * 2 + x, "sp": y * 2 + c}


def remote(src, dst, send_sem, recv_sem, device):
    return pltpu.make_async_remote_copy(
        src_ref=src,
        dst_ref=dst,
        send_sem=send_sem,
        recv_sem=recv_sem,
        device_id=device,
        device_id_type=MESH,
    )


def order_at(tau, z):
    step = lax.div(tau + 1, 2)
    return z + jnp.where(lax.rem(tau, 2) == 1, -step, step)


class Gather:
    lag = 1
    reach = 0
    count = 2
    cut = 0.5

    def __init__(self, slots, send, recv, zn, rows):
        self.slots, self.send, self.recv, self.zn = slots, send, recv, zn
        self.parts = self.pieces(rows)
        self.size = rows // self.parts
        self.half = max(1, round(self.size // 16 * self.cut)) * 16
        self.steps = zn * self.parts
        self.turns = self.steps + 2 * self.lag
        self.z, self.x, self.y, self.c = coords()
        z, x, y, c = self.z, self.x, self.y, self.c
        self.to_x = place(z, 1 - x, y, c)
        self.to_y = place(z, x, 1 - y, c)
        self.to_c = place(z, x, y, 1 - c)
        self.ahead = z >= zn // 2

    @classmethod
    def pieces(cls, rows):
        return cls.count if rows > 1000 else 1

    def until(self, zp):
        return zp * self.parts + 2 * self.lag if zp < self.zn else self.turns

    def at(self, k):
        return lax.div(k, self.parts), lax.rem(k, self.parts) * self.size

    def ref(self, k, xp, yp, low=0, size=None):
        zp, base = self.at(k)
        span = pl.ds(pl.multiple_of(base + low, 16), self.size if size is None else size)
        return self.slots.at[zp, self.c, xp * 2 + yp, span]

    def cp(self, ref, k, s, r, device):
        return remote(ref, ref, self.send.at[k, s], self.recv.at[k, r], device)

    def right(self, k):
        return self.cp(self.ref(k, self.x, self.y), k, 0, 0, place(self.z + 1, self.x, self.y, self.c))

    def left(self, k):
        return self.cp(self.ref(k, self.x, self.y), k, 1, 0, place(self.z - 1, self.x, self.y, self.c))

    def over_x(self, k):
        return self.cp(self.ref(k, self.x, self.y), k, 2, 1, self.to_x)

    def over_y(self, k):
        return self.cp(self.ref(k, self.x, self.y), k, 3, 2, self.to_y)

    def upper(self, k):
        return self.cp(self.ref(k, 1 - self.x, self.y, 0, self.half), k, 4, 3, self.to_y)

    def lower(self, k):
        ref = self.ref(k, self.x, 1 - self.y, self.half, self.size - self.half)
        return self.cp(ref, k, 5, 4, self.to_x)

    def over_c(self, k, c):
        zp, base = self.at(k)
        ref = self.slots.at[zp, c, :, pl.ds(pl.multiple_of(base, 16), self.size)]
        return self.cp(ref, k, 6, 5, self.to_c)

    def arrival(self, ref, k, r):
        self.cp(ref, k, 0, r, self.to_c).wait_recv()

    def along(self, k):
        zp, base = self.at(k)
        z = self.z

        @pl.when((k < self.steps) & ((zp != z) | (z < self.zn // 2)))
        def _():
            pl.when(zp != z)(lambda: self.arrival(self.ref(k, self.x, self.y), k, 0))
            self.onward(k)

    def onward(self, k):
        zp, base = self.at(k)
        z = self.z
        pl.when((zp <= z) & (z < self.zn - 1))(lambda: self.right(k).start())
        pl.when((zp >= z) & (z > 0))(lambda: self.left(k).start())

    def across(self, k):
        self.over_x(k).start()
        self.over_y(k).start()

    def begin(self):
        @pl.when(self.ahead)
        def _():
            for j in range(self.parts):
                self.onward(self.z * self.parts + j)
                self.across(self.z * self.parts + j)

        for k in range(self.reach):
            self.along(k)

    def turn(self, k):
        z, x, y = self.z, self.x, self.y
        zp, base = self.at(k)
        self.along(k + self.reach)
        pl.when((k < self.steps) & ((zp != z) | (z < self.zn // 2)))(lambda: self.across(k))

        q = k - self.lag

        @pl.when((q >= 0) & (q < self.steps))
        def _():
            self.arrival(self.ref(q, 1 - x, y), q, 1)
            self.upper(q).start()
            self.arrival(self.ref(q, x, 1 - y), q, 2)
            self.lower(q).start()

        r = k - 2 * self.lag

        @pl.when((r >= 0) & (r < self.steps))
        def _():
            self.arrival(self.ref(r, 1 - x, 1 - y, 0, self.half), r, 3)
            self.arrival(self.ref(r, 1 - x, 1 - y, self.half, self.size - self.half), r, 4)
            self.over_c(r, self.c).start()

    def pump(self, low, high):
        def one(k, carry):
            self.turn(k)
            return carry

        if high > low:
            lax.fori_loop(low, high, one, 0)

    def arrived(self, low, high):
        def one(k, carry):
            self.over_c(k, 1 - self.c).wait_recv()
            return carry

        lax.fori_loop(low * self.parts, high * self.parts, one, 0)

    def sent(self):
        z = self.z

        def one(k, carry):
            zp, base = self.at(k)
            pl.when((zp <= z) & (z < self.zn - 1))(lambda: self.right(k).wait_send())
            pl.when((zp >= z) & (z > 0))(lambda: self.left(k).wait_send())
            for item in (self.over_x(k), self.over_y(k), self.upper(k), self.lower(k)):
                item.wait_send()
            self.over_c(k, self.c).wait_send()
            return carry

        lax.fori_loop(0, self.steps, one, 0)


class KeyExchange:
    def __init__(self, kv_ref, all_ref, send, recv, lsem, parts):
        z, x, y, c = coords()
        rows = kv_ref.shape[0]
        piece = rows // parts
        to_y = place(z, x, 1 - y, c)
        to_c = place(z, x, y, 1 - c)
        mine = y * 2 + c
        beyond = (1 - y) * 2 + c
        self.parts = parts

        def part(row, k):
            return all_ref.at[pl.ds(pl.multiple_of(row * rows, rows) + k * piece, piece)]

        self.keep = pltpu.make_async_copy(
            kv_ref, all_ref.at[pl.ds(pl.multiple_of(mine * rows, rows), rows)], lsem
        )
        self.own_y, self.own_c, self.pass_c = [], [], []
        for k in range(parts):
            src, dst = kv_ref.at[pl.ds(k * piece, piece)], part(mine, k)
            self.own_y.append(remote(src, dst, send.at[0, k], recv.at[0, k], to_y))
            self.own_c.append(remote(src, dst, send.at[1, k], recv.at[1, k], to_c))
            ref = part(beyond, k)
            self.pass_c.append(remote(ref, ref, send.at[2, k], recv.at[2, k], to_c))

    def start(self):
        self.keep.start()
        for item in self.own_y + self.own_c:
            item.start()

    def forward(self):
        for k in range(self.parts):
            self.own_y[k].wait_recv()
            self.pass_c[k].start()

    def finish(self):
        for k in range(self.parts):
            self.own_c[k].wait_recv()
            self.pass_c[k].wait_recv()
        for item in self.own_y + self.own_c + self.pass_c:
            item.wait_send()
        self.keep.wait()


REGIONS = {"qkv": (0, BASE_OUT), "out": (BASE_OUT, BASE_GU), "gu": (BASE_GU, BASE_DOWN), "down": (BASE_DOWN, LAYER_ROWS)}
GROUPS = ((0, 6), (6, TILES))


def fill_flat(slots, flat, layer, name, rows, share):
    low, high = REGIONS[name]
    step = chunk_rows(rows)
    per_layer = LAYER_ROWS * LANES // share

    def one(i, carry):
        start = lax.div(share * i, LANES) - low + rows
        shift = lax.rem(share * i, LANES)
        index = i + layer * per_layer
        z, x = lax.div(index, 8), lax.rem(lax.div(index, 4), 2)
        y, c = lax.rem(lax.div(index, 2), 2), lax.rem(index, 2)
        edge = flat[pl.ds(start, 1), :]

        def fill(j, inner):
            flat[pl.ds(start + j * step, step), :] = slots[
                z, c, x * 2 + y, pl.ds(j * step, step), :
            ].astype(f32)
            return inner

        lax.fori_loop(0, rows // step, fill, 0)

        @pl.when(shift > 0)
        def _():
            flat[pl.ds(start, 1), :] = flat[pl.ds(start, 1), :] + edge

        return carry

    lax.fori_loop(low * LANES // share, (high * LANES - 1) // share + 1, one, 0)


def take_qkv(flat, top, qkv_ref):
    for col in range(12):
        qkv_ref[:, 128 * col : 128 * col + 128] = flat[pl.ds(top + col, D, stride=12), :].astype(bf16)


def take_out(flat, top, out_ref):
    for col in range(4):
        span = slice(128 * col, 128 * col + 128)
        out_ref[:, span] = flat[pl.ds(top + col, D, stride=4), :].astype(bf16)


def take_down(flat, top, down_ref, gains_ref):
    base = top + BASE_GAINS - BASE_DOWN
    for col in range(4):
        span = slice(128 * col, 128 * col + 128)
        down_ref[0:FF, span] = flat[pl.ds(top + col, FF, stride=4), :].astype(bf16)
        gains_ref[:, span] = flat[pl.ds(base + col, 2, stride=4), :]
    down_ref[FF:FFP, :] = jnp.zeros((FFP - FF, D), bf16)


def take_gate_up(flat, top, gate_up, gu_ref, group):
    lane = lax.broadcasted_iota(jnp.int32, (64, LANES), 1)
    low, high = group
    for r in range(8):
        for part in range(2):
            for tile in range(low, high):
                first = GU_ROW * r + FF * part + LANES * tile
                q, s = first // LANES, first % LANES
                value = flat[pl.ds(top + q, 64, stride=PERIOD), :]
                if s:
                    after = flat[pl.ds(top + q + 1, 64, stride=PERIOD), :]
                    value = jnp.where(
                        lane < LANES - s,
                        pltpu.roll(value, LANES - s, 1),
                        pltpu.roll(after, LANES - s, 1),
                    )
                if tile == TILES - 1:
                    value = jnp.where(lane < FF - LANES * tile, value, 0.0)
                gate_up[2 * (tile - low) + part, pl.ds(r, 64, stride=8), :] = value
    for k in range(2 * (high - low)):
        span = slice(256 * low + 128 * k, 256 * low + 128 * k + 128)
        gu_ref[:, span] = gate_up[k].astype(bf16)


def gate_up_segments(q):
    pieces = []
    place_now = LANES * q
    end = place_now + LANES
    while place_now < end:
        r, within = divmod(place_now, GU_ROW)
        part, unit = divmod(within, FF)
        tile, lane_src = divmod(unit, LANES)
        room = min(end - place_now, FF - unit, LANES - lane_src)
        lane_dst = place_now - LANES * q
        pieces.append((r, 2 * tile + part, lane_dst, lane_dst + room, (lane_dst - lane_src) % LANES))
        place_now += room
    return pieces


def gate_up_rows(tile):
    out = []
    for q in range(PERIOD):
        pieces = gate_up_segments(q)
        if max(k // 2 for _, k, _, _, _ in pieces) == tile:
            out.append((q, pieces))
    return out


def grad_qkv(flat, a_low, lin_ref):
    for t in range(6):
        value = mm_tn(a_low, lin_ref[:, 256 * t : 256 * t + 256])
        for k in range(2):
            flat[pl.ds(2 * t + k, D, stride=12), :] = value[:, 128 * k : 128 * k + 128]


def grad_out(flat, ctx, ea):
    for t in range(2):
        value = mm_tn(ctx, ea[:, 256 * t : 256 * t + 256])
        for k in range(2):
            flat[pl.ds(BASE_OUT + 2 * t + k, D, stride=4), :] = value[:, 128 * k : 128 * k + 128]


def grad_down(flat, units, ef):
    for t in range(2):
        value = mm_tn(units, ef[:, 256 * t : 256 * t + 256])
        for k in range(2):
            start = BASE_DOWN - BASE_GU + 2 * t + k
            flat[pl.ds(start, FF, stride=4), :] = value[0:FF, 128 * k : 128 * k + 128]


def grad_gate_up(flat, ring, t, b_low, eboth_ref):
    def at(tile):
        return 2 if tile == 0 else tile % 2

    value = mm_tn(b_low, eboth_ref[:, 256 * t : 256 * t + 256])
    for k in range(2):
        ring[2 * at(t) + k] = value[:, 128 * k : 128 * k + 128]
    lane = lax.broadcasted_iota(jnp.int32, (64, LANES), 1)
    for q, pieces in gate_up_rows(t):
        total = None
        for r, k, low, high, turn in pieces:
            piece = ring[2 * at(k // 2) + k % 2, pl.ds(r, 64, stride=8), :]
            if turn:
                piece = pltpu.roll(piece, turn, 1)
            total = piece if total is None else jnp.where(lane < low, total, piece)
        flat[pl.ds(q, 64, stride=PERIOD), :] = total


def grad_gains(flat, first, second):
    base = BASE_GAINS - BASE_GU
    for col in range(4):
        flat[pl.ds(base + col, 1), :] = first[:, 128 * col : 128 * col + 128]
        flat[pl.ds(base + 4 + col, 1), :] = second[:, 128 * col : 128 * col + 128]
    flat[LAYER_ROWS - BASE_GU :, :] = jnp.zeros((flat.shape[0] - LAYER_ROWS + BASE_GU, LANES), f32)


def flat_rows(rows):
    return LAYER_ROWS - BASE_GU + rows


def split_slot(share):
    return BASE_GU * LANES // share + 1


def carry_edge(flat, rows):
    flat[BASE_GU : BASE_GU + rows, :] = flat[0:rows, :]


def emit_slots(flat, base, stage, out_ref, sem, rows, share, low, high):
    step = chunk_rows(rows)

    def put(i):
        k = lax.rem(i, 2)
        z, x = lax.div(i, 8), lax.rem(lax.div(i, 4), 2)
        y, c = lax.rem(lax.div(i, 2), 2), lax.rem(i, 2)
        return pltpu.make_async_copy(stage.at[k], out_ref.at[z, c, x, y], sem.at[k])

    def one(i, carry):
        pl.when(i >= low + 2)(lambda: put(i - 2).wait())
        start = lax.div(share * i, LANES) - base
        k = lax.rem(i, 2)

        def fill(j, inner):
            stage[k, pl.ds(j * step, step), :] = flat[pl.ds(start + j * step, step), :].astype(bf16)
            return inner

        lax.fori_loop(0, rows // step, fill, 0)
        put(i).start()
        return carry

    lax.fori_loop(low, high, one, 0)
    put(high - 2).wait()
    put(high - 1).wait()


class KeySum:
    def __init__(self, part_ref, sum_ref, from_c, pair, from_y, send, recv):
        z, x, y, c = coords()
        self.part, self.sum_ref = part_ref, sum_ref
        self.from_c, self.pair, self.from_y = from_c, pair, from_y
        self.send, self.recv = send, recv
        self.rows = pair.shape[1]
        self.y, self.c = y, c
        self.to_y = place(z, x, 1 - y, c)
        self.to_c = place(z, x, y, 1 - c)

    def block(self, i, yp, cp):
        start = pl.multiple_of((yp * 2 + cp) * self.rows, self.rows)
        return self.part.at[i, pl.ds(start, self.rows)]

    def near(self, i, h):
        yp = self.y if h else 1 - self.y
        return remote(
            self.block(i, yp, 1 - self.c), self.from_c.at[h, i],
            self.send.at[i, h], self.recv.at[i, h], self.to_c,
        )

    def wide(self, i):
        return remote(
            self.pair.at[i], self.from_y.at[i], self.send.at[i, 2], self.recv.at[i, 2], self.to_y
        )

    def start(self, i):
        self.near(i, 0).start()
        self.near(i, 1).start()

    def middle(self, i):
        self.near(i, 0).wait_recv()
        self.pair[i] = (
            self.from_c[0, i].astype(f32) + self.block(i, 1 - self.y, self.c)[...].astype(f32)
        ).astype(bf16)
        self.wide(i).start()

    def end(self, i):
        self.near(i, 1).wait_recv()
        self.wide(i).wait_recv()
        total = (
            self.from_c[1, i].astype(f32)
            + self.block(i, self.y, self.c)[...].astype(f32)
            + self.from_y[i].astype(f32)
        ).astype(bf16)
        self.sum_ref[:, LANES * i : LANES * i + LANES] = total[:, :LANES]
        self.sum_ref[:, D + LANES * i : D + LANES * i + LANES] = total[:, LANES:]

    def sent(self):
        for i in range(HEADS // 2):
            self.near(i, 0).wait_send()
            self.near(i, 1).wait_send()
            self.wide(i).wait_send()


def key_sum_scratch(rows):
    pairs = HEADS // 2
    return [
        pltpu.VMEM((pairs, 4 * rows, 2 * LANES), bf16),
        pltpu.VMEM((2, pairs, rows, 2 * LANES), bf16),
        pltpu.VMEM((pairs, rows, 2 * LANES), bf16),
        pltpu.VMEM((pairs, rows, 2 * LANES), bf16),
        pltpu.SemaphoreType.DMA((pairs, 3)),
        pltpu.SemaphoreType.DMA((pairs, 3)),
    ]


def half_swap(u):
    lane = lax.broadcasted_iota(jnp.int32, u.shape, 1)
    return jnp.where(lax.rem(lane, 64) < 32, pltpu.roll(u, 96, 1), pltpu.roll(u, 32, 1))


def project_heads(a_low, w_ref, cos_ref, sin_ref, q_ref, kv_ref, tiles=range(6)):
    for t in tiles:
        lin = mm(a_low, w_ref[:, 256 * t : 256 * t + 256])
        for k in range(2):
            u = lin[:, 128 * k : 128 * k + 128]
            if t < 4:
                u = u * cos_ref[...] + half_swap(u) * sin_ref[...]
            col = 256 * t + 128 * k
            if col < D:
                q_ref[:, col : col + 128] = u.astype(bf16)
            else:
                kv_ref[:, col - D : col - D + 128] = u.astype(bf16)


def norm_factor(r):
    return lax.rsqrt(jnp.mean(r * r, axis=-1, keepdims=True) + NORM_EPS)


def norm_back(e, r, f, g):
    scaled = e * g
    gain = jnp.sum(e * r * f, axis=0, keepdims=True)
    grad = f * scaled - r * (f * f * f) * jnp.mean(scaled * r, axis=-1, keepdims=True)
    return grad, gain


def head_mask(rows, h):
    lane = lax.broadcasted_iota(jnp.int32, (rows, LANES), 1)
    return (lane >= 64) if h else (lane < 64)


def make_bias(bias, length):
    rows, cols = bias.shape
    first = lax.axis_index("sp") * rows
    row = lax.broadcasted_iota(jnp.int32, (rows, cols), 0) + first
    col = lax.broadcasted_iota(jnp.int32, (rows, cols), 1)
    bias[...] = jnp.where((col <= row) & (col < length), 0.0, -1e9)


def attend(i, q_ref, kv_ref, bias, p_ref, ctx_ref):
    rows = q_ref.shape[0]
    span = slice(LANES * i, LANES * i + LANES)
    keys = kv_ref[:, span]
    values = kv_ref[:, D + LANES * i : D + LANES * i + LANES]
    queries = q_ref[:, span]
    total = jnp.zeros((rows, LANES), f32)
    for h in range(2):
        qm = jnp.where(head_mask(rows, h), queries, jnp.zeros_like(queries))
        vm = jnp.where(head_mask(values.shape[0], h), values, jnp.zeros_like(values))
        logits = mm_nt(qm, keys) * HEAD_DIM ** (-0.5) + bias[...]
        top = jnp.max(logits, axis=-1, keepdims=True)
        soft = jnp.exp(logits - top)
        norm = 1.0 / jnp.sum(soft, axis=-1, keepdims=True)
        low = (soft * norm).astype(bf16)
        p_ref[2 * i + h] = low
        total = total + mm(low, vm)
    ctx_ref[:, span] = total.astype(bf16)


def attend_back(i, q_ref, kv_ref, p_ref, ectx_ref, eq_ref, dkv_ref):
    rows = q_ref.shape[0]
    cols = kv_ref.shape[0]
    span = slice(LANES * i, LANES * i + LANES)
    keys = kv_ref[:, span]
    values = kv_ref[:, D + LANES * i : D + LANES * i + LANES]
    queries = q_ref[:, span]
    grads = ectx_ref[:, span]
    dq = jnp.zeros((rows, LANES), f32)
    dk = jnp.zeros((LANES, cols), f32)
    dv = jnp.zeros((LANES, cols), f32)
    for h in range(2):
        mask = head_mask(rows, h)
        qm = jnp.where(mask, queries, jnp.zeros_like(queries))
        em = jnp.where(mask, grads, jnp.zeros_like(grads))
        km = jnp.where(head_mask(cols, h), keys, jnp.zeros_like(keys))
        low = p_ref[2 * i + h]
        soft = low.astype(f32)
        dp = mm_nt(em, values)
        center = jnp.sum(soft * dp, axis=-1, keepdims=True)
        raw = (soft * (dp - center) * HEAD_DIM ** (-0.5)).astype(bf16)
        dv = dv + mm_tn(em, low)
        dk = dk + mm_tn(qm, raw)
        dq = dq + mm(raw, km)
    eq_ref[:, span] = dq.astype(bf16)
    dkv_ref[i, :, :LANES] = dk.T.astype(bf16)
    dkv_ref[i, :, LANES:] = dv.T.astype(bf16)


def feed_forward(b_low, gu_ref, down_ref, both_ref, units_ref):
    for t in range(TILES):
        both = mm(b_low, gu_ref[:, 256 * t : 256 * t + 256])
        both_ref[:, 256 * t : 256 * t + 256] = both
        gate, up = both[:, :128], both[:, 128:]
        units_ref[:, 128 * t : 128 * t + 128] = (gate / (1.0 + jnp.exp(-gate)) * up).astype(bf16)
    return mm(units_ref[...], down_ref[...])


def feed_back(e_low, gu_ref, down_ref, both_ref, eboth_ref, pump=None):
    for t in range(TILES):
        if pump is not None and t % 4 == 3:
            pump()
        eu = mm_nt(e_low, down_ref[128 * t : 128 * t + 128, :])
        gate = both_ref[:, 256 * t : 256 * t + 128]
        up = both_ref[:, 256 * t + 128 : 256 * t + 256]
        sig = 1.0 / (1.0 + jnp.exp(-gate))
        eboth_ref[:, 256 * t : 256 * t + 128] = (eu * up * sig * (1.0 + gate * (1.0 - sig))).astype(bf16)
        eboth_ref[:, 256 * t + 128 : 256 * t + 256] = (eu * gate * sig).astype(bf16)
    return mm_nt(eboth_ref[...], gu_ref[...])


def stage_head(length, master_pad, hidden, cos, sin, zn, rows_slot, share):
    rows = hidden.shape[0]
    cols = 4 * rows
    step = chunk_rows(rows_slot)
    half_zn = zn // 2
    ndev = zn * 8
    gains_row = BASE_GAINS - share * (ndev // 2 - 1) // LANES
    first_zp = -(-BASE_OUT * LANES // (8 * share))
    parts = 4
    gather_steps = zn * Gather.pieces(rows_slot)
    top = rows_slot

    def body(
        l_ref, x_ref, h_ref, c_ref, s_ref,
        g0, g1, q0, ctx_ref, r1_ref, b_ref, units_ref, r2_ref, sec_ref, a1_ref, q1,
        wq0_any, wo0_any, wg0_any, wd0_any, wq1_any, wo1_any, wg1_any, wd1_any,
        kv0_any, kv1_any, p_any, both_any,
        wq0, wo0, wg0, wd0, wq1, wo1, wg1, wd1, all0, all1, p_ref, both_ref,
        slots, flat, gate_up, kv0, kv1, bias, send, recv,
        ksend0, krecv0, ksend1, krecv1, lsem, osem, gains_out, gains_in, gsend, grecv,
    ):
        z, x, y, c = coords()
        bar = pltpu.get_barrier_semaphore()

        def hello(device):
            pl.semaphore_signal(bar, inc=1, device_id=device, device_id_type=MESH)

        hello(place(z, 1 - x, y, c))
        hello(place(z, x, 1 - y, c))
        hello(place(z, x, y, 1 - c))
        pl.when(z > 0)(lambda: hello(place(z - 1, x, y, c)))
        pl.when(z < zn - 1)(lambda: hello(place(z + 1, x, y, c)))
        me = ((z * 2 + x) * 2 + y) * 2 + c
        owner = me == ndev - 1
        pl.when(me != ndev - 1)(lambda: hello(place(zn - 1, 1, 1, 1)))

        shift = lax.rem(share * (((z * 2 + x) * 2 + y) * 2 + c), LANES)
        lane = lax.broadcasted_iota(jnp.int32, (step, LANES), 1)

        def align(i, carry):
            now = pltpu.roll(x_ref[pl.ds(8 + i * step, step), :], shift, 1)
            before = pltpu.roll(x_ref[pl.ds(7 + i * step, step), :], shift, 1)
            slots[z, c, x * 2 + y, pl.ds(i * step, step), :] = jnp.where(
                lane >= shift, now, before
            ).astype(bf16)
            return carry

        lax.fori_loop(0, rows_slot // step, align, 0)
        now = pltpu.roll(x_ref[pl.ds(8 + gains_row, 8), :], shift, 1)
        before = pltpu.roll(x_ref[pl.ds(7 + gains_row, 8), :], shift, 1)
        gains_out[...] = jnp.zeros((16, LANES), bf16)
        gains_out[0:8, :] = jnp.where(lane[0:8] >= shift, now, before).astype(bf16)
        pl.semaphore_wait(
            bar,
            3
            + (z > 0).astype(jnp.int32)
            + (z < zn - 1).astype(jnp.int32)
            + owner.astype(jnp.int32) * (ndev - 1),
        )

        def tell_gains(d):
            device = {"dp": lax.div(d, 4), "sp": lax.rem(d, 4)}
            return remote(gains_out, gains_in, gsend.at[d], grecv, device)

        @pl.when(owner)
        def _():
            def go(d, carry):
                tell_gains(d).start()
                return carry

            lax.fori_loop(0, ndev - 1, go, 0)
            gains_in[...] = gains_out[...]

        gather = Gather(slots, send, recv, zn, rows_slot)
        done = [0]

        def pump(until):
            gather.pump(done[0], until)
            done[0] = max(done[0], until)

        def between(low, high, k, n):
            pump(low + (high - low) * k // n)

        saves = [
            pltpu.make_async_copy(src, dst, osem.at[i])
            for i, (src, dst) in enumerate(
                [
                    (wq0, wq0_any), (wo0, wo0_any), (wg0, wg0_any), (wd0, wd0_any),
                    (wq1, wq1_any), (wo1, wo1_any), (wg1, wg1_any), (wd1, wd1_any),
                    (all0, kv0_any), (all1, kv1_any), (p_ref, p_any), (both_ref, both_any),
                ]
            )
        ]

        def fill(layer, name):
            fill_flat(slots, flat, layer, name, rows_slot, share)

        gather.begin()
        make_bias(bias, l_ref[0])
        pump(gather.until(first_zp))
        gather.arrived(0, first_zp)
        fill(0, "qkv")
        take_qkv(flat, top, wq0)
        exchange0 = KeyExchange(kv0, all0, ksend0, krecv0, lsem.at[0], parts)
        project_heads(h_ref[...], wq0, c_ref, s_ref, q0, kv0, range(2, 6))
        exchange0.start()
        saves[0].start()
        low, high = gather.until(first_zp), gather.until(half_zn)
        between(low, high, 1, 2)
        project_heads(h_ref[...], wq0, c_ref, s_ref, q0, kv0, range(2))
        exchange0.forward()
        pump(high)
        exchange0.finish()
        saves[8].start()
        low, high = high, gather.until(half_zn + first_zp)
        for i in range(HEADS // 2):
            attend(i, q0, all0, bias, p_ref, ctx_ref)
            if i == 1:
                between(low, high, 1, 2)
        saves[10].start()
        gather.arrived(first_zp, half_zn)
        fill(0, "out")
        take_out(flat, top, wo0)
        saves[1].start()
        fill(0, "down")
        take_down(flat, top, wd0, g0)
        saves[3].start()
        pump(high)
        fill(0, "gu")
        for group in GROUPS:
            take_gate_up(flat, top, gate_up, wg0, group)
        saves[2].start()
        low, high = high, gather.until(zn)
        between(low, high, 1, 3)
        r1 = h_ref[...].astype(f32) + mm(ctx_ref[...], wo0[...])
        r1_ref[...] = r1
        first = r1 * norm_factor(r1) * g0[0:1, :]
        b_ref[...] = first.astype(bf16)
        r2 = first + feed_forward(b_ref[...], wg0, wd0, both_ref, units_ref)
        saves[11].start()
        r2_ref[...] = r2
        second = r2 * norm_factor(r2) * g0[1:2, :]
        sec_ref[...] = second
        between(low, high, 2, 3)
        gather.arrived(half_zn, half_zn + first_zp)
        fill(1, "qkv")
        take_qkv(flat, top, wq1)
        saves[4].start()

        @pl.when(me != ndev - 1)
        def _():
            tell_gains(0).wait_recv()

        known = gains_in[...].astype(f32)
        for col in range(4):
            span = slice(LANES * col, LANES * col + LANES)
            g1[0:1, span] = known[col : col + 1, :]
            g1[1:2, span] = known[4 + col : 5 + col, :]
        a1_ref[...] = (second * norm_factor(second) * g1[0:1, :]).astype(bf16)
        exchange1 = KeyExchange(kv1, all1, ksend1, krecv1, lsem.at[1], parts)
        project_heads(a1_ref[...], wq1, c_ref, s_ref, q1, kv1, range(2, 6))
        exchange1.start()
        project_heads(a1_ref[...], wq1, c_ref, s_ref, q1, kv1, range(2))
        pump(high)
        gather.arrived(half_zn + first_zp, zn)
        fill(1, "down")
        take_down(flat, top, wd1, g1)
        saves[7].start()
        fill(1, "out")
        take_out(flat, top, wo1)
        saves[5].start()
        fill(1, "gu")
        take_gate_up(flat, top, gate_up, wg1, GROUPS[0])
        exchange1.forward()
        take_gate_up(flat, top, gate_up, wg1, GROUPS[1])
        saves[6].start()
        exchange1.finish()
        saves[9].start()
        gather.sent()

        @pl.when(owner)
        def _():
            def wait(d, carry):
                tell_gains(d).wait_send()
                return carry

            lax.fori_loop(0, ndev - 1, wait, 0)

        for item in saves:
            item.wait()

    layer = [((D, 3 * D), bf16), ((D, D), bf16), ((D, 2 * FFP), bf16), ((FFP, D), bf16)]
    kept = layer + layer + [
        ((cols, 2 * D), bf16),
        ((cols, 2 * D), bf16),
        ((HEADS, rows, cols), bf16),
        ((rows, 2 * FFP), f32),
    ]
    low_rows, full_rows = ((rows, D), bf16), ((rows, D), f32)
    outs = [
        ((2, D), f32),
        ((2, D), f32),
        low_rows,
        low_rows,
        full_rows,
        low_rows,
        ((rows, FFP), bf16),
        full_rows,
        full_rows,
        low_rows,
        low_rows,
    ]
    ins = [length, master_pad, hidden, cos, sin]
    longest = max(high - low for low, high in REGIONS.values())
    kv_scratch = pltpu.VMEM((rows, 2 * D), bf16)
    return pl.pallas_call(
        body,
        out_shape=[jax.ShapeDtypeStruct(s, d) for s, d in outs + kept],
        in_specs=[pl.BlockSpec(memory_space=pltpu.SMEM)] + [vmem_spec()] * (len(ins) - 1),
        out_specs=[vmem_spec()] * len(outs) + [any_spec()] * len(kept),
        scratch_shapes=[pltpu.VMEM(s, d) for s, d in kept]
        + [
            pltpu.VMEM((zn, 2, 4, rows_slot, LANES), bf16),
            pltpu.VMEM((longest + 2 * rows_slot, LANES), f32),
            pltpu.VMEM((12, D, LANES), f32),
            kv_scratch,
            kv_scratch,
            pltpu.VMEM((rows, cols), f32),
            pltpu.SemaphoreType.DMA((gather_steps, 7)),
            pltpu.SemaphoreType.DMA((gather_steps, 6)),
            pltpu.SemaphoreType.DMA((3, parts)),
            pltpu.SemaphoreType.DMA((3, parts)),
            pltpu.SemaphoreType.DMA((3, parts)),
            pltpu.SemaphoreType.DMA((3, parts)),
            pltpu.SemaphoreType.DMA((2,)),
            pltpu.SemaphoreType.DMA((12,)),
            pltpu.VMEM((16, LANES), bf16),
            pltpu.VMEM((16, LANES), bf16),
            pltpu.SemaphoreType.DMA((ndev,)),
            pltpu.SemaphoreType.DMA,
        ],
        compiler_params=pltpu.CompilerParams(
            collective_id=1, has_side_effects=True, vmem_limit_bytes=62 * MIB
        ),
    )(*ins)


class Loads:
    def __init__(self, pairs, sem):
        self.items = [pltpu.make_async_copy(src, dst, sem.at[i]) for i, (src, dst) in enumerate(pairs)]
        for item in self.items:
            item.start()

    def wait(self, *which):
        for i in which:
            self.items[i].wait()


def meet(devices):
    bar = pltpu.get_barrier_semaphore()
    for device in devices:
        pl.semaphore_signal(bar, inc=1, device_id=device, device_id_type=MESH)
    pl.semaphore_wait(bar, len(devices))


def stage_second(
    length, cotangent, second, q, kv, w_out, w_gu, w_down, w_qkv, gains, a1, cos, sin, share, rows_slot
):
    rows = q.shape[0]
    cols = kv.shape[0]
    per_layer = LAYER_ROWS * LANES // share
    middle = split_slot(share)

    def body(
        l_ref, cot_ref, sec_ref, q_ref, g_ref, a_ref, c_ref, s_ref, kv_any, wo_any, gu_any, dn_any, wq_any,
        o_ref, e2_ref, gg_ref, slots_ref,
        kv_ref, wo_ref, gu_ref, dn_ref, wq_ref, lsem, eq_ref, lin_ref,
        bias, p_ref, ctx_ref, b_ref, both_ref, units_ref, eboth_ref, ef_ref, ea_ref, ectx_ref,
        ekv_ref, flat, ring, stage, esem,
        dkv_ref, from_c, pair, from_y, send, recv,
    ):
        loads = Loads(
            [
                (kv_any, kv_ref), (wo_any, wo_ref), (gu_any, gu_ref), (dn_any, dn_ref), (wq_any, wq_ref)
            ],
            lsem,
        )
        z, x, y, c = coords()
        meet([place(z, x, 1 - y, c), place(z, x, y, 1 - c)])
        total = KeySum(dkv_ref, ekv_ref, from_c, pair, from_y, send, recv)
        length_now = l_ref[0]
        make_bias(bias, length_now)
        loads.wait(0)
        for i in range(HEADS // 2):
            attend(i, q_ref, kv_ref, bias, p_ref, ctx_ref)
        loads.wait(1, 2, 3)
        third = sec_ref[...] + mm(ctx_ref[...], wo_ref[...])
        f4 = norm_factor(third)
        b_ref[...] = (third * f4 * g_ref[1:2, :]).astype(bf16)
        o_ref[...] = third + feed_forward(b_ref[...], gu_ref, dn_ref, both_ref, units_ref)
        place_now = lax.broadcasted_iota(jnp.int32, (rows, D), 0) + lax.axis_index("sp") * rows
        e_out = jnp.where(place_now < length_now, cot_ref[...], 0.0)
        ef_ref[...] = e_out.astype(bf16)
        e_b = feed_back(ef_ref[...], gu_ref, dn_ref, both_ref, eboth_ref)
        grad, gain = norm_back(e_b, third, f4, g_ref[1:2, :])
        gg_ref[1:2, :] = gain
        e3 = e_out + grad
        e2_ref[...] = e3
        ea_ref[...] = e3.astype(bf16)
        ectx_ref[...] = mm_nt(ea_ref[...], wo_ref[...]).astype(bf16)
        for i in range(HEADS // 2):
            attend_back(i, q_ref, kv_ref, p_ref, ectx_ref, eq_ref, dkv_ref)
            total.start(i)
            if i >= 1:
                total.middle(i - 1)
        for t in range(TILES):
            grad_gate_up(flat, ring, t, b_ref[...], eboth_ref)
            if t == 0:
                total.middle(3)
            if t in (1, 4, 7, 10):
                total.end((t - 1) // 3)
        lin_grads(eq_ref, ekv_ref, c_ref, s_ref, lin_ref)
        grad_down(flat, units_ref[...], ef_ref[...])
        loads.wait(4)
        second = sec_ref[...]
        grad, gain = norm_back(
            mm_nt(lin_ref[...], wq_ref[...]), second, norm_factor(second), g_ref[0:1, :]
        )
        gg_ref[0:1, :] = gain
        e2_ref[...] = e2_ref[...] + grad
        grad_gains(flat, gg_ref[0:1, :], gg_ref[1:2, :])
        emit_slots(flat, BASE_GU, stage, slots_ref, esem, rows_slot, share, middle, per_layer)
        carry_edge(flat, rows_slot)
        grad_out(flat, ctx_ref[...], ea_ref[...])
        grad_qkv(flat, a_ref[...], lin_ref)
        emit_slots(flat, 0, stage, slots_ref, esem, rows_slot, share, 0, middle)
        total.sent()

    outs = [
        ((rows, D), f32),
        ((rows, D), f32),
        ((2, D), f32),
        ((per_layer // 8, 2, 2, 2, rows_slot, LANES), bf16),
    ]
    ins = [length, cotangent, second, q, gains, a1, cos, sin, kv, w_out, w_gu, w_down, w_qkv]
    return pl.pallas_call(
        body,
        out_shape=[jax.ShapeDtypeStruct(s, d) for s, d in outs],
        in_specs=[pl.BlockSpec(memory_space=pltpu.SMEM)] + [vmem_spec()] * 7 + [any_spec()] * 5,
        out_specs=[vmem_spec()] * 3 + [any_spec()],
        scratch_shapes=[
            pltpu.VMEM((cols, 2 * D), bf16),
            pltpu.VMEM((D, D), bf16),
            pltpu.VMEM((D, 2 * FFP), bf16),
            pltpu.VMEM((FFP, D), bf16),
            pltpu.VMEM((D, 3 * D), bf16),
            pltpu.SemaphoreType.DMA((5,)),
            pltpu.VMEM((rows, D), bf16),
            pltpu.VMEM((rows, 3 * D), bf16),
            pltpu.VMEM((rows, cols), f32),
            pltpu.VMEM((HEADS, rows, cols), bf16),
            pltpu.VMEM((rows, D), bf16),
            pltpu.VMEM((rows, D), bf16),
            pltpu.VMEM((rows, 2 * FFP), f32),
            pltpu.VMEM((rows, FFP), bf16),
            pltpu.VMEM((rows, 2 * FFP), bf16),
            pltpu.VMEM((rows, D), bf16),
            pltpu.VMEM((rows, D), bf16),
            pltpu.VMEM((rows, D), bf16),
            pltpu.VMEM((rows, 2 * D), bf16),
            pltpu.VMEM((flat_rows(rows_slot), LANES), f32),
            pltpu.VMEM((6, D, LANES), f32),
            pltpu.VMEM((2, rows_slot, LANES), bf16),
            pltpu.SemaphoreType.DMA((2,)),
        ]
        + key_sum_scratch(rows),
        compiler_params=pltpu.CompilerParams(
            collective_id=3, has_side_effects=True, vmem_limit_bytes=60 * MIB
        ),
    )(*ins)


def lin_grads(eq_ref, ekv_ref, cos_ref, sin_ref, lin_ref):
    for t in range(12):
        col = 128 * t
        src = eq_ref[:, col : col + 128] if t < 4 else ekv_ref[:, col - D : col - D + 128]
        if t < 8:
            w = src.astype(f32)
            src = (w * cos_ref[...] - half_swap(w) * sin_ref[...]).astype(bf16)
        lin_ref[:, col : col + 128] = src


def when(condition):
    if isinstance(condition, bool):
        return (lambda act: act()) if condition else (lambda act: None)
    return pl.when(condition)


class Reduce:
    room_static = 3
    lags = (1, 2, 3)

    def __init__(self, early, late, bufs, fin, send, recv, lsem, free, zn, rows, ahead=2):
        self.early, self.late, self.fin, self.free = early, late, fin, free
        self.acc, self.rc, self.first, self.second, self.rz = bufs
        self.send, self.recv, self.lsem = send, recv, lsem
        self.zn, self.half = zn, zn // 2
        self.static, self.room, self.table = self.plan(zn, rows)
        self.steps = len(self.table)
        self.ahead = ahead
        self.two, self.three, self.hop = self.lags
        self.retired = self.hop + zn - 1
        self.gap = 0 if self.static else max(0, self.retired - self.room) + ahead
        self.turns = self.steps + self.gap + self.retired + 1
        self.z, self.x, self.y, self.c = coords()
        z, x, y, c = self.z, self.x, self.y, self.c
        self.to_x = place(z, 1 - x, y, c)
        self.to_y = place(z, x, 1 - y, c)
        self.to_c = place(z, x, y, 1 - c)

    @classmethod
    def plan(cls, zn, rows):
        if rows // 16 != 98:
            chunk = (0, rows, rows // 32 * 16)
            return False, zn // 2, [(zp, chunk) for zp in range(zn - 1, -1, -1)]
        table = []
        for zp in range(zn - 1, -1, -1):
            base = 0
            for tiles in cls.sizes[min(zp, len(cls.sizes) - 1)]:
                table.append((zp, (base, 16 * tiles, 16 * round(tiles * cls.share_x))))
                base += 16 * tiles
        return True, min(cls.room_static, zn), table

    sizes = ((20, 20, 20, 19, 19), (33, 32, 33))
    share_x = 0.5

    def at(self, k):
        if self.static:
            zp, chunk = self.table[k]
            return zp, zp % self.room, chunk
        zp = self.zn - 1 - k
        return zp, lax.rem(zp, self.room), self.table[0][1]

    def ends(self, k):
        return k + 1 == self.steps or self.table[k + 1][0] != self.table[k][0]

    def opens(self, k):
        return k == 0 or self.table[k - 1][0] != self.table[k][0]

    def last_of(self, zp):
        return max(k for k in range(self.steps) if self.table[k][0] == zp)

    def step_at(self, u):
        if self.static:
            return u
        later = jnp.where(u < self.room + self.gap, -1, u - self.gap)
        return jnp.where(u < self.room, u, later)

    def starts_at(self, k):
        zp = self.table[k][0]
        turn = k - self.ahead
        if zp + self.room < self.zn:
            if not self.static:
                return k + self.gap - self.ahead
            turn = max(turn, self.last_of(zp + self.room) + self.retired)
            assert turn <= k
        return turn

    def limit(self, zp):
        return self.starts_at(min(k for k in range(self.steps) if self.table[k][0] == zp))

    def from_source(self, k, act):
        zp, loc, chunk = self.at(k)
        if isinstance(zp, int):
            act((self.late if zp >= self.half else self.early).at[zp % self.half])
        else:
            index = lax.rem(zp, self.half)
            pl.when(zp >= self.half)(lambda: act(self.late.at[index]))
            pl.when(zp < self.half)(lambda: act(self.early.at[index]))

    def cp(self, src, dst, k, s, r, device):
        return remote(src, dst, self.send.at[k, s], self.recv.at[k, r], device)

    def spans(self, k):
        zp, loc, (base, size, cut) = self.at(k)
        return pl.ds(base, cut), pl.ds(base + cut, size - cut)

    def core(self, k, src=None):
        zp, loc, (base, size, cut) = self.at(k)
        span = pl.ds(base, size)
        src = self.early.at[0] if src is None else src
        return self.cp(
            src.at[1 - self.c, :, :, span], self.rc.at[loc, :, :, span], k, 0, 0, self.to_c
        )

    def load(self, k, src=None):
        zp, loc, (base, size, cut) = self.at(k)
        span = pl.ds(base, size)
        src = self.early.at[0] if src is None else src
        return pltpu.make_async_copy(
            src.at[self.c, :, :, span], self.acc.at[loc, :, :, span], self.lsem.at[k]
        )

    def far_x(self, k):
        zp, loc, chunk = self.at(k)
        span = self.spans(k)[0]
        return self.cp(
            self.acc.at[loc, 1 - self.x, :, span], self.first.at[loc, :, span], k, 1, 1, self.to_x
        )

    def far_y(self, k):
        zp, loc, chunk = self.at(k)
        span = self.spans(k)[1]
        return self.cp(
            self.acc.at[loc, :, 1 - self.y, span], self.first.at[loc, :, span], k, 2, 2, self.to_y
        )

    def then_y(self, k):
        zp, loc, chunk = self.at(k)
        span = self.spans(k)[0]
        src = self.acc.at[loc, self.x, 1 - self.y, span]
        return self.cp(src, self.second.at[loc, span], k, 3, 3, self.to_y)

    def then_x(self, k):
        zp, loc, chunk = self.at(k)
        span = self.spans(k)[1]
        src = self.acc.at[loc, 1 - self.x, self.y, span]
        return self.cp(src, self.second.at[loc, span], k, 4, 4, self.to_x)

    def right(self, k):
        zp, loc, (base, size, cut) = self.at(k)
        span = pl.ds(base, size)
        return self.cp(
            self.acc.at[loc, self.x, self.y, span], self.rz.at[loc, 0, span], k, 5, 5,
            place(self.z + 1, self.x, self.y, self.c),
        )

    def left(self, k):
        zp, loc, (base, size, cut) = self.at(k)
        span = pl.ds(base, size)
        return self.cp(
            self.acc.at[loc, self.x, self.y, span], self.rz.at[loc, 1, span], k, 5, 6,
            place(self.z - 1, self.x, self.y, self.c),
        )

    def add(self, loc, xp, yp, span, src):
        value = self.acc[loc, xp, yp, span, :].astype(f32) + src.astype(f32)
        self.acc[loc, xp, yp, span, :] = value.astype(bf16)

    def ok(self, k):
        return (k >= 0) & (k < self.steps)

    def guard(self, k, act):
        if isinstance(k, int):
            if 0 <= k < self.steps:
                act()
        else:
            pl.when(self.ok(k))(act)

    def neighbours(self, act):
        z, x, y, c = self.z, self.x, self.y, self.c
        for device in (self.to_x, self.to_y, self.to_c):
            act(device)
        pl.when(z > 0)(lambda: act(place(z - 1, x, y, c)))
        pl.when(z < self.zn - 1)(lambda: act(place(z + 1, x, y, c)))

    def stage_core(self, k):
        def act():
            if self.static:
                if self.opens(k) and self.table[k][0] + self.room < self.zn:
                    self.claim(k)
            else:
                pl.when(k >= self.room)(lambda: self.claim(k))
            self.from_source(k, lambda src: self.core(k, src).start())
            self.from_source(k, lambda src: self.load(k, src).start())

        self.guard(k, act)

    def claim(self, k):
        z = self.z
        zp, loc, chunk = self.at(k)
        pl.semaphore_wait(
            self.free.at[loc],
            3 + (z > 0).astype(jnp.int32) + (z < self.zn - 1).astype(jnp.int32),
        )

    def retire(self, k):
        def act():
            zp, loc, chunk = self.at(k)
            for item in (
                self.core(k), self.far_x(k), self.far_y(k), self.then_x(k), self.then_y(k)
            ):
                item.wait_send()
            pl.when(zp > self.z)(lambda: self.right(k).wait_send())
            pl.when(zp < self.z)(lambda: self.left(k).wait_send())

            def tell():
                self.neighbours(
                    lambda d: pl.semaphore_signal(
                        self.free.at[loc], inc=1, device_id=d, device_id_type=MESH
                    )
                )

            if self.static:
                if self.ends(k) and zp >= self.room:
                    tell()
            else:
                pl.when(zp >= self.room)(tell)

        self.guard(k, act)

    def stage_one(self, k):
        def act():
            zp, loc, chunk = self.at(k)
            over_x, over_y = self.spans(k)
            x, y = self.x, self.y
            self.core(k).wait_recv()
            self.load(k).wait()

            def add(xp, yp, span):
                self.add(loc, xp, yp, span, self.rc[loc, xp, yp, span, :])

            add(1 - x, 0, over_x)
            add(1 - x, 1, over_x)
            self.far_x(k).start()
            add(0, 1 - y, over_y)
            add(1, 1 - y, over_y)
            self.far_y(k).start()
            add(x, 0, over_x)
            add(x, 1, over_x)
            add(0, y, over_y)
            add(1, y, over_y)

        self.guard(k, act)

    def stage_two(self, k):
        def act():
            zp, loc, chunk = self.at(k)
            over_x, over_y = self.spans(k)
            x, y = self.x, self.y

            def add(xp, yp, span, row):
                self.add(loc, xp, yp, span, self.first[loc, row, span, :])

            self.far_x(k).wait_recv()
            add(x, 1 - y, over_x, 1 - y)
            self.then_y(k).start()
            self.far_y(k).wait_recv()
            add(1 - x, y, over_y, 1 - x)
            self.then_x(k).start()
            add(x, y, over_x, y)
            add(x, y, over_y, x)

        self.guard(k, act)

    def stage_three(self, k):
        def act():
            zp, loc, (base, size, cut) = self.at(k)
            span = pl.ds(base, size)
            z, x, y = self.z, self.x, self.y
            self.then_y(k).wait_recv()
            self.then_x(k).wait_recv()

            @pl.when(zp == z)
            def _():
                self.fin[span, :] = self.acc[loc, x, y, span, :].astype(f32) + self.second[
                    loc, span, :
                ].astype(f32)

            @pl.when(zp != z)
            def _():
                self.add(loc, x, y, span, self.second[loc, span, :])

            pl.when((zp > z) & (z == 0))(lambda: self.right(k).start())
            pl.when((zp < z) & (z == self.zn - 1))(lambda: self.left(k).start())

        self.guard(k, act)

    def stage_hop(self, k, z, rightward):
        def act():
            zp, loc, (base, size, cut) = self.at(k)
            span = pl.ds(base, size)
            x, y = self.x, self.y
            item = self.right(k) if rightward else self.left(k)
            part = self.rz.at[loc, 0 if rightward else 1, span]

            onward = (zp > z) if rightward else (zp < z)

            @when(onward)
            def _():
                item.wait_recv()
                self.add(loc, x, y, span, part[...])
                item.start()

            @when(zp == z)
            def _():
                item.wait_recv()
                self.fin[span, :] = self.fin[span, :] + part[...].astype(f32)

        self.guard(k, act)

    def stage_four(self, u):
        z, last = self.z, self.zn - 1
        if not self.static:
            @pl.when(z > 0)
            def _():
                self.stage_hop(self.step_at(u - self.hop - (z - 1)), z, True)

            @pl.when(z < last)
            def _():
                self.stage_hop(self.step_at(u - self.hop - (last - z - 1)), z, False)

            return
        for place_z in range(self.zn):
            steps = []
            if place_z > 0:
                k = self.step_at(u - self.hop - (place_z - 1))
                if 0 <= k < self.steps and self.at(k)[0] >= place_z:
                    steps.append((k, True))
            if place_z < last:
                k = self.step_at(u - self.hop - (last - place_z - 1))
                if 0 <= k < self.steps and self.at(k)[0] <= place_z:
                    steps.append((k, False))
            if steps:

                @pl.when(z == place_z)
                def _(steps=steps, place_z=place_z):
                    for k, rightward in steps:
                        self.stage_hop(k, place_z, rightward)

    def begin(self):
        for k in range(min(self.ahead, self.steps)):
            self.stage_core(k)

    def turn(self, u):
        self.retire(self.step_at(u - self.retired))
        if self.static:
            for j in range(self.ahead, self.steps):
                if self.starts_at(j) == u:
                    self.stage_core(j)
        else:
            k = self.step_at(u + self.ahead)
            pl.when(k >= self.ahead)(lambda: self.stage_core(k))
        self.stage_one(self.step_at(u))
        self.stage_two(self.step_at(u - self.two))
        self.stage_three(self.step_at(u - self.three))
        self.stage_four(u)

    def pump(self, low, high):
        if self.static:
            for k in range(low, high):
                self.turn(k)
        elif high > low:

            def one(k, carry):
                self.turn(k)
                return carry

            lax.fori_loop(low, high, one, 0)


def stage_last(
    e2, r1, r2, gains, hidden, q, ctx, b_low, units, cos, sin, gains_one, master, one, two,
    slots_one, p, both, kv, w_gu, w_down, w_out, w_qkv, zn, rows_slot, share,
):
    rows = e2.shape[0]
    cols = kv.shape[0]
    ndev = zn * 8
    per_layer = ndev // 2
    half_zn = zn // 2
    step = chunk_rows(rows_slot)
    turns = rows_slot // step
    middle = split_slot(share)
    static, room, table = Reduce.plan(zn, rows_slot)
    steps = len(table)

    def body(
        e2_ref, r1_ref, r2_ref, g_ref, h_ref, q_ref, ctx_ref, b_ref, units_ref, c_ref, s_ref, g1_ref,
        m_ref, one_ref, two_ref,
        s1_any, p_any, both_any, kv_any, gu_any, dn_any, wo_any, wq_any,
        ig_ref, nm_ref, n1_ref, n2_ref, gn_ref, gg_ref, s0_any,
        p_ref, both_ref, kv_ref, gu_ref, dn_ref, wo_ref, wq_ref, load_sem,
        eboth_ref, ef_ref, ea_ref, ectx_ref, eq_ref, ekv_ref, lin_ref,
        flat, ring, stage, esem,
        acc, rc, first_buf, second_buf, rz, fin, sq, sqs,
        send, recv, lsem, ssem, rsem, free,
        dkv_ref, from_c, pair, from_y, ksend, krecv,
    ):
        z, x, y, c = coords()
        me = ((z * 2 + x) * 2 + y) * 2 + c
        bar = pltpu.get_barrier_semaphore()

        def peer(d):
            tgt = lax.rem(me + d, ndev)
            return {"dp": lax.div(tgt, 4), "sp": lax.rem(tgt, 4)}

        def hello(d, carry):
            pl.semaphore_signal(bar, inc=1, device_id=peer(d), device_id_type=MESH)
            return carry

        lax.fori_loop(1, ndev, hello, 0)
        loads = Loads(
            [
                (gu_any, gu_ref), (dn_any, dn_ref), (both_any, both_ref), (wo_any, wo_ref),
                (kv_any, kv_ref), (p_any, p_ref), (wq_any, wq_ref),
            ],
            load_sem,
        )
        bufs = (acc, rc, first_buf, second_buf, rz)
        stream = Reduce(s0_any, s1_any, bufs, fin, send, recv, lsem, free, zn, rows_slot)
        total = KeySum(dkv_ref, ekv_ref, from_c, pair, from_y, ksend, krecv)
        pl.semaphore_wait(bar, ndev - 1)
        stream.begin()
        done = [0]

        def pump(until):
            if until > done[0]:
                stream.pump(done[0], until)
                done[0] = until

        first_limit = stream.limit(half_zn - 1)
        second_limit = stream.limit((middle + 7) // 8 - 1)

        def ahead(part):
            pump(min(int(first_limit * part), first_limit))

        r2 = r2_ref[...]
        er2, gain2 = norm_back(e2_ref[...], r2, norm_factor(r2), g_ref[1:2, :])
        sq[12:16, :] = gain2.reshape(4, LANES)
        sq[16:24, :] = g1_ref[...].reshape(8, LANES)
        ef_ref[...] = er2.astype(bf16)
        loads.wait(0, 1, 2)
        ahead(0.1)
        e_first = er2 + feed_back(ef_ref[...], gu_ref, dn_ref, both_ref, eboth_ref)
        ahead(0.25)
        r1 = r1_ref[...]
        er1, gain1 = norm_back(e_first, r1, norm_factor(r1), g_ref[0:1, :])
        sq[8:12, :] = gain1.reshape(4, LANES)
        ig_ref[...] = er1
        ea_ref[...] = er1.astype(bf16)
        for t in range(TILES):
            grad_gate_up(flat, ring, t, b_ref[...], eboth_ref)
            if t % 3 == 2:
                ahead(0.25 + 0.15 * (t // 3 + 1))
        grad_down(flat, units_ref[...], ef_ref[...])
        grad_gains(flat, gain1, gain2)
        ahead(0.8)
        emit_slots(flat, BASE_GU, stage, s0_any, esem, rows_slot, share, middle, per_layer)
        loads.wait(3, 4, 5)
        ectx_ref[...] = mm_nt(ea_ref[...], wo_ref[...]).astype(bf16)
        pump(first_limit)
        pairs = HEADS // 2
        for i in range(pairs):
            attend_back(i, q_ref, kv_ref, p_ref, ectx_ref, eq_ref, dkv_ref)
            total.start(i)
            if i >= 1:
                total.middle(i - 1)
            pump(first_limit + (second_limit - first_limit) * (i + 1) // (2 * pairs))
        total.middle(pairs - 1)
        carry_edge(flat, rows_slot)
        grad_out(flat, ctx_ref[...], ea_ref[...])
        for i in range(pairs):
            total.end(i)
        pump(first_limit + (second_limit - first_limit) * 3 // 4)
        lin_grads(eq_ref, ekv_ref, c_ref, s_ref, lin_ref)
        grad_qkv(flat, h_ref[...], lin_ref)
        emit_slots(flat, 0, stage, s0_any, esem, rows_slot, share, 0, middle)
        pump(second_limit + 2)
        loads.wait(6)
        ig_ref[...] = ig_ref[...] + mm_nt(lin_ref[...], wq_ref[...])
        pump(stream.turns)

        fin[pl.ds(rows_slot, 8), :] = jnp.zeros((8, LANES), f32)
        shift = lax.rem(share * me, LANES)
        back = lax.rem(LANES - shift, LANES)
        lane = lax.broadcasted_iota(jnp.int32, (step, LANES), 1)
        row = lax.broadcasted_iota(jnp.int32, (step, LANES), 0)

        def realign(i, carry):
            now = pltpu.roll(fin[pl.ds(i * step, step), :], back, 1)
            after = pltpu.roll(fin[pl.ds(i * step + 1, step), :], back, 1)
            value = jnp.where(lane < LANES - shift, now, after)
            value = jnp.where((row + i * step) * LANES + lane < share, value, 0.0)
            n1_ref[pl.ds(i * step, step), :] = value
            square = value * value
            return carry + jnp.sum(square.reshape(step // 8, 8, LANES), axis=0)

        sq[0:8, :] = lax.fori_loop(0, turns, realign, jnp.zeros((8, LANES), f32))

        def tell(d, carry):
            remote(sq, sqs.at[me], ssem, rsem, peer(d)).start()
            return carry

        lax.fori_loop(1, ndev, tell, 0)
        sqs[me] = sq[...]
        total.sent()
        part = sqs.at[pl.ds(0, ndev - 1)]
        both = remote(part, part, ssem, rsem, stream.to_c)
        both.wait_send()
        both.wait_recv()
        sums = lax.fori_loop(1, ndev, lambda i, s: s + sqs[i], sqs[0])
        gg_ref[...] = sums[8:24, :]
        squares = sums[0:8, :]
        norm = jnp.sqrt(jnp.sum(squares, keepdims=True))
        gn_ref[...] = jnp.broadcast_to(norm, (8, LANES))
        scale = jnp.minimum(1.0, 1.0 / norm)
        correction = 1.0 - 0.5**STEP

        def update(i, carry):
            span = pl.ds(pl.multiple_of(i * step, 16), step)
            clipped = n1_ref[span, :] * scale
            new_one = 0.5 * one_ref[span, :] + 0.5 * clipped
            new_two = 0.5 * two_ref[span, :] + 0.5 * clipped * clipped
            n1_ref[span, :] = new_one
            n2_ref[span, :] = new_two
            nm_ref[span, :] = m_ref[pl.ds(8 + i * step, step), :] * (
                1.0 - LEARN_RATE * DECAY_RATE
            ) - LEARN_RATE * (new_one / correction) / (jnp.sqrt(new_two / correction) + ADAM_EPS)
            return carry

        lax.fori_loop(0, turns, update, 0)

    slot_flat = ((rows_slot, LANES), f32)
    outs = [
        ((rows, D), f32),
        slot_flat,
        slot_flat,
        slot_flat,
        ((8, LANES), f32),
        ((16, LANES), f32),
        ((per_layer // 8, 2, 2, 2, rows_slot, LANES), bf16),
    ]
    small = [e2, r1, r2, gains, hidden, q, ctx, b_low, units, cos, sin, gains_one, master, one, two]
    large = [slots_one, p, both, kv, w_gu, w_down, w_out, w_qkv]
    act = pltpu.VMEM((rows, D), bf16)
    return pl.pallas_call(
        body,
        out_shape=[jax.ShapeDtypeStruct(s, d) for s, d in outs],
        in_specs=[vmem_spec()] * len(small) + [any_spec()] * len(large),
        out_specs=[vmem_spec()] * 6 + [any_spec()],
        scratch_shapes=[
            pltpu.VMEM(p.shape, bf16),
            pltpu.VMEM(both.shape, f32),
            pltpu.VMEM(kv.shape, bf16),
            pltpu.VMEM(w_gu.shape, bf16),
            pltpu.VMEM(w_down.shape, bf16),
            pltpu.VMEM(w_out.shape, bf16),
            pltpu.VMEM(w_qkv.shape, bf16),
            pltpu.SemaphoreType.DMA((7,)),
            pltpu.VMEM((rows, 2 * FFP), bf16),
            act,
            act,
            act,
            act,
            pltpu.VMEM((rows, 2 * D), bf16),
            pltpu.VMEM((rows, 3 * D), bf16),
            pltpu.VMEM((flat_rows(rows_slot), LANES), f32),
            pltpu.VMEM((6, D, LANES), f32),
            pltpu.VMEM((2, rows_slot, LANES), bf16),
            pltpu.SemaphoreType.DMA((2,)),
            pltpu.VMEM((room, 2, 2, rows_slot, LANES), bf16),
            pltpu.VMEM((room, 2, 2, rows_slot, LANES), bf16),
            pltpu.VMEM((room, 2, rows_slot, LANES), bf16),
            pltpu.VMEM((room, rows_slot, LANES), bf16),
            pltpu.VMEM((room, 2, rows_slot, LANES), bf16),
            pltpu.VMEM((rows_slot + 8, LANES), f32),
            pltpu.VMEM((24, LANES), f32),
            pltpu.VMEM((ndev, 24, LANES), f32),
            pltpu.SemaphoreType.DMA((steps, 6)),
            pltpu.SemaphoreType.DMA((steps, 7)),
            pltpu.SemaphoreType.DMA((steps,)),
            pltpu.SemaphoreType.DMA,
            pltpu.SemaphoreType.DMA,
            pltpu.SemaphoreType.REGULAR((room,)),
        ]
        + key_sum_scratch(rows),
        compiler_params=pltpu.CompilerParams(
            collective_id=4, has_side_effects=True, vmem_limit_bytes=63 * MIB
        ),
    )(*small, *large)


def rope_rows(rows):
    frequency = jnp.exp(
        -jnp.log(10000.0) * jnp.arange(HEAD_DIM // 2).astype(f32) * 2.0 / HEAD_DIM
    )
    positions = lax.axis_index("sp") * rows + jnp.arange(rows)
    angles = positions.astype(f32)[:, None] * frequency[None, :]
    cos = jnp.cos(angles)
    sin = jnp.sin(angles)
    return (
        jnp.concatenate([cos] * 4, axis=1),
        jnp.concatenate([-sin, sin, -sin, sin], axis=1),
    )


def step_shard(dp_size, sp_size, hidden_in, cotangent, lengths, master, moment_one, moment_two):
    share = master.shape[0]
    zn = dp_size // 2
    per_layer = dp_size * sp_size // 2
    rows = -(-(-(-share // LANES) + 1) // 32) * 32
    seqs, tokens, width = hidden_in.shape

    def pad(flat, lead):
        return jnp.pad(flat, (lead * LANES, rows * LANES - share)).reshape(rows + lead, LANES)

    master_pad = pad(master, 8)
    cos, sin = rope_rows(tokens)
    hidden = hidden_in.reshape(tokens, width)

    (
        g0, g1, q0, ctx0, r1, b0, units0, r2, second, a1, q1,
        wq0, wo0, wg0, wd0, wq1, wo1, wg1, wd1, kv0, kv1, p0, both0,
    ) = stage_head(lengths, master_pad, hidden, cos, sin, zn, rows, share)
    output, e2, gains_one, slots_one = stage_second(
        lengths, cotangent.reshape(tokens, width), second, q1, kv1, wo1, wg1, wd1, wq1, g1, a1,
        cos, sin, share, rows,
    )
    input_grad, new_master, new_one, new_two, norm, gains, _ = stage_last(
        e2, r1, r2, g0, hidden, q0, ctx0, b0, units0, cos, sin, gains_one,
        master_pad, pad(moment_one, 0), pad(moment_two, 0),
        slots_one, p0, both0, kv0, wg0, wd0, wo0, wq0, zn, rows, share,
    )

    def flat(value):
        return value.reshape(-1)[:share]

    new_master = flat(new_master)
    return (
        output.reshape(hidden_in.shape),
        input_grad.reshape(hidden_in.shape),
        new_master,
        flat(new_one),
        flat(new_two),
        new_master.astype(bf16),
        norm[0, 0],
        gains.reshape(2, 2, width),
    )


def solution(mesh):
    in_specs = (
        P("dp", "sp", None),
        P("dp", "sp", None),
        P("dp"),
        P(("dp", "sp")),
        P(("dp", "sp")),
        P(("dp", "sp")),
    )
    out_specs = (
        P("dp", "sp", None),
        P("dp", "sp", None),
        P(("dp", "sp")),
        P(("dp", "sp")),
        P(("dp", "sp")),
        P(("dp", "sp")),
        P(),
        P(),
    )
    body = functools.partial(step_shard, mesh.shape["dp"], mesh.shape["sp"])
    return jax.shard_map(body, mesh=mesh, in_specs=in_specs, out_specs=out_specs, check_vma=False)
```

```python
import functools

import jax
import jax.numpy as jnp
from jax import lax
from jax.experimental import pallas as pl
from jax.experimental.pallas import tpu as pltpu
from jax.sharding import PartitionSpec as P

D = 512
HEADS = 8
HEAD_DIM = 64
FF = 1368
FFP = 1408
TILES = 11
STEP = 5
NORM_EPS = 1e-06
ADAM_EPS = 1e-08
LEARN_RATE = 0.02
DECAY_RATE = 0.01
LANES = 128
LAYER_ROWS = 24616
BASE_OUT = 6144
BASE_GU = 8192
BASE_DOWN = 19136
BASE_GAINS = 24608
GU_ROW = 2 * FF
PERIOD = 171
MESH = pl.DeviceIdType.MESH
MIB = 1 << 20
f32 = jnp.float32
bf16 = jnp.bfloat16


def mm(a, b):
    return lax.dot_general(a, b, (((1,), (0,)), ((), ())), preferred_element_type=f32)


def mm_nt(a, b):
    return lax.dot_general(a, b, (((1,), (1,)), ((), ())), preferred_element_type=f32)


def mm_tn(a, b):
    return lax.dot_general(a, b, (((0,), (0,)), ((), ())), preferred_element_type=f32)


def chunk_rows(rows):
    tiles = rows // 16
    best = max(d for d in range(1, 17) if tiles % d == 0)
    return best * 16


def vmem_spec():
    return pl.BlockSpec(memory_space=pltpu.VMEM)


def any_spec():
    return pl.BlockSpec(memory_space=pl.ANY)


def local_call(body, outs, ins, scratch=(), limit=60, flops=0):
    return pl.pallas_call(
        body,
        out_shape=[jax.ShapeDtypeStruct(s, d) for s, d in outs],
        in_specs=[vmem_spec()] * len(ins),
        out_specs=[vmem_spec()] * len(outs),
        scratch_shapes=list(scratch),
        compiler_params=pltpu.CompilerParams(vmem_limit_bytes=limit * MIB),
    )(*ins)


def coords():
    dp = lax.axis_index("dp")
    sp = lax.axis_index("sp")
    return lax.div(dp, 2), lax.rem(dp, 2), lax.div(sp, 2), lax.rem(sp, 2)


def place(z, x, y, c):
    return {"dp": z * 2 + x, "sp": y * 2 + c}


def remote(src, dst, send_sem, recv_sem, device):
    return pltpu.make_async_remote_copy(
        src_ref=src,
        dst_ref=dst,
        send_sem=send_sem,
        recv_sem=recv_sem,
        device_id=device,
        device_id_type=MESH,
    )


def order_at(tau, z):
    step = lax.div(tau + 1, 2)
    return z + jnp.where(lax.rem(tau, 2) == 1, -step, step)


class Gather:
    lag = 2
    sizes = ((25, 24, 25, 24), (33, 32, 33))
    cut = 0.5

    def __init__(self, slots, send, recv, zn, rows):
        self.slots, self.send, self.recv, self.zn = slots, send, recv, zn
        self.static, self.table = self.plan(zn, rows)
        self.steps = len(self.table)
        self.turns = self.steps + 2 * self.lag
        self.z, self.x, self.y, self.c = coords()
        z, x, y, c = self.z, self.x, self.y, self.c
        self.to_x = place(z, 1 - x, y, c)
        self.to_y = place(z, x, 1 - y, c)
        self.to_c = place(z, x, y, 1 - c)
        self.ahead = z >= zn // 2

    @classmethod
    def plan(cls, zn, rows):
        if rows // 16 != 98:
            return False, [(zp, 0, rows, rows // 32 * 16) for zp in range(zn)]
        table = []
        for zp in range(zn):
            base = 0
            for tiles in cls.sizes[min(zp, len(cls.sizes) - 1)]:
                table.append((zp, base, 16 * tiles, 16 * round(tiles * cls.cut)))
                base += 16 * tiles
        return True, table

    def first(self, zp):
        return min(k for k in range(self.steps) if self.table[k][0] == zp)

    def until(self, zp):
        return self.first(zp) + 2 * self.lag if zp < self.zn else self.turns

    def at(self, k):
        return self.table[k] if self.static else (k,) + self.table[0][1:]

    def ref(self, k, xp, yp, part=None):
        zp, base, size, half = self.at(k)
        if part == 0:
            size = half
        if part == 1:
            base, size = base + half, size - half
        return self.slots.at[zp, self.c, xp * 2 + yp, pl.ds(base, size)]

    def cp(self, ref, k, s, r, device):
        return remote(ref, ref, self.send.at[k, s], self.recv.at[k, r], device)

    def right(self, k):
        return self.cp(self.ref(k, self.x, self.y), k, 0, 0, place(self.z + 1, self.x, self.y, self.c))

    def left(self, k):
        return self.cp(self.ref(k, self.x, self.y), k, 1, 0, place(self.z - 1, self.x, self.y, self.c))

    def over_x(self, k):
        return self.cp(self.ref(k, self.x, self.y), k, 2, 1, self.to_x)

    def over_y(self, k):
        return self.cp(self.ref(k, self.x, self.y), k, 3, 2, self.to_y)

    def upper(self, k):
        return self.cp(self.ref(k, 1 - self.x, self.y, 0), k, 4, 3, self.to_y)

    def lower(self, k):
        return self.cp(self.ref(k, self.x, 1 - self.y, 1), k, 5, 4, self.to_x)

    def over_c(self, k, c):
        zp, base, size, half = self.at(k)
        return self.cp(self.slots.at[zp, c, :, pl.ds(base, size)], k, 6, 5, self.to_c)

    def arrival(self, ref, k, r):
        self.cp(ref, k, 0, r, self.to_c).wait_recv()

    def onward(self, k):
        zp, z = self.at(k)[0], self.z
        pl.when((zp <= z) & (z < self.zn - 1))(lambda: self.right(k).start())
        pl.when((zp >= z) & (z > 0))(lambda: self.left(k).start())

    def across(self, k):
        self.over_x(k).start()
        self.over_y(k).start()

    def begin(self):
        def own(k):
            self.onward(k)
            self.across(k)

        if self.static:
            for k in range(self.first(self.zn // 2), self.steps):
                pl.when(self.z == self.at(k)[0])(functools.partial(own, k))
        else:
            pl.when(self.ahead)(lambda: own(self.z))

    def guard(self, k, act):
        if isinstance(k, int):
            if 0 <= k < self.steps:
                act()
        else:
            pl.when((k >= 0) & (k < self.steps))(act)

    def turn(self, k):
        z, x, y = self.z, self.x, self.y

        def come():
            zp = self.at(k)[0]

            @pl.when((zp != z) | (z < self.zn // 2))
            def _():
                pl.when(zp != z)(lambda: self.arrival(self.ref(k, x, y), k, 0))
                self.onward(k)
                self.across(k)

        def go_on():
            q = k - self.lag
            self.arrival(self.ref(q, 1 - x, y), q, 1)
            self.upper(q).start()
            self.arrival(self.ref(q, x, 1 - y), q, 2)
            self.lower(q).start()

        def share():
            r = k - 2 * self.lag
            self.arrival(self.ref(r, 1 - x, 1 - y, 0), r, 3)
            self.arrival(self.ref(r, 1 - x, 1 - y, 1), r, 4)
            self.over_c(r, self.c).start()

        self.guard(k, come)
        self.guard(k - self.lag, go_on)
        self.guard(k - 2 * self.lag, share)

    def loop(self, low, high, act):
        if self.static:
            for k in range(low, high):
                act(k)
        elif high > low:

            def one(k, carry):
                act(k)
                return carry

            lax.fori_loop(low, high, one, 0)

    def pump(self, low, high):
        self.loop(low, high, self.turn)

    def arrived(self, low, high):
        end = self.first(high) if high < self.zn else self.steps
        self.loop(self.first(low), end, lambda k: self.over_c(k, 1 - self.c).wait_recv())

    def sent(self):
        def one(k):
            zp, z = self.at(k)[0], self.z
            pl.when((zp <= z) & (z < self.zn - 1))(lambda: self.right(k).wait_send())
            pl.when((zp >= z) & (z > 0))(lambda: self.left(k).wait_send())
            for item in (self.over_x(k), self.over_y(k), self.upper(k), self.lower(k)):
                item.wait_send()
            self.over_c(k, self.c).wait_send()

        self.loop(0, self.steps, one)


class KeyExchange:
    def __init__(self, kv_ref, all_ref, send, recv, lsem, parts):
        z, x, y, c = coords()
        rows = kv_ref.shape[0]
        piece = rows // parts
        to_y = place(z, x, 1 - y, c)
        to_c = place(z, x, y, 1 - c)
        mine = y * 2 + c
        beyond = (1 - y) * 2 + c
        self.parts = parts

        def part(row, k):
            return all_ref.at[pl.ds(pl.multiple_of(row * rows, rows) + k * piece, piece)]

        self.keep = pltpu.make_async_copy(
            kv_ref, all_ref.at[pl.ds(pl.multiple_of(mine * rows, rows), rows)], lsem
        )
        self.own_y, self.own_c, self.pass_c = [], [], []
        for k in range(parts):
            src, dst = kv_ref.at[pl.ds(k * piece, piece)], part(mine, k)
            self.own_y.append(remote(src, dst, send.at[0, k], recv.at[0, k], to_y))
            self.own_c.append(remote(src, dst, send.at[1, k], recv.at[1, k], to_c))
            ref = part(beyond, k)
            self.pass_c.append(remote(ref, ref, send.at[2, k], recv.at[2, k], to_c))

    def start(self):
        self.keep.start()
        for item in self.own_y + self.own_c:
            item.start()

    def forward(self, *parts):
        for k in parts:
            self.own_y[k].wait_recv()
            self.pass_c[k].start()

    def finish(self):
        for k in range(self.parts):
            self.own_c[k].wait_recv()
            self.pass_c[k].wait_recv()
        for item in self.own_y + self.own_c + self.pass_c:
            item.wait_send()
        self.keep.wait()


REGIONS = {"qkv": (0, BASE_OUT), "out": (BASE_OUT, BASE_GU), "gu": (BASE_GU, BASE_DOWN), "down": (BASE_DOWN, LAYER_ROWS)}
GROUPS = ((0, 6), (6, TILES))


def fill_flat(slots, flat, layer, name, rows, share):
    low, high = REGIONS[name]
    step = chunk_rows(rows)
    per_layer = LAYER_ROWS * LANES // share

    def one(i, carry):
        start = lax.div(share * i, LANES) - low + rows
        shift = lax.rem(share * i, LANES)
        index = i + layer * per_layer
        z, x = lax.div(index, 8), lax.rem(lax.div(index, 4), 2)
        y, c = lax.rem(lax.div(index, 2), 2), lax.rem(index, 2)
        edge = flat[pl.ds(start, 1), :]

        def fill(j, inner):
            flat[pl.ds(start + j * step, step), :] = slots[
                z, c, x * 2 + y, pl.ds(j * step, step), :
            ].astype(f32)
            return inner

        lax.fori_loop(0, rows // step, fill, 0)

        @pl.when(shift > 0)
        def _():
            flat[pl.ds(start, 1), :] = flat[pl.ds(start, 1), :] + edge

        return carry

    lax.fori_loop(low * LANES // share, (high * LANES - 1) // share + 1, one, 0)


def take_qkv(flat, top, qkv_ref):
    for col in range(12):
        qkv_ref[:, 128 * col : 128 * col + 128] = flat[pl.ds(top + col, D, stride=12), :].astype(bf16)


def take_out(flat, top, out_ref):
    for col in range(4):
        span = slice(128 * col, 128 * col + 128)
        out_ref[:, span] = flat[pl.ds(top + col, D, stride=4), :].astype(bf16)


def take_down(flat, top, down_ref, gains_ref):
    base = top + BASE_GAINS - BASE_DOWN
    for col in range(4):
        span = slice(128 * col, 128 * col + 128)
        down_ref[0:FF, span] = flat[pl.ds(top + col, FF, stride=4), :].astype(bf16)
        gains_ref[:, span] = flat[pl.ds(base + col, 2, stride=4), :]
    down_ref[FF:FFP, :] = jnp.zeros((FFP - FF, D), bf16)


def take_gate_up(flat, top, gate_up, gu_ref, group):
    lane = lax.broadcasted_iota(jnp.int32, (64, LANES), 1)
    low, high = group
    for r in range(8):
        for part in range(2):
            for tile in range(low, high):
                first = GU_ROW * r + FF * part + LANES * tile
                q, s = first // LANES, first % LANES
                value = flat[pl.ds(top + q, 64, stride=PERIOD), :]
                if s:
                    after = flat[pl.ds(top + q + 1, 64, stride=PERIOD), :]
                    value = jnp.where(
                        lane < LANES - s,
                        pltpu.roll(value, LANES - s, 1),
                        pltpu.roll(after, LANES - s, 1),
                    )
                if tile == TILES - 1:
                    value = jnp.where(lane < FF - LANES * tile, value, 0.0)
                gate_up[2 * (tile - low) + part, pl.ds(r, 64, stride=8), :] = value
    for k in range(2 * (high - low)):
        span = slice(256 * low + 128 * k, 256 * low + 128 * k + 128)
        gu_ref[:, span] = gate_up[k].astype(bf16)


def gate_up_segments(q):
    pieces = []
    place_now = LANES * q
    end = place_now + LANES
    while place_now < end:
        r, within = divmod(place_now, GU_ROW)
        part, unit = divmod(within, FF)
        tile, lane_src = divmod(unit, LANES)
        room = min(end - place_now, FF - unit, LANES - lane_src)
        lane_dst = place_now - LANES * q
        pieces.append((r, 2 * tile + part, lane_dst, lane_dst + room, (lane_dst - lane_src) % LANES))
        place_now += room
    return pieces


def gate_up_rows(tile):
    out = []
    for q in range(PERIOD):
        pieces = gate_up_segments(q)
        if max(k // 2 for _, k, _, _, _ in pieces) == tile:
            out.append((q, pieces))
    return out


def grad_qkv(flat, a_low, lin_ref):
    for t in range(6):
        value = mm_tn(a_low, lin_ref[:, 256 * t : 256 * t + 256])
        for k in range(2):
            flat[pl.ds(2 * t + k, D, stride=12), :] = value[:, 128 * k : 128 * k + 128]


def grad_out(flat, ctx, ea):
    for t in range(2):
        value = mm_tn(ctx, ea[:, 256 * t : 256 * t + 256])
        for k in range(2):
            flat[pl.ds(BASE_OUT + 2 * t + k, D, stride=4), :] = value[:, 128 * k : 128 * k + 128]


def grad_down(flat, units, ef):
    for t in range(2):
        value = mm_tn(units, ef[:, 256 * t : 256 * t + 256])
        for k in range(2):
            start = BASE_DOWN - BASE_GU + 2 * t + k
            flat[pl.ds(start, FF, stride=4), :] = value[0:FF, 128 * k : 128 * k + 128]


def grad_gate_up(flat, ring, t, b_low, eboth_ref):
    def at(tile):
        return 2 if tile == 0 else tile % 2

    value = mm_tn(b_low, eboth_ref[:, 256 * t : 256 * t + 256])
    for k in range(2):
        ring[2 * at(t) + k] = value[:, 128 * k : 128 * k + 128]
    lane = lax.broadcasted_iota(jnp.int32, (64, LANES), 1)
    for q, pieces in gate_up_rows(t):
        total = None
        for r, k, low, high, turn in pieces:
            piece = ring[2 * at(k // 2) + k % 2, pl.ds(r, 64, stride=8), :]
            if turn:
                piece = pltpu.roll(piece, turn, 1)
            total = piece if total is None else jnp.where(lane < low, total, piece)
        flat[pl.ds(q, 64, stride=PERIOD), :] = total


def grad_gains(flat, first, second):
    base = BASE_GAINS - BASE_GU
    for col in range(4):
        flat[pl.ds(base + col, 1), :] = first[:, 128 * col : 128 * col + 128]
        flat[pl.ds(base + 4 + col, 1), :] = second[:, 128 * col : 128 * col + 128]
    flat[LAYER_ROWS - BASE_GU :, :] = jnp.zeros((flat.shape[0] - LAYER_ROWS + BASE_GU, LANES), f32)


def flat_rows(rows):
    return LAYER_ROWS - BASE_GU + rows


def split_slot(share):
    return BASE_GU * LANES // share + 1


def carry_edge(flat, rows):
    flat[BASE_GU : BASE_GU + rows, :] = flat[0:rows, :]


def emit_slots(flat, base, stage, out_ref, sem, rows, share, low, high):
    step = chunk_rows(rows)

    def put(i):
        k = lax.rem(i, 2)
        z, x = lax.div(i, 8), lax.rem(lax.div(i, 4), 2)
        y, c = lax.rem(lax.div(i, 2), 2), lax.rem(i, 2)
        return pltpu.make_async_copy(stage.at[k], out_ref.at[z, c, x, y], sem.at[k])

    def one(i, carry):
        pl.when(i >= low + 2)(lambda: put(i - 2).wait())
        start = lax.div(share * i, LANES) - base
        k = lax.rem(i, 2)

        def fill(j, inner):
            stage[k, pl.ds(j * step, step), :] = flat[pl.ds(start + j * step, step), :].astype(bf16)
            return inner

        lax.fori_loop(0, rows // step, fill, 0)
        put(i).start()
        return carry

    lax.fori_loop(low, high, one, 0)
    put(high - 2).wait()
    put(high - 1).wait()


class KeySum:
    def __init__(self, part_ref, sum_ref, from_c, pair, from_y, send, recv):
        z, x, y, c = coords()
        self.part, self.sum_ref = part_ref, sum_ref
        self.from_c, self.pair, self.from_y = from_c, pair, from_y
        self.send, self.recv = send, recv
        self.rows = pair.shape[1]
        self.y, self.c = y, c
        self.to_y = place(z, x, 1 - y, c)
        self.to_c = place(z, x, y, 1 - c)

    def block(self, i, yp, cp):
        start = pl.multiple_of((yp * 2 + cp) * self.rows, self.rows)
        return self.part.at[i, pl.ds(start, self.rows)]

    def near(self, i, h):
        yp = self.y if h else 1 - self.y
        return remote(
            self.block(i, yp, 1 - self.c), self.from_c.at[h, i],
            self.send.at[i, h], self.recv.at[i, h], self.to_c,
        )

    def wide(self, i):
        return remote(
            self.pair.at[i], self.from_y.at[i], self.send.at[i, 2], self.recv.at[i, 2], self.to_y
        )

    def start(self, i):
        self.near(i, 0).start()
        self.near(i, 1).start()

    def middle(self, i):
        self.near(i, 0).wait_recv()
        self.pair[i] = (
            self.from_c[0, i].astype(f32) + self.block(i, 1 - self.y, self.c)[...].astype(f32)
        ).astype(bf16)
        self.wide(i).start()

    def end(self, i):
        self.near(i, 1).wait_recv()
        self.wide(i).wait_recv()
        total = (
            self.from_c[1, i].astype(f32)
            + self.block(i, self.y, self.c)[...].astype(f32)
            + self.from_y[i].astype(f32)
        ).astype(bf16)
        self.sum_ref[:, LANES * i : LANES * i + LANES] = total[:, :LANES]
        self.sum_ref[:, D + LANES * i : D + LANES * i + LANES] = total[:, LANES:]

    def sent(self):
        for i in range(HEADS // 2):
            self.near(i, 0).wait_send()
            self.near(i, 1).wait_send()
            self.wide(i).wait_send()


def key_sum_scratch(rows):
    pairs = HEADS // 2
    return [
        pltpu.VMEM((pairs, 4 * rows, 2 * LANES), bf16),
        pltpu.VMEM((2, pairs, rows, 2 * LANES), bf16),
        pltpu.VMEM((pairs, rows, 2 * LANES), bf16),
        pltpu.VMEM((pairs, rows, 2 * LANES), bf16),
        pltpu.SemaphoreType.DMA((pairs, 3)),
        pltpu.SemaphoreType.DMA((pairs, 3)),
    ]


def half_swap(u):
    lane = lax.broadcasted_iota(jnp.int32, u.shape, 1)
    return jnp.where(lax.rem(lane, 64) < 32, pltpu.roll(u, 96, 1), pltpu.roll(u, 32, 1))


def project_heads(a_low, w_ref, cos_ref, sin_ref, q_ref, kv_ref, tiles=range(6)):
    for t in tiles:
        lin = mm(a_low, w_ref[:, 256 * t : 256 * t + 256])
        for k in range(2):
            u = lin[:, 128 * k : 128 * k + 128]
            if t < 4:
                u = u * cos_ref[...] + half_swap(u) * sin_ref[...]
            col = 256 * t + 128 * k
            if col < D:
                q_ref[:, col : col + 128] = u.astype(bf16)
            else:
                kv_ref[:, col - D : col - D + 128] = u.astype(bf16)


def norm_factor(r):
    return lax.rsqrt(jnp.mean(r * r, axis=-1, keepdims=True) + NORM_EPS)


def norm_back(e, r, f, g):
    scaled = e * g
    gain = jnp.sum(e * r * f, axis=0, keepdims=True)
    grad = f * scaled - r * (f * f * f) * jnp.mean(scaled * r, axis=-1, keepdims=True)
    return grad, gain


def head_mask(rows, h):
    lane = lax.broadcasted_iota(jnp.int32, (rows, LANES), 1)
    return (lane >= 64) if h else (lane < 64)


def make_bias(bias, length):
    rows, cols = bias.shape
    first = lax.axis_index("sp") * rows
    row = lax.broadcasted_iota(jnp.int32, (rows, cols), 0) + first
    col = lax.broadcasted_iota(jnp.int32, (rows, cols), 1)
    bias[...] = jnp.where((col <= row) & (col < length), 0.0, -1e9)


def attend(i, q_ref, kv_ref, bias, p_ref, ctx_ref):
    rows = q_ref.shape[0]
    span = slice(LANES * i, LANES * i + LANES)
    keys = kv_ref[:, span]
    values = kv_ref[:, D + LANES * i : D + LANES * i + LANES]
    queries = q_ref[:, span]
    total = jnp.zeros((rows, LANES), f32)
    for h in range(2):
        qm = jnp.where(head_mask(rows, h), queries, jnp.zeros_like(queries))
        vm = jnp.where(head_mask(values.shape[0], h), values, jnp.zeros_like(values))
        logits = mm_nt(qm, keys) * HEAD_DIM ** (-0.5) + bias[...]
        top = jnp.max(logits, axis=-1, keepdims=True)
        soft = jnp.exp(logits - top)
        norm = 1.0 / jnp.sum(soft, axis=-1, keepdims=True)
        low = (soft * norm).astype(bf16)
        p_ref[2 * i + h] = low
        total = total + mm(low, vm)
    ctx_ref[:, span] = total.astype(bf16)


def attend_back(i, q_ref, kv_ref, p_ref, ectx_ref, eq_ref, dkv_ref):
    rows = q_ref.shape[0]
    cols = kv_ref.shape[0]
    span = slice(LANES * i, LANES * i + LANES)
    keys = kv_ref[:, span]
    values = kv_ref[:, D + LANES * i : D + LANES * i + LANES]
    queries = q_ref[:, span]
    grads = ectx_ref[:, span]
    dq = jnp.zeros((rows, LANES), f32)
    dk = jnp.zeros((LANES, cols), f32)
    dv = jnp.zeros((LANES, cols), f32)
    for h in range(2):
        mask = head_mask(rows, h)
        qm = jnp.where(mask, queries, jnp.zeros_like(queries))
        em = jnp.where(mask, grads, jnp.zeros_like(grads))
        km = jnp.where(head_mask(cols, h), keys, jnp.zeros_like(keys))
        low = p_ref[2 * i + h]
        soft = low.astype(f32)
        dp = mm_nt(em, values)
        center = jnp.sum(soft * dp, axis=-1, keepdims=True)
        raw = (soft * (dp - center) * HEAD_DIM ** (-0.5)).astype(bf16)
        dv = dv + mm_tn(em, low)
        dk = dk + mm_tn(qm, raw)
        dq = dq + mm(raw, km)
    eq_ref[:, span] = dq.astype(bf16)
    dkv_ref[i, :, :LANES] = dk.T.astype(bf16)
    dkv_ref[i, :, LANES:] = dv.T.astype(bf16)


def feed_forward(b_low, gu_ref, down_ref, both_ref, units_ref):
    for t in range(TILES):
        both = mm(b_low, gu_ref[:, 256 * t : 256 * t + 256])
        both_ref[:, 256 * t : 256 * t + 256] = both
        gate, up = both[:, :128], both[:, 128:]
        units_ref[:, 128 * t : 128 * t + 128] = (gate / (1.0 + jnp.exp(-gate)) * up).astype(bf16)
    return mm(units_ref[...], down_ref[...])


def feed_back(e_low, gu_ref, down_ref, both_ref, eboth_ref, pump=None):
    for t in range(TILES):
        if pump is not None and t % 4 == 3:
            pump()
        eu = mm_nt(e_low, down_ref[128 * t : 128 * t + 128, :])
        gate = both_ref[:, 256 * t : 256 * t + 128]
        up = both_ref[:, 256 * t + 128 : 256 * t + 256]
        sig = 1.0 / (1.0 + jnp.exp(-gate))
        eboth_ref[:, 256 * t : 256 * t + 128] = (eu * up * sig * (1.0 + gate * (1.0 - sig))).astype(bf16)
        eboth_ref[:, 256 * t + 128 : 256 * t + 256] = (eu * gate * sig).astype(bf16)
    return mm_nt(eboth_ref[...], gu_ref[...])


def stage_head(length, master_pad, hidden, cos, sin, zn, rows_slot, share):
    rows = hidden.shape[0]
    cols = 4 * rows
    step = chunk_rows(rows_slot)
    half_zn = zn // 2
    ndev = zn * 8
    gains_row = BASE_GAINS - share * (ndev // 2 - 1) // LANES
    first_zp = -(-BASE_OUT * LANES // (8 * share))
    parts = 4
    gather_steps = len(Gather.plan(zn, rows_slot)[1])
    top = rows_slot

    def body(
        l_ref, x_ref, h_ref, c_ref, s_ref,
        g0, g1, q0, ctx_ref, r1_ref, b_ref, units_ref, r2_ref, sec_ref, a1_ref, q1,
        wq0_any, wo0_any, wg0_any, wd0_any, wq1_any, wo1_any, wg1_any, wd1_any,
        kv0_any, kv1_any, p_any, both_any,
        wq0, wo0, wg0, wd0, wq1, wo1, wg1, wd1, all0, all1, p_ref, both_ref,
        slots, flat, gate_up, kv0, kv1, bias, send, recv,
        ksend0, krecv0, ksend1, krecv1, lsem, osem, gains_out, gains_in, gsend, grecv,
    ):
        z, x, y, c = coords()
        bar = pltpu.get_barrier_semaphore()

        def hello(device):
            pl.semaphore_signal(bar, inc=1, device_id=device, device_id_type=MESH)

        hello(place(z, 1 - x, y, c))
        hello(place(z, x, 1 - y, c))
        hello(place(z, x, y, 1 - c))
        pl.when(z > 0)(lambda: hello(place(z - 1, x, y, c)))
        pl.when(z < zn - 1)(lambda: hello(place(z + 1, x, y, c)))
        me = ((z * 2 + x) * 2 + y) * 2 + c
        owner = me == ndev - 1
        pl.when(me != ndev - 1)(lambda: hello(place(zn - 1, 1, 1, 1)))

        shift = lax.rem(share * (((z * 2 + x) * 2 + y) * 2 + c), LANES)
        lane = lax.broadcasted_iota(jnp.int32, (step, LANES), 1)

        def align(i, carry):
            now = pltpu.roll(x_ref[pl.ds(8 + i * step, step), :], shift, 1)
            before = pltpu.roll(x_ref[pl.ds(7 + i * step, step), :], shift, 1)
            slots[z, c, x * 2 + y, pl.ds(i * step, step), :] = jnp.where(
                lane >= shift, now, before
            ).astype(bf16)
            return carry

        lax.fori_loop(0, rows_slot // step, align, 0)
        now = pltpu.roll(x_ref[pl.ds(8 + gains_row, 8), :], shift, 1)
        before = pltpu.roll(x_ref[pl.ds(7 + gains_row, 8), :], shift, 1)
        gains_out[...] = jnp.zeros((16, LANES), bf16)
        gains_out[0:8, :] = jnp.where(lane[0:8] >= shift, now, before).astype(bf16)
        pl.semaphore_wait(
            bar,
            3
            + (z > 0).astype(jnp.int32)
            + (z < zn - 1).astype(jnp.int32)
            + owner.astype(jnp.int32) * (ndev - 1),
        )

        def tell_gains(d):
            device = {"dp": lax.div(d, 4), "sp": lax.rem(d, 4)}
            return remote(gains_out, gains_in, gsend.at[d], grecv, device)

        @pl.when(owner)
        def _():
            def go(d, carry):
                tell_gains(d).start()
                return carry

            lax.fori_loop(0, ndev - 1, go, 0)
            gains_in[...] = gains_out[...]

        gather = Gather(slots, send, recv, zn, rows_slot)
        done = [0]

        def pump(until):
            gather.pump(done[0], until)
            done[0] = max(done[0], until)

        def between(low, high, k, n):
            pump(low + (high - low) * k // n)

        saves = [
            pltpu.make_async_copy(src, dst, osem.at[i])
            for i, (src, dst) in enumerate(
                [
                    (wq0, wq0_any), (wo0, wo0_any), (wg0, wg0_any), (wd0, wd0_any),
                    (wq1, wq1_any), (wo1, wo1_any), (wg1, wg1_any), (wd1, wd1_any),
                    (all0, kv0_any), (all1, kv1_any), (p_ref, p_any), (both_ref, both_any),
                ]
            )
        ]

        def fill(layer, name):
            fill_flat(slots, flat, layer, name, rows_slot, share)

        gather.begin()
        make_bias(bias, l_ref[0])
        pump(gather.until(first_zp))
        gather.arrived(0, first_zp)
        fill(0, "qkv")
        take_qkv(flat, top, wq0)
        exchange0 = KeyExchange(kv0, all0, ksend0, krecv0, lsem.at[0], parts)
        project_heads(h_ref[...], wq0, c_ref, s_ref, q0, kv0, range(2, 6))
        exchange0.start()
        saves[0].start()
        low, high = gather.until(first_zp), gather.until(half_zn)
        between(low, high, 1, 2)
        project_heads(h_ref[...], wq0, c_ref, s_ref, q0, kv0, range(2))
        exchange0.forward(0, 1, 2, 3)
        pump(high)
        exchange0.finish()
        saves[8].start()
        low, high = high, gather.until(half_zn + first_zp)
        for i in range(HEADS // 2):
            attend(i, q0, all0, bias, p_ref, ctx_ref)
            if i == 1:
                between(low, high, 1, 2)
        saves[10].start()
        gather.arrived(first_zp, half_zn)
        fill(0, "out")
        take_out(flat, top, wo0)
        saves[1].start()
        fill(0, "down")
        take_down(flat, top, wd0, g0)
        saves[3].start()
        pump(high)
        fill(0, "gu")
        for group in GROUPS:
            take_gate_up(flat, top, gate_up, wg0, group)
        saves[2].start()
        low, high = high, gather.until(zn)
        between(low, high, 1, 3)
        r1 = h_ref[...].astype(f32) + mm(ctx_ref[...], wo0[...])
        r1_ref[...] = r1
        first = r1 * norm_factor(r1) * g0[0:1, :]
        b_ref[...] = first.astype(bf16)
        r2 = first + feed_forward(b_ref[...], wg0, wd0, both_ref, units_ref)
        saves[11].start()
        r2_ref[...] = r2
        second = r2 * norm_factor(r2) * g0[1:2, :]
        sec_ref[...] = second
        between(low, high, 2, 3)
        gather.arrived(half_zn, half_zn + first_zp)
        fill(1, "qkv")
        take_qkv(flat, top, wq1)
        saves[4].start()

        @pl.when(me != ndev - 1)
        def _():
            tell_gains(0).wait_recv()

        known = gains_in[...].astype(f32)
        for col in range(4):
            span = slice(LANES * col, LANES * col + LANES)
            g1[0:1, span] = known[col : col + 1, :]
            g1[1:2, span] = known[4 + col : 5 + col, :]
        a1_ref[...] = (second * norm_factor(second) * g1[0:1, :]).astype(bf16)
        exchange1 = KeyExchange(kv1, all1, ksend1, krecv1, lsem.at[1], parts)
        project_heads(a1_ref[...], wq1, c_ref, s_ref, q1, kv1, range(2, 6))
        exchange1.start()
        project_heads(a1_ref[...], wq1, c_ref, s_ref, q1, kv1, range(2))
        pump(high)
        gather.arrived(half_zn + first_zp, zn)
        fill(1, "down")
        take_down(flat, top, wd1, g1)
        saves[7].start()
        fill(1, "out")
        take_out(flat, top, wo1)
        saves[5].start()
        fill(1, "gu")
        take_gate_up(flat, top, gate_up, wg1, GROUPS[0])
        exchange1.forward(0, 1, 2, 3)
        take_gate_up(flat, top, gate_up, wg1, GROUPS[1])
        saves[6].start()
        exchange1.finish()
        saves[9].start()
        gather.sent()

        @pl.when(owner)
        def _():
            def wait(d, carry):
                tell_gains(d).wait_send()
                return carry

            lax.fori_loop(0, ndev - 1, wait, 0)

        for item in saves:
            item.wait()

    layer = [((D, 3 * D), bf16), ((D, D), bf16), ((D, 2 * FFP), bf16), ((FFP, D), bf16)]
    kept = layer + layer + [
        ((cols, 2 * D), bf16),
        ((cols, 2 * D), bf16),
        ((HEADS, rows, cols), bf16),
        ((rows, 2 * FFP), f32),
    ]
    low_rows, full_rows = ((rows, D), bf16), ((rows, D), f32)
    outs = [
        ((2, D), f32),
        ((2, D), f32),
        low_rows,
        low_rows,
        full_rows,
        low_rows,
        ((rows, FFP), bf16),
        full_rows,
        full_rows,
        low_rows,
        low_rows,
    ]
    ins = [length, master_pad, hidden, cos, sin]
    longest = max(high - low for low, high in REGIONS.values())
    kv_scratch = pltpu.VMEM((rows, 2 * D), bf16)
    return pl.pallas_call(
        body,
        out_shape=[jax.ShapeDtypeStruct(s, d) for s, d in outs + kept],
        in_specs=[pl.BlockSpec(memory_space=pltpu.SMEM)] + [vmem_spec()] * (len(ins) - 1),
        out_specs=[vmem_spec()] * len(outs) + [any_spec()] * len(kept),
        scratch_shapes=[pltpu.VMEM(s, d) for s, d in kept]
        + [
            pltpu.VMEM((zn, 2, 4, rows_slot, LANES), bf16),
            pltpu.VMEM((longest + 2 * rows_slot, LANES), f32),
            pltpu.VMEM((12, D, LANES), f32),
            kv_scratch,
            kv_scratch,
            pltpu.VMEM((rows, cols), f32),
            pltpu.SemaphoreType.DMA((gather_steps, 7)),
            pltpu.SemaphoreType.DMA((gather_steps, 6)),
            pltpu.SemaphoreType.DMA((3, parts)),
            pltpu.SemaphoreType.DMA((3, parts)),
            pltpu.SemaphoreType.DMA((3, parts)),
            pltpu.SemaphoreType.DMA((3, parts)),
            pltpu.SemaphoreType.DMA((2,)),
            pltpu.SemaphoreType.DMA((12,)),
            pltpu.VMEM((16, LANES), bf16),
            pltpu.VMEM((16, LANES), bf16),
            pltpu.SemaphoreType.DMA((ndev,)),
            pltpu.SemaphoreType.DMA,
        ],
        compiler_params=pltpu.CompilerParams(
            collective_id=1, has_side_effects=True, vmem_limit_bytes=62 * MIB
        ),
    )(*ins)


class Loads:
    def __init__(self, pairs, sem):
        self.items = [pltpu.make_async_copy(src, dst, sem.at[i]) for i, (src, dst) in enumerate(pairs)]
        for item in self.items:
            item.start()

    def wait(self, *which):
        for i in which:
            self.items[i].wait()


def meet(devices):
    bar = pltpu.get_barrier_semaphore()
    for device in devices:
        pl.semaphore_signal(bar, inc=1, device_id=device, device_id_type=MESH)
    pl.semaphore_wait(bar, len(devices))


def stage_second(
    length, cotangent, second, q, kv, w_out, w_gu, w_down, w_qkv, gains, a1, cos, sin, share, rows_slot
):
    rows = q.shape[0]
    cols = kv.shape[0]
    per_layer = LAYER_ROWS * LANES // share
    middle = split_slot(share)

    def body(
        l_ref, cot_ref, sec_ref, q_ref, g_ref, a_ref, c_ref, s_ref, kv_any, wo_any, gu_any, dn_any, wq_any,
        o_ref, e2_ref, gg_ref, slots_ref,
        kv_ref, wo_ref, gu_ref, dn_ref, wq_ref, lsem, eq_ref, lin_ref,
        bias, p_ref, ctx_ref, b_ref, both_ref, units_ref, eboth_ref, ef_ref, ea_ref, ectx_ref,
        ekv_ref, flat, ring, stage, esem,
        dkv_ref, from_c, pair, from_y, send, recv,
    ):
        loads = Loads(
            [
                (kv_any, kv_ref), (wo_any, wo_ref), (gu_any, gu_ref), (dn_any, dn_ref), (wq_any, wq_ref)
            ],
            lsem,
        )
        z, x, y, c = coords()
        meet([place(z, x, 1 - y, c), place(z, x, y, 1 - c)])
        total = KeySum(dkv_ref, ekv_ref, from_c, pair, from_y, send, recv)
        length_now = l_ref[0]
        make_bias(bias, length_now)
        loads.wait(0)
        for i in range(HEADS // 2):
            attend(i, q_ref, kv_ref, bias, p_ref, ctx_ref)
        loads.wait(1, 2, 3)
        third = sec_ref[...] + mm(ctx_ref[...], wo_ref[...])
        f4 = norm_factor(third)
        b_ref[...] = (third * f4 * g_ref[1:2, :]).astype(bf16)
        o_ref[...] = third + feed_forward(b_ref[...], gu_ref, dn_ref, both_ref, units_ref)
        place_now = lax.broadcasted_iota(jnp.int32, (rows, D), 0) + lax.axis_index("sp") * rows
        e_out = jnp.where(place_now < length_now, cot_ref[...], 0.0)
        ef_ref[...] = e_out.astype(bf16)
        e_b = feed_back(ef_ref[...], gu_ref, dn_ref, both_ref, eboth_ref)
        grad, gain = norm_back(e_b, third, f4, g_ref[1:2, :])
        gg_ref[1:2, :] = gain
        e3 = e_out + grad
        e2_ref[...] = e3
        ea_ref[...] = e3.astype(bf16)
        ectx_ref[...] = mm_nt(ea_ref[...], wo_ref[...]).astype(bf16)
        for i in range(HEADS // 2):
            attend_back(i, q_ref, kv_ref, p_ref, ectx_ref, eq_ref, dkv_ref)
            total.start(i)
            if i >= 1:
                total.middle(i - 1)
        for t in range(TILES):
            grad_gate_up(flat, ring, t, b_ref[...], eboth_ref)
            if t == 0:
                total.middle(3)
            if t in (1, 4, 7, 10):
                total.end((t - 1) // 3)
        lin_grads(eq_ref, ekv_ref, c_ref, s_ref, lin_ref)
        grad_down(flat, units_ref[...], ef_ref[...])
        loads.wait(4)
        second = sec_ref[...]
        grad, gain = norm_back(
            mm_nt(lin_ref[...], wq_ref[...]), second, norm_factor(second), g_ref[0:1, :]
        )
        gg_ref[0:1, :] = gain
        e2_ref[...] = e2_ref[...] + grad
        grad_gains(flat, gg_ref[0:1, :], gg_ref[1:2, :])
        emit_slots(flat, BASE_GU, stage, slots_ref, esem, rows_slot, share, middle, per_layer)
        carry_edge(flat, rows_slot)
        grad_out(flat, ctx_ref[...], ea_ref[...])
        grad_qkv(flat, a_ref[...], lin_ref)
        emit_slots(flat, 0, stage, slots_ref, esem, rows_slot, share, 0, middle)
        total.sent()

    outs = [
        ((rows, D), f32),
        ((rows, D), f32),
        ((2, D), f32),
        ((per_layer // 8, 2, 2, 2, rows_slot, LANES), bf16),
    ]
    ins = [length, cotangent, second, q, gains, a1, cos, sin, kv, w_out, w_gu, w_down, w_qkv]
    return pl.pallas_call(
        body,
        out_shape=[jax.ShapeDtypeStruct(s, d) for s, d in outs],
        in_specs=[pl.BlockSpec(memory_space=pltpu.SMEM)] + [vmem_spec()] * 7 + [any_spec()] * 5,
        out_specs=[vmem_spec()] * 3 + [any_spec()],
        scratch_shapes=[
            pltpu.VMEM((cols, 2 * D), bf16),
            pltpu.VMEM((D, D), bf16),
            pltpu.VMEM((D, 2 * FFP), bf16),
            pltpu.VMEM((FFP, D), bf16),
            pltpu.VMEM((D, 3 * D), bf16),
            pltpu.SemaphoreType.DMA((5,)),
            pltpu.VMEM((rows, D), bf16),
            pltpu.VMEM((rows, 3 * D), bf16),
            pltpu.VMEM((rows, cols), f32),
            pltpu.VMEM((HEADS, rows, cols), bf16),
            pltpu.VMEM((rows, D), bf16),
            pltpu.VMEM((rows, D), bf16),
            pltpu.VMEM((rows, 2 * FFP), f32),
            pltpu.VMEM((rows, FFP), bf16),
            pltpu.VMEM((rows, 2 * FFP), bf16),
            pltpu.VMEM((rows, D), bf16),
            pltpu.VMEM((rows, D), bf16),
            pltpu.VMEM((rows, D), bf16),
            pltpu.VMEM((rows, 2 * D), bf16),
            pltpu.VMEM((flat_rows(rows_slot), LANES), f32),
            pltpu.VMEM((6, D, LANES), f32),
            pltpu.VMEM((2, rows_slot, LANES), bf16),
            pltpu.SemaphoreType.DMA((2,)),
        ]
        + key_sum_scratch(rows),
        compiler_params=pltpu.CompilerParams(
            collective_id=3, has_side_effects=True, vmem_limit_bytes=60 * MIB
        ),
    )(*ins)


def lin_grads(eq_ref, ekv_ref, cos_ref, sin_ref, lin_ref):
    for t in range(12):
        col = 128 * t
        src = eq_ref[:, col : col + 128] if t < 4 else ekv_ref[:, col - D : col - D + 128]
        if t < 8:
            w = src.astype(f32)
            src = (w * cos_ref[...] - half_swap(w) * sin_ref[...]).astype(bf16)
        lin_ref[:, col : col + 128] = src


def when(condition):
    if isinstance(condition, bool):
        return (lambda act: act()) if condition else (lambda act: None)
    return pl.when(condition)


class Reduce:
    room_static = 3
    lags = (1, 2, 3)

    def __init__(self, early, late, bufs, fin, send, recv, lsem, free, zn, rows, ahead=2):
        self.early, self.late, self.fin, self.free = early, late, fin, free
        self.acc, self.rc, self.first, self.second, self.rz = bufs
        self.send, self.recv, self.lsem = send, recv, lsem
        self.zn, self.half = zn, zn // 2
        self.static, self.room, self.table = self.plan(zn, rows)
        self.steps = len(self.table)
        self.ahead = ahead
        self.two, self.three, self.hop = self.lags
        self.retired = self.hop + zn - 1
        self.gap = 0 if self.static else max(0, self.retired - self.room) + ahead
        self.turns = self.steps + self.gap + self.retired + 1
        self.z, self.x, self.y, self.c = coords()
        z, x, y, c = self.z, self.x, self.y, self.c
        self.to_x = place(z, 1 - x, y, c)
        self.to_y = place(z, x, 1 - y, c)
        self.to_c = place(z, x, y, 1 - c)

    @classmethod
    def plan(cls, zn, rows):
        if rows // 16 != 98:
            chunk = (0, rows, rows // 32 * 16)
            return False, zn // 2, [(zp, chunk) for zp in range(zn - 1, -1, -1)]
        table = []
        for zp in range(zn - 1, -1, -1):
            base = 0
            for tiles in cls.sizes[min(zp, len(cls.sizes) - 1)]:
                table.append((zp, (base, 16 * tiles, 16 * round(tiles * cls.share_x))))
                base += 16 * tiles
        return True, min(cls.room_static, zn), table

    sizes = ((20, 20, 20, 19, 19), (33, 32, 33))
    share_x = 0.5

    def at(self, k):
        if self.static:
            zp, chunk = self.table[k]
            return zp, zp % self.room, chunk
        zp = self.zn - 1 - k
        return zp, lax.rem(zp, self.room), self.table[0][1]

    def ends(self, k):
        return k + 1 == self.steps or self.table[k + 1][0] != self.table[k][0]

    def opens(self, k):
        return k == 0 or self.table[k - 1][0] != self.table[k][0]

    def last_of(self, zp):
        return max(k for k in range(self.steps) if self.table[k][0] == zp)

    def step_at(self, u):
        if self.static:
            return u
        later = jnp.where(u < self.room + self.gap, -1, u - self.gap)
        return jnp.where(u < self.room, u, later)

    def starts_at(self, k):
        zp = self.table[k][0]
        turn = k - self.ahead
        if zp + self.room < self.zn:
            if not self.static:
                return k + self.gap - self.ahead
            turn = max(turn, self.last_of(zp + self.room) + self.retired)
            assert turn <= k
        return turn

    def limit(self, zp):
        return self.starts_at(min(k for k in range(self.steps) if self.table[k][0] == zp))

    def from_source(self, k, act):
        zp, loc, chunk = self.at(k)
        if isinstance(zp, int):
            act((self.late if zp >= self.half else self.early).at[zp % self.half])
        else:
            index = lax.rem(zp, self.half)
            pl.when(zp >= self.half)(lambda: act(self.late.at[index]))
            pl.when(zp < self.half)(lambda: act(self.early.at[index]))

    def cp(self, src, dst, k, s, r, device):
        return remote(src, dst, self.send.at[k, s], self.recv.at[k, r], device)

    def spans(self, k):
        zp, loc, (base, size, cut) = self.at(k)
        return pl.ds(base, cut), pl.ds(base + cut, size - cut)

    def core(self, k, src=None):
        zp, loc, (base, size, cut) = self.at(k)
        span = pl.ds(base, size)
        src = self.early.at[0] if src is None else src
        return self.cp(
            src.at[1 - self.c, :, :, span], self.rc.at[loc, :, :, span], k, 0, 0, self.to_c
        )

    def load(self, k, src=None):
        zp, loc, (base, size, cut) = self.at(k)
        span = pl.ds(base, size)
        src = self.early.at[0] if src is None else src
        return pltpu.make_async_copy(
            src.at[self.c, :, :, span], self.acc.at[loc, :, :, span], self.lsem.at[k]
        )

    def far_x(self, k):
        zp, loc, chunk = self.at(k)
        span = self.spans(k)[0]
        return self.cp(
            self.acc.at[loc, 1 - self.x, :, span], self.first.at[loc, :, span], k, 1, 1, self.to_x
        )

    def far_y(self, k):
        zp, loc, chunk = self.at(k)
        span = self.spans(k)[1]
        return self.cp(
            self.acc.at[loc, :, 1 - self.y, span], self.first.at[loc, :, span], k, 2, 2, self.to_y
        )

    def then_y(self, k):
        zp, loc, chunk = self.at(k)
        span = self.spans(k)[0]
        src = self.acc.at[loc, self.x, 1 - self.y, span]
        return self.cp(src, self.second.at[loc, span], k, 3, 3, self.to_y)

    def then_x(self, k):
        zp, loc, chunk = self.at(k)
        span = self.spans(k)[1]
        src = self.acc.at[loc, 1 - self.x, self.y, span]
        return self.cp(src, self.second.at[loc, span], k, 4, 4, self.to_x)

    def right(self, k):
        zp, loc, (base, size, cut) = self.at(k)
        span = pl.ds(base, size)
        return self.cp(
            self.acc.at[loc, self.x, self.y, span], self.rz.at[loc, 0, span], k, 5, 5,
            place(self.z + 1, self.x, self.y, self.c),
        )

    def left(self, k):
        zp, loc, (base, size, cut) = self.at(k)
        span = pl.ds(base, size)
        return self.cp(
            self.acc.at[loc, self.x, self.y, span], self.rz.at[loc, 1, span], k, 5, 6,
            place(self.z - 1, self.x, self.y, self.c),
        )

    def add(self, loc, xp, yp, span, src):
        value = self.acc[loc, xp, yp, span, :].astype(f32) + src.astype(f32)
        self.acc[loc, xp, yp, span, :] = value.astype(bf16)

    def ok(self, k):
        return (k >= 0) & (k < self.steps)

    def guard(self, k, act):
        if isinstance(k, int):
            if 0 <= k < self.steps:
                act()
        else:
            pl.when(self.ok(k))(act)

    def neighbours(self, act):
        z, x, y, c = self.z, self.x, self.y, self.c
        for device in (self.to_x, self.to_y, self.to_c):
            act(device)
        pl.when(z > 0)(lambda: act(place(z - 1, x, y, c)))
        pl.when(z < self.zn - 1)(lambda: act(place(z + 1, x, y, c)))

    def stage_core(self, k):
        def act():
            if self.static:
                if self.opens(k) and self.table[k][0] + self.room < self.zn:
                    self.claim(k)
            else:
                pl.when(k >= self.room)(lambda: self.claim(k))
            self.from_source(k, lambda src: self.core(k, src).start())
            self.from_source(k, lambda src: self.load(k, src).start())

        self.guard(k, act)

    def claim(self, k):
        z = self.z
        zp, loc, chunk = self.at(k)
        pl.semaphore_wait(
            self.free.at[loc],
            3 + (z > 0).astype(jnp.int32) + (z < self.zn - 1).astype(jnp.int32),
        )

    def retire(self, k):
        def act():
            zp, loc, chunk = self.at(k)
            for item in (
                self.core(k), self.far_x(k), self.far_y(k), self.then_x(k), self.then_y(k)
            ):
                item.wait_send()
            pl.when(zp > self.z)(lambda: self.right(k).wait_send())
            pl.when(zp < self.z)(lambda: self.left(k).wait_send())

            def tell():
                self.neighbours(
                    lambda d: pl.semaphore_signal(
                        self.free.at[loc], inc=1, device_id=d, device_id_type=MESH
                    )
                )

            if self.static:
                if self.ends(k) and zp >= self.room:
                    tell()
            else:
                pl.when(zp >= self.room)(tell)

        self.guard(k, act)

    def stage_one(self, k):
        def act():
            zp, loc, chunk = self.at(k)
            over_x, over_y = self.spans(k)
            x, y = self.x, self.y
            self.core(k).wait_recv()
            self.load(k).wait()

            def add(xp, yp, span):
                self.add(loc, xp, yp, span, self.rc[loc, xp, yp, span, :])

            add(1 - x, 0, over_x)
            add(1 - x, 1, over_x)
            self.far_x(k).start()
            add(0, 1 - y, over_y)
            add(1, 1 - y, over_y)
            self.far_y(k).start()
            add(x, 0, over_x)
            add(x, 1, over_x)
            add(0, y, over_y)
            add(1, y, over_y)

        self.guard(k, act)

    def stage_two(self, k):
        def act():
            zp, loc, chunk = self.at(k)
            over_x, over_y = self.spans(k)
            x, y = self.x, self.y

            def add(xp, yp, span, row):
                self.add(loc, xp, yp, span, self.first[loc, row, span, :])

            self.far_x(k).wait_recv()
            add(x, 1 - y, over_x, 1 - y)
            self.then_y(k).start()
            self.far_y(k).wait_recv()
            add(1 - x, y, over_y, 1 - x)
            self.then_x(k).start()
            add(x, y, over_x, y)
            add(x, y, over_y, x)

        self.guard(k, act)

    def stage_three(self, k):
        def act():
            zp, loc, (base, size, cut) = self.at(k)
            span = pl.ds(base, size)
            z, x, y = self.z, self.x, self.y
            self.then_y(k).wait_recv()
            self.then_x(k).wait_recv()

            @pl.when(zp == z)
            def _():
                self.fin[span, :] = self.acc[loc, x, y, span, :].astype(f32) + self.second[
                    loc, span, :
                ].astype(f32)

            @pl.when(zp != z)
            def _():
                self.add(loc, x, y, span, self.second[loc, span, :])

            pl.when((zp > z) & (z == 0))(lambda: self.right(k).start())
            pl.when((zp < z) & (z == self.zn - 1))(lambda: self.left(k).start())

        self.guard(k, act)

    def stage_hop(self, k, z, rightward):
        def act():
            zp, loc, (base, size, cut) = self.at(k)
            span = pl.ds(base, size)
            x, y = self.x, self.y
            item = self.right(k) if rightward else self.left(k)
            part = self.rz.at[loc, 0 if rightward else 1, span]

            onward = (zp > z) if rightward else (zp < z)

            @when(onward)
            def _():
                item.wait_recv()
                self.add(loc, x, y, span, part[...])
                item.start()

            @when(zp == z)
            def _():
                item.wait_recv()
                self.fin[span, :] = self.fin[span, :] + part[...].astype(f32)

        self.guard(k, act)

    def stage_four(self, u):
        z, last = self.z, self.zn - 1
        if not self.static:
            @pl.when(z > 0)
            def _():
                self.stage_hop(self.step_at(u - self.hop - (z - 1)), z, True)

            @pl.when(z < last)
            def _():
                self.stage_hop(self.step_at(u - self.hop - (last - z - 1)), z, False)

            return
        for place_z in range(self.zn):
            steps = []
            if place_z > 0:
                k = self.step_at(u - self.hop - (place_z - 1))
                if 0 <= k < self.steps and self.at(k)[0] >= place_z:
                    steps.append((k, True))
            if place_z < last:
                k = self.step_at(u - self.hop - (last - place_z - 1))
                if 0 <= k < self.steps and self.at(k)[0] <= place_z:
                    steps.append((k, False))
            if steps:

                @pl.when(z == place_z)
                def _(steps=steps, place_z=place_z):
                    for k, rightward in steps:
                        self.stage_hop(k, place_z, rightward)

    def begin(self):
        for k in range(min(self.ahead, self.steps)):
            self.stage_core(k)

    def turn(self, u):
        self.retire(self.step_at(u - self.retired))
        if self.static:
            for j in range(self.ahead, self.steps):
                if self.starts_at(j) == u:
                    self.stage_core(j)
        else:
            k = self.step_at(u + self.ahead)
            pl.when(k >= self.ahead)(lambda: self.stage_core(k))
        self.stage_one(self.step_at(u))
        self.stage_two(self.step_at(u - self.two))
        self.stage_three(self.step_at(u - self.three))
        self.stage_four(u)

    def pump(self, low, high):
        if self.static:
            for k in range(low, high):
                self.turn(k)
        elif high > low:

            def one(k, carry):
                self.turn(k)
                return carry

            lax.fori_loop(low, high, one, 0)


def stage_last(
    e2, r1, r2, gains, hidden, q, ctx, b_low, units, cos, sin, gains_one, master, one, two,
    slots_one, p, both, kv, w_gu, w_down, w_out, w_qkv, zn, rows_slot, share,
):
    rows = e2.shape[0]
    cols = kv.shape[0]
    ndev = zn * 8
    per_layer = ndev // 2
    half_zn = zn // 2
    step = chunk_rows(rows_slot)
    turns = rows_slot // step
    middle = split_slot(share)
    static, room, table = Reduce.plan(zn, rows_slot)
    steps = len(table)

    def body(
        e2_ref, r1_ref, r2_ref, g_ref, c_ref, s_ref, g1_ref, b_ref,
        s1_any, p_any, both_any, kv_any, gu_any, dn_any, wo_any, wq_any,
        h_any, q_any, ctx_any, units_any, m_any, one_any, two_any,
        ig_ref, nm_ref, n1_ref, n2_ref, nw_ref, gn_ref, gg_ref, s0_any,
        p_ref, both_ref, kv_ref, gu_ref, dn_ref, wo_ref, wq_ref,
        h_ref, q_ref, ctx_ref, units_ref, m_ref, one_ref, two_ref, load_sem,
        eboth_ref, ef_ref, ea_ref, ectx_ref, eq_ref, ekv_ref, lin_ref,
        flat, ring, stage, esem,
        acc, rc, first_buf, second_buf, rz, fin, sq, sqs,
        send, recv, lsem, ssem, rsem, free,
        dkv_ref, from_c, pair, from_y, ksend, krecv,
    ):
        z, x, y, c = coords()
        me = ((z * 2 + x) * 2 + y) * 2 + c
        bar = pltpu.get_barrier_semaphore()

        def peer(d):
            tgt = lax.rem(me + d, ndev)
            return {"dp": lax.div(tgt, 4), "sp": lax.rem(tgt, 4)}

        def hello(d, carry):
            pl.semaphore_signal(bar, inc=1, device_id=peer(d), device_id_type=MESH)
            return carry

        lax.fori_loop(1, ndev, hello, 0)
        loads = Loads(
            [
                (gu_any, gu_ref), (dn_any, dn_ref), (both_any, both_ref), (wo_any, wo_ref),
                (kv_any, kv_ref), (p_any, p_ref), (wq_any, wq_ref),
                (units_any, units_ref), (q_any, q_ref), (ctx_any, ctx_ref), (h_any, h_ref),
                (m_any, m_ref), (one_any, one_ref), (two_any, two_ref),
            ],
            load_sem,
        )
        bufs = (acc, rc, first_buf, second_buf, rz)
        stream = Reduce(s0_any, s1_any, bufs, fin, send, recv, lsem, free, zn, rows_slot)
        total = KeySum(dkv_ref, ekv_ref, from_c, pair, from_y, ksend, krecv)
        pl.semaphore_wait(bar, ndev - 1)
        stream.begin()
        done = [0]

        def pump(until):
            if until > done[0]:
                stream.pump(done[0], until)
                done[0] = until

        first_limit = stream.limit(half_zn - 1)
        second_limit = stream.limit((middle + 7) // 8 - 1)

        def ahead(part):
            pump(min(int(first_limit * part), first_limit))

        r2 = r2_ref[...]
        er2, gain2 = norm_back(e2_ref[...], r2, norm_factor(r2), g_ref[1:2, :])
        sq[12:16, :] = gain2.reshape(4, LANES)
        sq[16:24, :] = g1_ref[...].reshape(8, LANES)
        ef_ref[...] = er2.astype(bf16)
        loads.wait(0, 1, 2)
        ahead(0.1)
        e_first = er2 + feed_back(ef_ref[...], gu_ref, dn_ref, both_ref, eboth_ref)
        ahead(0.25)
        r1 = r1_ref[...]
        er1, gain1 = norm_back(e_first, r1, norm_factor(r1), g_ref[0:1, :])
        sq[8:12, :] = gain1.reshape(4, LANES)
        ig_ref[...] = er1
        ea_ref[...] = er1.astype(bf16)
        for t in range(TILES):
            grad_gate_up(flat, ring, t, b_ref[...], eboth_ref)
            if t % 3 == 2:
                ahead(0.25 + 0.15 * (t // 3 + 1))
        loads.wait(7)
        grad_down(flat, units_ref[...], ef_ref[...])
        grad_gains(flat, gain1, gain2)
        ahead(0.8)
        emit_slots(flat, BASE_GU, stage, s0_any, esem, rows_slot, share, middle, per_layer)
        loads.wait(3, 4, 5, 8)
        ectx_ref[...] = mm_nt(ea_ref[...], wo_ref[...]).astype(bf16)
        pump(first_limit)
        pairs = HEADS // 2
        for i in range(pairs):
            attend_back(i, q_ref, kv_ref, p_ref, ectx_ref, eq_ref, dkv_ref)
            total.start(i)
            if i >= 1:
                total.middle(i - 1)
            pump(first_limit + (second_limit - first_limit) * (i + 1) // (2 * pairs))
        total.middle(pairs - 1)
        carry_edge(flat, rows_slot)
        loads.wait(9, 10)
        grad_out(flat, ctx_ref[...], ea_ref[...])
        for i in range(pairs):
            total.end(i)
        pump(first_limit + (second_limit - first_limit) * 3 // 4)
        lin_grads(eq_ref, ekv_ref, c_ref, s_ref, lin_ref)
        grad_qkv(flat, h_ref[...], lin_ref)
        emit_slots(flat, 0, stage, s0_any, esem, rows_slot, share, 0, middle)
        pump(second_limit + 2)
        loads.wait(6, 11, 12, 13)
        ig_ref[...] = ig_ref[...] + mm_nt(lin_ref[...], wq_ref[...])
        pump(stream.turns)

        fin[pl.ds(rows_slot, 8), :] = jnp.zeros((8, LANES), f32)
        shift = lax.rem(share * me, LANES)
        back = lax.rem(LANES - shift, LANES)
        lane = lax.broadcasted_iota(jnp.int32, (step, LANES), 1)
        row = lax.broadcasted_iota(jnp.int32, (step, LANES), 0)

        def realign(i, carry):
            now = pltpu.roll(fin[pl.ds(i * step, step), :], back, 1)
            after = pltpu.roll(fin[pl.ds(i * step + 1, step), :], back, 1)
            value = jnp.where(lane < LANES - shift, now, after)
            value = jnp.where((row + i * step) * LANES + lane < share, value, 0.0)
            n1_ref[pl.ds(i * step, step), :] = value
            square = value * value
            return carry + jnp.sum(square.reshape(step // 8, 8, LANES), axis=0)

        sq[0:8, :] = lax.fori_loop(0, turns, realign, jnp.zeros((8, LANES), f32))

        def tell(d, carry):
            remote(sq, sqs.at[me], ssem, rsem, peer(d)).start()
            return carry

        lax.fori_loop(1, ndev, tell, 0)
        sqs[me] = sq[...]
        total.sent()
        part = sqs.at[pl.ds(0, ndev - 1)]
        both = remote(part, part, ssem, rsem, stream.to_c)
        both.wait_send()
        both.wait_recv()
        sums = lax.fori_loop(1, ndev, lambda i, s: s + sqs[i], sqs[0])
        gg_ref[...] = sums[8:24, :]
        squares = sums[0:8, :]
        norm = jnp.sqrt(jnp.sum(squares, keepdims=True))
        gn_ref[...] = jnp.broadcast_to(norm, (8, LANES))
        scale = jnp.minimum(1.0, 1.0 / norm)
        correction = 1.0 - 0.5**STEP

        def update(i, carry):
            span = pl.ds(pl.multiple_of(i * step, 16), step)
            clipped = n1_ref[span, :] * scale
            new_one = 0.5 * one_ref[span, :] + 0.5 * clipped
            new_two = 0.5 * two_ref[span, :] + 0.5 * clipped * clipped
            n1_ref[span, :] = new_one
            n2_ref[span, :] = new_two
            new_master = m_ref[pl.ds(8 + i * step, step), :] * (
                1.0 - LEARN_RATE * DECAY_RATE
            ) - LEARN_RATE * (new_one / correction) / (jnp.sqrt(new_two / correction) + ADAM_EPS)
            nm_ref[span, :] = new_master
            nw_ref[span, :] = new_master.astype(bf16)
            return carry

        lax.fori_loop(0, turns, update, 0)

    slot_flat = ((rows_slot, LANES), f32)
    outs = [
        ((rows, D), f32),
        slot_flat,
        slot_flat,
        slot_flat,
        ((rows_slot, LANES), bf16),
        ((8, LANES), f32),
        ((16, LANES), f32),
        ((per_layer // 8, 2, 2, 2, rows_slot, LANES), bf16),
    ]
    small = [e2, r1, r2, gains, cos, sin, gains_one, b_low]
    late = [hidden, q, ctx, units, master, one, two]
    large = [slots_one, p, both, kv, w_gu, w_down, w_out, w_qkv] + late
    act = pltpu.VMEM((rows, D), bf16)
    return pl.pallas_call(
        body,
        out_shape=[jax.ShapeDtypeStruct(s, d) for s, d in outs],
        in_specs=[vmem_spec()] * len(small) + [any_spec()] * len(large),
        out_specs=[vmem_spec()] * 7 + [any_spec()],
        scratch_shapes=[
            pltpu.VMEM(p.shape, bf16),
            pltpu.VMEM(both.shape, f32),
            pltpu.VMEM(kv.shape, bf16),
            pltpu.VMEM(w_gu.shape, bf16),
            pltpu.VMEM(w_down.shape, bf16),
            pltpu.VMEM(w_out.shape, bf16),
            pltpu.VMEM(w_qkv.shape, bf16),
        ]
        + [pltpu.VMEM(v.shape, v.dtype) for v in late]
        + [
            pltpu.SemaphoreType.DMA((14,)),
            pltpu.VMEM((rows, 2 * FFP), bf16),
            act,
            act,
            act,
            act,
            pltpu.VMEM((rows, 2 * D), bf16),
            pltpu.VMEM((rows, 3 * D), bf16),
            pltpu.VMEM((flat_rows(rows_slot), LANES), f32),
            pltpu.VMEM((6, D, LANES), f32),
            pltpu.VMEM((2, rows_slot, LANES), bf16),
            pltpu.SemaphoreType.DMA((2,)),
            pltpu.VMEM((room, 2, 2, rows_slot, LANES), bf16),
            pltpu.VMEM((room, 2, 2, rows_slot, LANES), bf16),
            pltpu.VMEM((room, 2, rows_slot, LANES), bf16),
            pltpu.VMEM((room, rows_slot, LANES), bf16),
            pltpu.VMEM((room, 2, rows_slot, LANES), bf16),
            pltpu.VMEM((rows_slot + 8, LANES), f32),
            pltpu.VMEM((24, LANES), f32),
            pltpu.VMEM((ndev, 24, LANES), f32),
            pltpu.SemaphoreType.DMA((steps, 6)),
            pltpu.SemaphoreType.DMA((steps, 7)),
            pltpu.SemaphoreType.DMA((steps,)),
            pltpu.SemaphoreType.DMA,
            pltpu.SemaphoreType.DMA,
            pltpu.SemaphoreType.REGULAR((room,)),
        ]
        + key_sum_scratch(rows),
        compiler_params=pltpu.CompilerParams(
            collective_id=4, has_side_effects=True, vmem_limit_bytes=63 * MIB
        ),
    )(*small, *large)


def rope_rows(rows):
    frequency = jnp.exp(
        -jnp.log(10000.0) * jnp.arange(HEAD_DIM // 2).astype(f32) * 2.0 / HEAD_DIM
    )
    positions = lax.axis_index("sp") * rows + jnp.arange(rows)
    angles = positions.astype(f32)[:, None] * frequency[None, :]
    cos = jnp.cos(angles)
    sin = jnp.sin(angles)
    return (
        jnp.concatenate([cos] * 4, axis=1),
        jnp.concatenate([-sin, sin, -sin, sin], axis=1),
    )


def step_shard(dp_size, sp_size, hidden_in, cotangent, lengths, master, moment_one, moment_two):
    share = master.shape[0]
    zn = dp_size // 2
    per_layer = dp_size * sp_size // 2
    rows = -(-(-(-share // LANES) + 1) // 32) * 32
    seqs, tokens, width = hidden_in.shape

    def pad(flat, lead):
        return jnp.pad(flat, (lead * LANES, rows * LANES - share)).reshape(rows + lead, LANES)

    master_pad = pad(master, 8)
    cos, sin = rope_rows(tokens)
    hidden = hidden_in.reshape(tokens, width)

    (
        g0, g1, q0, ctx0, r1, b0, units0, r2, second, a1, q1,
        wq0, wo0, wg0, wd0, wq1, wo1, wg1, wd1, kv0, kv1, p0, both0,
    ) = stage_head(lengths, master_pad, hidden, cos, sin, zn, rows, share)
    output, e2, gains_one, slots_one = stage_second(
        lengths, cotangent.reshape(tokens, width), second, q1, kv1, wo1, wg1, wd1, wq1, g1, a1,
        cos, sin, share, rows,
    )
    input_grad, new_master, new_one, new_two, new_weights, norm, gains, _ = stage_last(
        e2, r1, r2, g0, hidden, q0, ctx0, b0, units0, cos, sin, gains_one,
        master_pad, pad(moment_one, 0), pad(moment_two, 0),
        slots_one, p0, both0, kv0, wg0, wd0, wo0, wq0, zn, rows, share,
    )

    def flat(value):
        return value.reshape(-1)[:share]

    return (
        output.reshape(hidden_in.shape),
        input_grad.reshape(hidden_in.shape),
        flat(new_master),
        flat(new_one),
        flat(new_two),
        flat(new_weights),
        norm[0, 0],
        gains.reshape(2, 2, width),
    )


def solution(mesh):
    in_specs = (
        P("dp", "sp", None),
        P("dp", "sp", None),
        P("dp"),
        P(("dp", "sp")),
        P(("dp", "sp")),
        P(("dp", "sp")),
    )
    out_specs = (
        P("dp", "sp", None),
        P("dp", "sp", None),
        P(("dp", "sp")),
        P(("dp", "sp")),
        P(("dp", "sp")),
        P(("dp", "sp")),
        P(),
        P(),
    )
    body = functools.partial(step_shard, mesh.shape["dp"], mesh.shape["sp"])
    return jax.shard_map(body, mesh=mesh, in_specs=in_specs, out_specs=out_specs, check_vma=False)
```

```python
import functools

import jax
import jax.numpy as jnp
from jax import lax
from jax.experimental import pallas as pl
from jax.experimental.pallas import tpu as pltpu
from jax.sharding import PartitionSpec as P

D = 512
HEADS = 8
HEAD_DIM = 64
FF = 1368
FFP = 1408
TILES = 11
STEP = 5
NORM_EPS = 1e-06
ADAM_EPS = 1e-08
LEARN_RATE = 0.02
DECAY_RATE = 0.01
LANES = 128
LAYER_ROWS = 24616
BASE_OUT = 6144
BASE_GU = 8192
BASE_DOWN = 19136
BASE_GAINS = 24608
GU_ROW = 2 * FF
PERIOD = 171
MESH = pl.DeviceIdType.MESH
MIB = 1 << 20
f32 = jnp.float32
bf16 = jnp.bfloat16


def mm(a, b):
    return lax.dot_general(a, b, (((1,), (0,)), ((), ())), preferred_element_type=f32)


def mm_nt(a, b):
    return lax.dot_general(a, b, (((1,), (1,)), ((), ())), preferred_element_type=f32)


def mm_tn(a, b):
    return lax.dot_general(a, b, (((0,), (0,)), ((), ())), preferred_element_type=f32)


def chunk_rows(rows):
    tiles = rows // 16
    best = max(d for d in range(1, 17) if tiles % d == 0)
    return best * 16


def vmem_spec():
    return pl.BlockSpec(memory_space=pltpu.VMEM)


def any_spec():
    return pl.BlockSpec(memory_space=pl.ANY)


def local_call(body, outs, ins, scratch=(), limit=60, flops=0):
    return pl.pallas_call(
        body,
        out_shape=[jax.ShapeDtypeStruct(s, d) for s, d in outs],
        in_specs=[vmem_spec()] * len(ins),
        out_specs=[vmem_spec()] * len(outs),
        scratch_shapes=list(scratch),
        compiler_params=pltpu.CompilerParams(vmem_limit_bytes=limit * MIB),
    )(*ins)


def coords():
    dp = lax.axis_index("dp")
    sp = lax.axis_index("sp")
    return lax.div(dp, 2), lax.rem(dp, 2), lax.div(sp, 2), lax.rem(sp, 2)


def place(z, x, y, c):
    return {"dp": z * 2 + x, "sp": y * 2 + c}


def remote(src, dst, send_sem, recv_sem, device):
    return pltpu.make_async_remote_copy(
        src_ref=src,
        dst_ref=dst,
        send_sem=send_sem,
        recv_sem=recv_sem,
        device_id=device,
        device_id_type=MESH,
    )


def order_at(tau, z):
    step = lax.div(tau + 1, 2)
    return z + jnp.where(lax.rem(tau, 2) == 1, -step, step)


class Gather:
    lag = 2
    sizes = ((25, 24, 25, 24), (33, 32, 33))
    cut = 0.5

    def __init__(self, slots, send, recv, zn, rows):
        self.slots, self.send, self.recv, self.zn = slots, send, recv, zn
        self.static, self.table = self.plan(zn, rows)
        self.steps = len(self.table)
        self.turns = self.steps + 2 * self.lag
        self.z, self.x, self.y, self.c = coords()
        z, x, y, c = self.z, self.x, self.y, self.c
        self.to_x = place(z, 1 - x, y, c)
        self.to_y = place(z, x, 1 - y, c)
        self.to_c = place(z, x, y, 1 - c)
        self.ahead = z >= zn // 2

    @classmethod
    def plan(cls, zn, rows):
        if rows // 16 != 98:
            return False, [(zp, 0, rows, rows // 32 * 16) for zp in range(zn)]
        table = []
        for zp in range(zn):
            base = 0
            for tiles in cls.sizes[min(zp, len(cls.sizes) - 1)]:
                table.append((zp, base, 16 * tiles, 16 * round(tiles * cls.cut)))
                base += 16 * tiles
        return True, table

    def first(self, zp):
        return min(k for k in range(self.steps) if self.table[k][0] == zp)

    def until(self, zp):
        return self.first(zp) + 2 * self.lag if zp < self.zn else self.turns

    def at(self, k):
        return self.table[k] if self.static else (k,) + self.table[0][1:]

    def ref(self, k, xp, yp, part=None):
        zp, base, size, half = self.at(k)
        if part == 0:
            size = half
        if part == 1:
            base, size = base + half, size - half
        return self.slots.at[zp, self.c, xp * 2 + yp, pl.ds(base, size)]

    def cp(self, ref, k, s, r, device):
        return remote(ref, ref, self.send.at[k, s], self.recv.at[k, r], device)

    def right(self, k):
        return self.cp(self.ref(k, self.x, self.y), k, 0, 0, place(self.z + 1, self.x, self.y, self.c))

    def left(self, k):
        return self.cp(self.ref(k, self.x, self.y), k, 1, 0, place(self.z - 1, self.x, self.y, self.c))

    def over_x(self, k):
        return self.cp(self.ref(k, self.x, self.y), k, 2, 1, self.to_x)

    def over_y(self, k):
        return self.cp(self.ref(k, self.x, self.y), k, 3, 2, self.to_y)

    def upper(self, k):
        return self.cp(self.ref(k, 1 - self.x, self.y, 0), k, 4, 3, self.to_y)

    def lower(self, k):
        return self.cp(self.ref(k, self.x, 1 - self.y, 1), k, 5, 4, self.to_x)

    def over_c(self, k, c):
        zp, base, size, half = self.at(k)
        return self.cp(self.slots.at[zp, c, :, pl.ds(base, size)], k, 6, 5, self.to_c)

    def arrival(self, ref, k, r):
        self.cp(ref, k, 0, r, self.to_c).wait_recv()

    def onward(self, k):
        zp, z = self.at(k)[0], self.z
        pl.when((zp <= z) & (z < self.zn - 1))(lambda: self.right(k).start())
        pl.when((zp >= z) & (z > 0))(lambda: self.left(k).start())

    def across(self, k):
        self.over_x(k).start()
        self.over_y(k).start()

    def begin(self):
        def own(k):
            self.onward(k)
            self.across(k)

        if self.static:
            for k in range(self.first(self.zn // 2), self.steps):
                pl.when(self.z == self.at(k)[0])(functools.partial(own, k))
        else:
            pl.when(self.ahead)(lambda: own(self.z))

    def guard(self, k, act):
        if isinstance(k, int):
            if 0 <= k < self.steps:
                act()
        else:
            pl.when((k >= 0) & (k < self.steps))(act)

    def turn(self, k):
        z, x, y = self.z, self.x, self.y

        def come():
            zp = self.at(k)[0]

            @pl.when((zp != z) | (z < self.zn // 2))
            def _():
                pl.when(zp != z)(lambda: self.arrival(self.ref(k, x, y), k, 0))
                self.onward(k)
                self.across(k)

        def go_on():
            q = k - self.lag
            self.arrival(self.ref(q, 1 - x, y), q, 1)
            self.upper(q).start()
            self.arrival(self.ref(q, x, 1 - y), q, 2)
            self.lower(q).start()

        def share():
            r = k - 2 * self.lag
            self.arrival(self.ref(r, 1 - x, 1 - y, 0), r, 3)
            self.arrival(self.ref(r, 1 - x, 1 - y, 1), r, 4)
            self.over_c(r, self.c).start()

        self.guard(k, come)
        self.guard(k - self.lag, go_on)
        self.guard(k - 2 * self.lag, share)

    def loop(self, low, high, act):
        if self.static:
            for k in range(low, high):
                act(k)
        elif high > low:

            def one(k, carry):
                act(k)
                return carry

            lax.fori_loop(low, high, one, 0)

    def pump(self, low, high):
        self.loop(low, high, self.turn)

    def arrived(self, low, high):
        end = self.first(high) if high < self.zn else self.steps
        self.loop(self.first(low), end, lambda k: self.over_c(k, 1 - self.c).wait_recv())

    def sent(self):
        def one(k):
            zp, z = self.at(k)[0], self.z
            pl.when((zp <= z) & (z < self.zn - 1))(lambda: self.right(k).wait_send())
            pl.when((zp >= z) & (z > 0))(lambda: self.left(k).wait_send())
            for item in (self.over_x(k), self.over_y(k), self.upper(k), self.lower(k)):
                item.wait_send()
            self.over_c(k, self.c).wait_send()

        self.loop(0, self.steps, one)


class KeyExchange:
    def __init__(self, kv_ref, all_ref, send, recv, lsem, parts):
        z, x, y, c = coords()
        rows = kv_ref.shape[0]
        piece = rows // parts
        to_y = place(z, x, 1 - y, c)
        to_c = place(z, x, y, 1 - c)
        mine = y * 2 + c
        beyond = (1 - y) * 2 + c
        self.parts = parts

        def part(row, k):
            return all_ref.at[pl.ds(pl.multiple_of(row * rows, rows) + k * piece, piece)]

        self.keep = pltpu.make_async_copy(
            kv_ref, all_ref.at[pl.ds(pl.multiple_of(mine * rows, rows), rows)], lsem
        )
        self.own_y, self.own_c, self.pass_c = [], [], []
        for k in range(parts):
            src, dst = kv_ref.at[pl.ds(k * piece, piece)], part(mine, k)
            self.own_y.append(remote(src, dst, send.at[0, k], recv.at[0, k], to_y))
            self.own_c.append(remote(src, dst, send.at[1, k], recv.at[1, k], to_c))
            ref = part(beyond, k)
            self.pass_c.append(remote(ref, ref, send.at[2, k], recv.at[2, k], to_c))

    def start(self):
        self.keep.start()
        for item in self.own_y + self.own_c:
            item.start()

    def forward(self, *parts):
        for k in parts:
            self.own_y[k].wait_recv()
            self.pass_c[k].start()

    def finish(self):
        for k in range(self.parts):
            self.own_c[k].wait_recv()
            self.pass_c[k].wait_recv()
        for item in self.own_y + self.own_c + self.pass_c:
            item.wait_send()
        self.keep.wait()


REGIONS = {"qkv": (0, BASE_OUT), "out": (BASE_OUT, BASE_GU), "gu": (BASE_GU, BASE_DOWN), "down": (BASE_DOWN, LAYER_ROWS)}
GROUPS = ((0, 6), (6, TILES))


def fill_flat(slots, flat, layer, name, rows, share):
    low, high = REGIONS[name]
    step = chunk_rows(rows)
    per_layer = LAYER_ROWS * LANES // share

    def one(i, carry):
        start = lax.div(share * i, LANES) - low + rows
        shift = lax.rem(share * i, LANES)
        index = i + layer * per_layer
        z, x = lax.div(index, 8), lax.rem(lax.div(index, 4), 2)
        y, c = lax.rem(lax.div(index, 2), 2), lax.rem(index, 2)
        edge = flat[pl.ds(start, 1), :]

        def fill(j, inner):
            flat[pl.ds(start + j * step, step), :] = slots[
                z, c, x * 2 + y, pl.ds(j * step, step), :
            ].astype(f32)
            return inner

        lax.fori_loop(0, rows // step, fill, 0)

        @pl.when(shift > 0)
        def _():
            flat[pl.ds(start, 1), :] = flat[pl.ds(start, 1), :] + edge

        return carry

    lax.fori_loop(low * LANES // share, (high * LANES - 1) // share + 1, one, 0)


def take_qkv(flat, top, qkv_ref):
    for col in range(12):
        qkv_ref[:, 128 * col : 128 * col + 128] = flat[pl.ds(top + col, D, stride=12), :].astype(bf16)


def take_out(flat, top, out_ref):
    for col in range(4):
        span = slice(128 * col, 128 * col + 128)
        out_ref[:, span] = flat[pl.ds(top + col, D, stride=4), :].astype(bf16)


def take_down(flat, top, down_ref, gains_ref):
    base = top + BASE_GAINS - BASE_DOWN
    for col in range(4):
        span = slice(128 * col, 128 * col + 128)
        down_ref[0:FF, span] = flat[pl.ds(top + col, FF, stride=4), :].astype(bf16)
        gains_ref[:, span] = flat[pl.ds(base + col, 2, stride=4), :]
    down_ref[FF:FFP, :] = jnp.zeros((FFP - FF, D), bf16)


def take_gate_up(flat, top, gate_up, gu_ref, group):
    lane = lax.broadcasted_iota(jnp.int32, (64, LANES), 1)
    low, high = group
    for r in range(8):
        for part in range(2):
            for tile in range(low, high):
                first = GU_ROW * r + FF * part + LANES * tile
                q, s = first // LANES, first % LANES
                value = flat[pl.ds(top + q, 64, stride=PERIOD), :]
                if s:
                    after = flat[pl.ds(top + q + 1, 64, stride=PERIOD), :]
                    value = jnp.where(
                        lane < LANES - s,
                        pltpu.roll(value, LANES - s, 1),
                        pltpu.roll(after, LANES - s, 1),
                    )
                if tile == TILES - 1:
                    value = jnp.where(lane < FF - LANES * tile, value, 0.0)
                gate_up[2 * (tile - low) + part, pl.ds(r, 64, stride=8), :] = value
    for k in range(2 * (high - low)):
        span = slice(256 * low + 128 * k, 256 * low + 128 * k + 128)
        gu_ref[:, span] = gate_up[k].astype(bf16)


def gate_up_segments(q):
    pieces = []
    place_now = LANES * q
    end = place_now + LANES
    while place_now < end:
        r, within = divmod(place_now, GU_ROW)
        part, unit = divmod(within, FF)
        tile, lane_src = divmod(unit, LANES)
        room = min(end - place_now, FF - unit, LANES - lane_src)
        lane_dst = place_now - LANES * q
        pieces.append((r, 2 * tile + part, lane_dst, lane_dst + room, (lane_dst - lane_src) % LANES))
        place_now += room
    return pieces


def gate_up_rows(tile):
    out = []
    for q in range(PERIOD):
        pieces = gate_up_segments(q)
        if max(k // 2 for _, k, _, _, _ in pieces) == tile:
            out.append((q, pieces))
    return out


def grad_qkv(flat, a_low, lin_ref):
    for t in range(6):
        value = mm_tn(a_low, lin_ref[:, 256 * t : 256 * t + 256])
        for k in range(2):
            flat[pl.ds(2 * t + k, D, stride=12), :] = value[:, 128 * k : 128 * k + 128]


def grad_out(flat, ctx, ea):
    for t in range(2):
        value = mm_tn(ctx, ea[:, 256 * t : 256 * t + 256])
        for k in range(2):
            flat[pl.ds(BASE_OUT + 2 * t + k, D, stride=4), :] = value[:, 128 * k : 128 * k + 128]


def grad_down(flat, units, ef):
    for t in range(2):
        value = mm_tn(units, ef[:, 256 * t : 256 * t + 256])
        for k in range(2):
            start = BASE_DOWN - BASE_GU + 2 * t + k
            flat[pl.ds(start, FF, stride=4), :] = value[0:FF, 128 * k : 128 * k + 128]


def grad_gate_up(flat, ring, t, b_low, eboth_ref):
    def at(tile):
        return 2 if tile == 0 else tile % 2

    value = mm_tn(b_low, eboth_ref[:, 256 * t : 256 * t + 256])
    for k in range(2):
        ring[2 * at(t) + k] = value[:, 128 * k : 128 * k + 128]
    lane = lax.broadcasted_iota(jnp.int32, (64, LANES), 1)
    for q, pieces in gate_up_rows(t):
        total = None
        for r, k, low, high, turn in pieces:
            piece = ring[2 * at(k // 2) + k % 2, pl.ds(r, 64, stride=8), :]
            if turn:
                piece = pltpu.roll(piece, turn, 1)
            total = piece if total is None else jnp.where(lane < low, total, piece)
        flat[pl.ds(q, 64, stride=PERIOD), :] = total


def grad_gains(flat, first, second):
    base = BASE_GAINS - BASE_GU
    for col in range(4):
        flat[pl.ds(base + col, 1), :] = first[:, 128 * col : 128 * col + 128]
        flat[pl.ds(base + 4 + col, 1), :] = second[:, 128 * col : 128 * col + 128]
    flat[LAYER_ROWS - BASE_GU :, :] = jnp.zeros((flat.shape[0] - LAYER_ROWS + BASE_GU, LANES), f32)


def flat_rows(rows):
    return LAYER_ROWS - BASE_GU + rows


def split_slot(share):
    return BASE_GU * LANES // share + 1


def carry_edge(flat, rows):
    flat[BASE_GU : BASE_GU + rows, :] = flat[0:rows, :]


def emit_slots(flat, base, stage, out_ref, sem, rows, share, low, high):
    step = chunk_rows(rows)

    def put(i):
        k = lax.rem(i, 2)
        z, x = lax.div(i, 8), lax.rem(lax.div(i, 4), 2)
        y, c = lax.rem(lax.div(i, 2), 2), lax.rem(i, 2)
        return pltpu.make_async_copy(stage.at[k], out_ref.at[z, c, x, y], sem.at[k])

    def one(i, carry):
        pl.when(i >= low + 2)(lambda: put(i - 2).wait())
        start = lax.div(share * i, LANES) - base
        k = lax.rem(i, 2)

        def fill(j, inner):
            stage[k, pl.ds(j * step, step), :] = flat[pl.ds(start + j * step, step), :].astype(bf16)
            return inner

        lax.fori_loop(0, rows // step, fill, 0)
        put(i).start()
        return carry

    lax.fori_loop(low, high, one, 0)
    put(high - 2).wait()
    put(high - 1).wait()


class KeySum:
    def __init__(self, part_ref, sum_ref, from_c, pair, from_y, send, recv):
        z, x, y, c = coords()
        self.part, self.sum_ref = part_ref, sum_ref
        self.from_c, self.pair, self.from_y = from_c, pair, from_y
        self.send, self.recv = send, recv
        self.rows = pair.shape[1]
        self.y, self.c = y, c
        self.to_y = place(z, x, 1 - y, c)
        self.to_c = place(z, x, y, 1 - c)

    def block(self, i, yp, cp):
        start = pl.multiple_of((yp * 2 + cp) * self.rows, self.rows)
        return self.part.at[i, pl.ds(start, self.rows)]

    def near(self, i, h):
        yp = self.y if h else 1 - self.y
        return remote(
            self.block(i, yp, 1 - self.c), self.from_c.at[h, i],
            self.send.at[i, h], self.recv.at[i, h], self.to_c,
        )

    def wide(self, i):
        return remote(
            self.pair.at[i], self.from_y.at[i], self.send.at[i, 2], self.recv.at[i, 2], self.to_y
        )

    def start(self, i):
        self.near(i, 0).start()
        self.near(i, 1).start()

    def middle(self, i):
        self.near(i, 0).wait_recv()
        self.pair[i] = (
            self.from_c[0, i].astype(f32) + self.block(i, 1 - self.y, self.c)[...].astype(f32)
        ).astype(bf16)
        self.wide(i).start()

    def end(self, i):
        self.near(i, 1).wait_recv()
        self.wide(i).wait_recv()
        total = (
            self.from_c[1, i].astype(f32)
            + self.block(i, self.y, self.c)[...].astype(f32)
            + self.from_y[i].astype(f32)
        ).astype(bf16)
        self.sum_ref[:, LANES * i : LANES * i + LANES] = total[:, :LANES]
        self.sum_ref[:, D + LANES * i : D + LANES * i + LANES] = total[:, LANES:]

    def sent(self):
        for i in range(HEADS // 2):
            self.near(i, 0).wait_send()
            self.near(i, 1).wait_send()
            self.wide(i).wait_send()


def key_sum_scratch(rows):
    pairs = HEADS // 2
    return [
        pltpu.VMEM((pairs, 4 * rows, 2 * LANES), bf16),
        pltpu.VMEM((2, pairs, rows, 2 * LANES), bf16),
        pltpu.VMEM((pairs, rows, 2 * LANES), bf16),
        pltpu.VMEM((pairs, rows, 2 * LANES), bf16),
        pltpu.SemaphoreType.DMA((pairs, 3)),
        pltpu.SemaphoreType.DMA((pairs, 3)),
    ]


def half_swap(u):
    lane = lax.broadcasted_iota(jnp.int32, u.shape, 1)
    return jnp.where(lax.rem(lane, 64) < 32, pltpu.roll(u, 96, 1), pltpu.roll(u, 32, 1))


def project_heads(a_low, w_ref, cos_ref, sin_ref, q_ref, kv_ref, tiles=range(6)):
    for t in tiles:
        lin = mm(a_low, w_ref[:, 256 * t : 256 * t + 256])
        for k in range(2):
            u = lin[:, 128 * k : 128 * k + 128]
            if t < 4:
                u = u * cos_ref[...] + half_swap(u) * sin_ref[...]
            col = 256 * t + 128 * k
            if col < D:
                q_ref[:, col : col + 128] = u.astype(bf16)
            else:
                kv_ref[:, col - D : col - D + 128] = u.astype(bf16)


def norm_factor(r):
    return lax.rsqrt(jnp.mean(r * r, axis=-1, keepdims=True) + NORM_EPS)


def norm_back(e, r, f, g):
    scaled = e * g
    gain = jnp.sum(e * r * f, axis=0, keepdims=True)
    grad = f * scaled - r * (f * f * f) * jnp.mean(scaled * r, axis=-1, keepdims=True)
    return grad, gain


def head_mask(rows, h):
    lane = lax.broadcasted_iota(jnp.int32, (rows, LANES), 1)
    return (lane >= 64) if h else (lane < 64)


def make_bias(bias, length):
    rows, cols = bias.shape
    first = lax.axis_index("sp") * rows
    row = lax.broadcasted_iota(jnp.int32, (rows, cols), 0) + first
    col = lax.broadcasted_iota(jnp.int32, (rows, cols), 1)
    bias[...] = jnp.where((col <= row) & (col < length), 0.0, -1e9)


def attend(i, q_ref, kv_ref, bias, p_ref, ctx_ref):
    rows = q_ref.shape[0]
    span = slice(LANES * i, LANES * i + LANES)
    keys = kv_ref[:, span]
    values = kv_ref[:, D + LANES * i : D + LANES * i + LANES]
    queries = q_ref[:, span]
    total = jnp.zeros((rows, LANES), f32)
    for h in range(2):
        qm = jnp.where(head_mask(rows, h), queries, jnp.zeros_like(queries))
        vm = jnp.where(head_mask(values.shape[0], h), values, jnp.zeros_like(values))
        logits = mm_nt(qm, keys) * HEAD_DIM ** (-0.5) + bias[...]
        top = jnp.max(logits, axis=-1, keepdims=True)
        soft = jnp.exp(logits - top)
        norm = 1.0 / jnp.sum(soft, axis=-1, keepdims=True)
        low = (soft * norm).astype(bf16)
        p_ref[2 * i + h] = low
        total = total + mm(low, vm)
    ctx_ref[:, span] = total.astype(bf16)


def attend_back(i, q_ref, kv_ref, p_ref, ectx_ref, eq_ref, dkv_ref):
    rows = q_ref.shape[0]
    cols = kv_ref.shape[0]
    span = slice(LANES * i, LANES * i + LANES)
    keys = kv_ref[:, span]
    values = kv_ref[:, D + LANES * i : D + LANES * i + LANES]
    queries = q_ref[:, span]
    grads = ectx_ref[:, span]
    dq = jnp.zeros((rows, LANES), f32)
    dk = jnp.zeros((LANES, cols), f32)
    dv = jnp.zeros((LANES, cols), f32)
    for h in range(2):
        mask = head_mask(rows, h)
        qm = jnp.where(mask, queries, jnp.zeros_like(queries))
        em = jnp.where(mask, grads, jnp.zeros_like(grads))
        km = jnp.where(head_mask(cols, h), keys, jnp.zeros_like(keys))
        low = p_ref[2 * i + h]
        soft = low.astype(f32)
        dp = mm_nt(em, values)
        center = jnp.sum(soft * dp, axis=-1, keepdims=True)
        raw = (soft * (dp - center) * HEAD_DIM ** (-0.5)).astype(bf16)
        dv = dv + mm_tn(em, low)
        dk = dk + mm_tn(qm, raw)
        dq = dq + mm(raw, km)
    eq_ref[:, span] = dq.astype(bf16)
    dkv_ref[i, :, :LANES] = dk.T.astype(bf16)
    dkv_ref[i, :, LANES:] = dv.T.astype(bf16)


def feed_forward(b_low, gu_ref, down_ref, both_ref, units_ref):
    for t in range(TILES):
        both = mm(b_low, gu_ref[:, 256 * t : 256 * t + 256])
        both_ref[:, 256 * t : 256 * t + 256] = both
        gate, up = both[:, :128], both[:, 128:]
        units_ref[:, 128 * t : 128 * t + 128] = (gate / (1.0 + jnp.exp(-gate)) * up).astype(bf16)
    return mm(units_ref[...], down_ref[...])


def feed_back(e_low, gu_ref, down_ref, both_ref, eboth_ref, pump=None):
    for t in range(TILES):
        if pump is not None and t % 4 == 3:
            pump()
        eu = mm_nt(e_low, down_ref[128 * t : 128 * t + 128, :])
        gate = both_ref[:, 256 * t : 256 * t + 128]
        up = both_ref[:, 256 * t + 128 : 256 * t + 256]
        sig = 1.0 / (1.0 + jnp.exp(-gate))
        eboth_ref[:, 256 * t : 256 * t + 128] = (eu * up * sig * (1.0 + gate * (1.0 - sig))).astype(bf16)
        eboth_ref[:, 256 * t + 128 : 256 * t + 256] = (eu * gate * sig).astype(bf16)
    return mm_nt(eboth_ref[...], gu_ref[...])


def stage_head(length, master_pad, hidden, cos, sin, zn, rows_slot, share):
    rows = hidden.shape[0]
    cols = 4 * rows
    step = chunk_rows(rows_slot)
    half_zn = zn // 2
    ndev = zn * 8
    gains_row = BASE_GAINS - share * (ndev // 2 - 1) // LANES
    first_zp = -(-BASE_OUT * LANES // (8 * share))
    parts = 4
    gather_steps = len(Gather.plan(zn, rows_slot)[1])
    top = rows_slot

    def body(
        l_ref, x_ref, h_ref, c_ref, s_ref,
        g0, g1, q0, ctx_ref, r1_ref, b_ref, units_ref, r2_ref, sec_ref, a1_ref, q1,
        wq0_any, wo0_any, wg0_any, wd0_any, wq1_any, wo1_any, wg1_any, wd1_any,
        kv0_any, kv1_any, p_any, both_any,
        wq0, wo0, wg0, wd0, wq1, wo1, wg1, wd1, all0, all1, p_ref, both_ref,
        slots, flat, gate_up, kv0, kv1, bias, send, recv,
        ksend0, krecv0, ksend1, krecv1, lsem, osem, gains_out, gains_in, gsend, grecv,
    ):
        z, x, y, c = coords()
        bar = pltpu.get_barrier_semaphore()

        def hello(device):
            pl.semaphore_signal(bar, inc=1, device_id=device, device_id_type=MESH)

        hello(place(z, 1 - x, y, c))
        hello(place(z, x, 1 - y, c))
        hello(place(z, x, y, 1 - c))
        pl.when(z > 0)(lambda: hello(place(z - 1, x, y, c)))
        pl.when(z < zn - 1)(lambda: hello(place(z + 1, x, y, c)))
        me = ((z * 2 + x) * 2 + y) * 2 + c
        owner = me == ndev - 1
        pl.when(me != ndev - 1)(lambda: hello(place(zn - 1, 1, 1, 1)))

        shift = lax.rem(share * (((z * 2 + x) * 2 + y) * 2 + c), LANES)
        lane = lax.broadcasted_iota(jnp.int32, (step, LANES), 1)

        def align(i, carry):
            now = pltpu.roll(x_ref[pl.ds(8 + i * step, step), :], shift, 1)
            before = pltpu.roll(x_ref[pl.ds(7 + i * step, step), :], shift, 1)
            slots[z, c, x * 2 + y, pl.ds(i * step, step), :] = jnp.where(
                lane >= shift, now, before
            ).astype(bf16)
            return carry

        lax.fori_loop(0, rows_slot // step, align, 0)
        now = pltpu.roll(x_ref[pl.ds(8 + gains_row, 8), :], shift, 1)
        before = pltpu.roll(x_ref[pl.ds(7 + gains_row, 8), :], shift, 1)
        gains_out[...] = jnp.zeros((16, LANES), bf16)
        gains_out[0:8, :] = jnp.where(lane[0:8] >= shift, now, before).astype(bf16)
        pl.semaphore_wait(
            bar,
            3
            + (z > 0).astype(jnp.int32)
            + (z < zn - 1).astype(jnp.int32)
            + owner.astype(jnp.int32) * (ndev - 1),
        )

        def tell_gains(d):
            device = {"dp": lax.div(d, 4), "sp": lax.rem(d, 4)}
            return remote(gains_out, gains_in, gsend.at[d], grecv, device)

        @pl.when(owner)
        def _():
            def go(d, carry):
                tell_gains(d).start()
                return carry

            lax.fori_loop(0, ndev - 1, go, 0)
            gains_in[...] = gains_out[...]

        gather = Gather(slots, send, recv, zn, rows_slot)
        done = [0]

        def pump(until):
            gather.pump(done[0], until)
            done[0] = max(done[0], until)

        def between(low, high, k, n):
            pump(low + (high - low) * k // n)

        saves = [
            pltpu.make_async_copy(src, dst, osem.at[i])
            for i, (src, dst) in enumerate(
                [
                    (wq0, wq0_any), (wo0, wo0_any), (wg0, wg0_any), (wd0, wd0_any),
                    (wq1, wq1_any), (wo1, wo1_any), (wg1, wg1_any), (wd1, wd1_any),
                    (all0, kv0_any), (all1, kv1_any), (p_ref, p_any), (both_ref, both_any),
                ]
            )
        ]

        def fill(layer, name):
            fill_flat(slots, flat, layer, name, rows_slot, share)

        gather.begin()
        make_bias(bias, l_ref[0])
        pump(gather.until(first_zp))
        gather.arrived(0, first_zp)
        fill(0, "qkv")
        take_qkv(flat, top, wq0)
        exchange0 = KeyExchange(kv0, all0, ksend0, krecv0, lsem.at[0], parts)
        project_heads(h_ref[...], wq0, c_ref, s_ref, q0, kv0, range(2, 6))
        exchange0.start()
        saves[0].start()
        low, high = gather.until(first_zp), gather.until(half_zn)
        between(low, high, 1, 2)
        project_heads(h_ref[...], wq0, c_ref, s_ref, q0, kv0, range(2))
        exchange0.forward(0, 1, 2, 3)
        pump(high)
        exchange0.finish()
        saves[8].start()
        low, high = high, gather.until(half_zn + first_zp)
        for i in range(HEADS // 2):
            attend(i, q0, all0, bias, p_ref, ctx_ref)
            if i == 1:
                between(low, high, 1, 2)
        saves[10].start()
        gather.arrived(first_zp, half_zn)
        fill(0, "out")
        take_out(flat, top, wo0)
        saves[1].start()
        fill(0, "down")
        take_down(flat, top, wd0, g0)
        saves[3].start()
        pump(high)
        fill(0, "gu")
        for group in GROUPS:
            take_gate_up(flat, top, gate_up, wg0, group)
        saves[2].start()
        low, high = high, gather.until(zn)
        between(low, high, 1, 3)
        r1 = h_ref[...].astype(f32) + mm(ctx_ref[...], wo0[...])
        r1_ref[...] = r1
        first = r1 * norm_factor(r1) * g0[0:1, :]
        b_ref[...] = first.astype(bf16)
        r2 = first + feed_forward(b_ref[...], wg0, wd0, both_ref, units_ref)
        saves[11].start()
        r2_ref[...] = r2
        second = r2 * norm_factor(r2) * g0[1:2, :]
        sec_ref[...] = second
        between(low, high, 2, 3)
        gather.arrived(half_zn, half_zn + first_zp)
        fill(1, "qkv")
        take_qkv(flat, top, wq1)
        saves[4].start()

        @pl.when(me != ndev - 1)
        def _():
            tell_gains(0).wait_recv()

        known = gains_in[...].astype(f32)
        for col in range(4):
            span = slice(LANES * col, LANES * col + LANES)
            g1[0:1, span] = known[col : col + 1, :]
            g1[1:2, span] = known[4 + col : 5 + col, :]
        a1_ref[...] = (second * norm_factor(second) * g1[0:1, :]).astype(bf16)
        exchange1 = KeyExchange(kv1, all1, ksend1, krecv1, lsem.at[1], parts)
        project_heads(a1_ref[...], wq1, c_ref, s_ref, q1, kv1, range(2, 6))
        exchange1.start()
        project_heads(a1_ref[...], wq1, c_ref, s_ref, q1, kv1, range(2))
        pump(high)
        gather.arrived(half_zn + first_zp, zn)
        fill(1, "down")
        take_down(flat, top, wd1, g1)
        saves[7].start()
        fill(1, "out")
        take_out(flat, top, wo1)
        saves[5].start()
        fill(1, "gu")
        take_gate_up(flat, top, gate_up, wg1, GROUPS[0])
        exchange1.forward(0, 1, 2, 3)
        take_gate_up(flat, top, gate_up, wg1, GROUPS[1])
        saves[6].start()
        exchange1.finish()
        saves[9].start()
        gather.sent()

        @pl.when(owner)
        def _():
            def wait(d, carry):
                tell_gains(d).wait_send()
                return carry

            lax.fori_loop(0, ndev - 1, wait, 0)

        for item in saves:
            item.wait()

    layer = [((D, 3 * D), bf16), ((D, D), bf16), ((D, 2 * FFP), bf16), ((FFP, D), bf16)]
    kept = layer + layer + [
        ((cols, 2 * D), bf16),
        ((cols, 2 * D), bf16),
        ((HEADS, rows, cols), bf16),
        ((rows, 2 * FFP), f32),
    ]
    low_rows, full_rows = ((rows, D), bf16), ((rows, D), f32)
    outs = [
        ((2, D), f32),
        ((2, D), f32),
        low_rows,
        low_rows,
        full_rows,
        low_rows,
        ((rows, FFP), bf16),
        full_rows,
        full_rows,
        low_rows,
        low_rows,
    ]
    ins = [length, master_pad, hidden, cos, sin]
    longest = max(high - low for low, high in REGIONS.values())
    kv_scratch = pltpu.VMEM((rows, 2 * D), bf16)
    return pl.pallas_call(
        body,
        out_shape=[jax.ShapeDtypeStruct(s, d) for s, d in outs + kept],
        in_specs=[pl.BlockSpec(memory_space=pltpu.SMEM)] + [vmem_spec()] * (len(ins) - 1),
        out_specs=[vmem_spec()] * len(outs) + [any_spec()] * len(kept),
        scratch_shapes=[pltpu.VMEM(s, d) for s, d in kept]
        + [
            pltpu.VMEM((zn, 2, 4, rows_slot, LANES), bf16),
            pltpu.VMEM((longest + 2 * rows_slot, LANES), f32),
            pltpu.VMEM((12, D, LANES), f32),
            kv_scratch,
            kv_scratch,
            pltpu.VMEM((rows, cols), f32),
            pltpu.SemaphoreType.DMA((gather_steps, 7)),
            pltpu.SemaphoreType.DMA((gather_steps, 6)),
            pltpu.SemaphoreType.DMA((3, parts)),
            pltpu.SemaphoreType.DMA((3, parts)),
            pltpu.SemaphoreType.DMA((3, parts)),
            pltpu.SemaphoreType.DMA((3, parts)),
            pltpu.SemaphoreType.DMA((2,)),
            pltpu.SemaphoreType.DMA((12,)),
            pltpu.VMEM((16, LANES), bf16),
            pltpu.VMEM((16, LANES), bf16),
            pltpu.SemaphoreType.DMA((ndev,)),
            pltpu.SemaphoreType.DMA,
        ],
        compiler_params=pltpu.CompilerParams(
            collective_id=1, has_side_effects=True, vmem_limit_bytes=62 * MIB
        ),
    )(*ins)


class Loads:
    def __init__(self, pairs, sem):
        self.items = [pltpu.make_async_copy(src, dst, sem.at[i]) for i, (src, dst) in enumerate(pairs)]
        for item in self.items:
            item.start()

    def wait(self, *which):
        for i in which:
            self.items[i].wait()


def meet(devices):
    bar = pltpu.get_barrier_semaphore()
    for device in devices:
        pl.semaphore_signal(bar, inc=1, device_id=device, device_id_type=MESH)
    pl.semaphore_wait(bar, len(devices))


def stage_second(
    length, cotangent, second, q, kv, w_out, w_gu, w_down, w_qkv, gains, a1, cos, sin, share, rows_slot
):
    rows = q.shape[0]
    cols = kv.shape[0]
    per_layer = LAYER_ROWS * LANES // share
    middle = split_slot(share)

    def body(
        l_ref, cot_ref, sec_ref, q_ref, g_ref, a_ref, c_ref, s_ref, kv_any, wo_any, gu_any, dn_any, wq_any,
        o_ref, e2_ref, gg_ref, slots_ref,
        kv_ref, wo_ref, gu_ref, dn_ref, wq_ref, lsem, eq_ref, lin_ref,
        bias, p_ref, ctx_ref, b_ref, both_ref, units_ref, eboth_ref, ef_ref, ea_ref, ectx_ref,
        ekv_ref, flat, ring, stage, esem,
        dkv_ref, from_c, pair, from_y, send, recv,
    ):
        loads = Loads(
            [
                (kv_any, kv_ref), (wo_any, wo_ref), (gu_any, gu_ref), (dn_any, dn_ref), (wq_any, wq_ref)
            ],
            lsem,
        )
        z, x, y, c = coords()
        meet([place(z, x, 1 - y, c), place(z, x, y, 1 - c)])
        total = KeySum(dkv_ref, ekv_ref, from_c, pair, from_y, send, recv)
        length_now = l_ref[0]
        make_bias(bias, length_now)
        loads.wait(0)
        for i in range(HEADS // 2):
            attend(i, q_ref, kv_ref, bias, p_ref, ctx_ref)
        loads.wait(1, 2, 3)
        third = sec_ref[...] + mm(ctx_ref[...], wo_ref[...])
        f4 = norm_factor(third)
        b_ref[...] = (third * f4 * g_ref[1:2, :]).astype(bf16)
        o_ref[...] = third + feed_forward(b_ref[...], gu_ref, dn_ref, both_ref, units_ref)
        place_now = lax.broadcasted_iota(jnp.int32, (rows, D), 0) + lax.axis_index("sp") * rows
        e_out = jnp.where(place_now < length_now, cot_ref[...], 0.0)
        ef_ref[...] = e_out.astype(bf16)
        e_b = feed_back(ef_ref[...], gu_ref, dn_ref, both_ref, eboth_ref)
        grad, gain = norm_back(e_b, third, f4, g_ref[1:2, :])
        gg_ref[1:2, :] = gain
        e3 = e_out + grad
        e2_ref[...] = e3
        ea_ref[...] = e3.astype(bf16)
        ectx_ref[...] = mm_nt(ea_ref[...], wo_ref[...]).astype(bf16)
        for i in range(HEADS // 2):
            attend_back(i, q_ref, kv_ref, p_ref, ectx_ref, eq_ref, dkv_ref)
            total.start(i)
            if i >= 1:
                total.middle(i - 1)
        for t in range(TILES):
            grad_gate_up(flat, ring, t, b_ref[...], eboth_ref)
            if t == 0:
                total.middle(3)
            if t in (1, 4, 7, 10):
                total.end((t - 1) // 3)
        lin_grads(eq_ref, ekv_ref, c_ref, s_ref, lin_ref)
        grad_down(flat, units_ref[...], ef_ref[...])
        loads.wait(4)
        second = sec_ref[...]
        grad, gain = norm_back(
            mm_nt(lin_ref[...], wq_ref[...]), second, norm_factor(second), g_ref[0:1, :]
        )
        gg_ref[0:1, :] = gain
        e2_ref[...] = e2_ref[...] + grad
        grad_gains(flat, gg_ref[0:1, :], gg_ref[1:2, :])
        emit_slots(flat, BASE_GU, stage, slots_ref, esem, rows_slot, share, middle, per_layer)
        carry_edge(flat, rows_slot)
        grad_out(flat, ctx_ref[...], ea_ref[...])
        grad_qkv(flat, a_ref[...], lin_ref)
        emit_slots(flat, 0, stage, slots_ref, esem, rows_slot, share, 0, middle)
        total.sent()

    outs = [
        ((rows, D), f32),
        ((rows, D), f32),
        ((2, D), f32),
        ((per_layer // 8, 2, 2, 2, rows_slot, LANES), bf16),
    ]
    ins = [length, cotangent, second, q, gains, a1, cos, sin, kv, w_out, w_gu, w_down, w_qkv]
    return pl.pallas_call(
        body,
        out_shape=[jax.ShapeDtypeStruct(s, d) for s, d in outs],
        in_specs=[pl.BlockSpec(memory_space=pltpu.SMEM)] + [vmem_spec()] * 7 + [any_spec()] * 5,
        out_specs=[vmem_spec()] * 3 + [any_spec()],
        scratch_shapes=[
            pltpu.VMEM((cols, 2 * D), bf16),
            pltpu.VMEM((D, D), bf16),
            pltpu.VMEM((D, 2 * FFP), bf16),
            pltpu.VMEM((FFP, D), bf16),
            pltpu.VMEM((D, 3 * D), bf16),
            pltpu.SemaphoreType.DMA((5,)),
            pltpu.VMEM((rows, D), bf16),
            pltpu.VMEM((rows, 3 * D), bf16),
            pltpu.VMEM((rows, cols), f32),
            pltpu.VMEM((HEADS, rows, cols), bf16),
            pltpu.VMEM((rows, D), bf16),
            pltpu.VMEM((rows, D), bf16),
            pltpu.VMEM((rows, 2 * FFP), f32),
            pltpu.VMEM((rows, FFP), bf16),
            pltpu.VMEM((rows, 2 * FFP), bf16),
            pltpu.VMEM((rows, D), bf16),
            pltpu.VMEM((rows, D), bf16),
            pltpu.VMEM((rows, D), bf16),
            pltpu.VMEM((rows, 2 * D), bf16),
            pltpu.VMEM((flat_rows(rows_slot), LANES), f32),
            pltpu.VMEM((6, D, LANES), f32),
            pltpu.VMEM((2, rows_slot, LANES), bf16),
            pltpu.SemaphoreType.DMA((2,)),
        ]
        + key_sum_scratch(rows),
        compiler_params=pltpu.CompilerParams(
            collective_id=3, has_side_effects=True, vmem_limit_bytes=60 * MIB
        ),
    )(*ins)


def lin_grads(eq_ref, ekv_ref, cos_ref, sin_ref, lin_ref):
    for t in range(12):
        col = 128 * t
        src = eq_ref[:, col : col + 128] if t < 4 else ekv_ref[:, col - D : col - D + 128]
        if t < 8:
            w = src.astype(f32)
            src = (w * cos_ref[...] - half_swap(w) * sin_ref[...]).astype(bf16)
        lin_ref[:, col : col + 128] = src


def when(condition):
    if isinstance(condition, bool):
        return (lambda act: act()) if condition else (lambda act: None)
    return pl.when(condition)


class Reduce:
    room_static = 3
    lags = (1, 2, 3)

    def __init__(self, early, late, bufs, fin, send, recv, lsem, free, zn, rows, ahead=2):
        self.early, self.late, self.fin, self.free = early, late, fin, free
        self.acc, self.rc, self.first, self.second, self.rz = bufs
        self.send, self.recv, self.lsem = send, recv, lsem
        self.zn, self.half = zn, zn // 2
        self.static, self.room, self.table = self.plan(zn, rows)
        self.steps = len(self.table)
        self.ahead = ahead
        self.two, self.three, self.hop = self.lags
        self.retired = self.hop + zn - 1
        self.gap = 0 if self.static else max(0, self.retired - self.room) + ahead
        self.turns = self.steps + self.gap + self.retired + 1
        self.z, self.x, self.y, self.c = coords()
        z, x, y, c = self.z, self.x, self.y, self.c
        self.to_x = place(z, 1 - x, y, c)
        self.to_y = place(z, x, 1 - y, c)
        self.to_c = place(z, x, y, 1 - c)

    @classmethod
    def plan(cls, zn, rows):
        if rows // 16 != 98:
            chunk = (0, rows, rows // 32 * 16)
            return False, zn // 2, [(zp, chunk) for zp in range(zn - 1, -1, -1)]
        table = []
        for zp in range(zn - 1, -1, -1):
            base = 0
            for tiles in cls.sizes[min(zp, len(cls.sizes) - 1)]:
                table.append((zp, (base, 16 * tiles, 16 * round(tiles * cls.share_x))))
                base += 16 * tiles
        return True, min(cls.room_static, zn), table

    sizes = ((24, 24, 20, 16, 14), (33, 32, 33), (33, 32, 33), (49, 49))
    share_x = 0.5

    def at(self, k):
        if self.static:
            zp, chunk = self.table[k]
            return zp, zp % self.room, chunk
        zp = self.zn - 1 - k
        return zp, lax.rem(zp, self.room), self.table[0][1]

    def ends(self, k):
        return k + 1 == self.steps or self.table[k + 1][0] != self.table[k][0]

    def opens(self, k):
        return k == 0 or self.table[k - 1][0] != self.table[k][0]

    def last_of(self, zp):
        return max(k for k in range(self.steps) if self.table[k][0] == zp)

    def step_at(self, u):
        if self.static:
            return u
        later = jnp.where(u < self.room + self.gap, -1, u - self.gap)
        return jnp.where(u < self.room, u, later)

    def starts_at(self, k):
        zp = self.table[k][0]
        turn = k - self.ahead
        if zp + self.room < self.zn:
            if not self.static:
                return k + self.gap - self.ahead
            turn = max(turn, self.last_of(zp + self.room) + self.retired)
            assert turn <= k
        return turn

    def limit(self, zp):
        return self.starts_at(min(k for k in range(self.steps) if self.table[k][0] == zp))

    def from_source(self, k, act):
        zp, loc, chunk = self.at(k)
        if isinstance(zp, int):
            act((self.late if zp >= self.half else self.early).at[zp % self.half])
        else:
            index = lax.rem(zp, self.half)
            pl.when(zp >= self.half)(lambda: act(self.late.at[index]))
            pl.when(zp < self.half)(lambda: act(self.early.at[index]))

    def cp(self, src, dst, k, s, r, device):
        return remote(src, dst, self.send.at[k, s], self.recv.at[k, r], device)

    def spans(self, k):
        zp, loc, (base, size, cut) = self.at(k)
        return pl.ds(base, cut), pl.ds(base + cut, size - cut)

    def core(self, k, src=None):
        zp, loc, (base, size, cut) = self.at(k)
        span = pl.ds(base, size)
        src = self.early.at[0] if src is None else src
        return self.cp(
            src.at[1 - self.c, :, :, span], self.rc.at[loc, :, :, span], k, 0, 0, self.to_c
        )

    def load(self, k, src=None):
        zp, loc, (base, size, cut) = self.at(k)
        span = pl.ds(base, size)
        src = self.early.at[0] if src is None else src
        return pltpu.make_async_copy(
            src.at[self.c, :, :, span], self.acc.at[loc, :, :, span], self.lsem.at[k]
        )

    def far_x(self, k):
        zp, loc, chunk = self.at(k)
        span = self.spans(k)[0]
        return self.cp(
            self.acc.at[loc, 1 - self.x, :, span], self.first.at[loc, :, span], k, 1, 1, self.to_x
        )

    def far_y(self, k):
        zp, loc, chunk = self.at(k)
        span = self.spans(k)[1]
        return self.cp(
            self.acc.at[loc, :, 1 - self.y, span], self.first.at[loc, :, span], k, 2, 2, self.to_y
        )

    def then_y(self, k):
        zp, loc, chunk = self.at(k)
        span = self.spans(k)[0]
        src = self.acc.at[loc, self.x, 1 - self.y, span]
        return self.cp(src, self.second.at[loc, span], k, 3, 3, self.to_y)

    def then_x(self, k):
        zp, loc, chunk = self.at(k)
        span = self.spans(k)[1]
        src = self.acc.at[loc, 1 - self.x, self.y, span]
        return self.cp(src, self.second.at[loc, span], k, 4, 4, self.to_x)

    def right(self, k):
        zp, loc, (base, size, cut) = self.at(k)
        span = pl.ds(base, size)
        return self.cp(
            self.acc.at[loc, self.x, self.y, span], self.rz.at[loc, 0, span], k, 5, 5,
            place(self.z + 1, self.x, self.y, self.c),
        )

    def left(self, k):
        zp, loc, (base, size, cut) = self.at(k)
        span = pl.ds(base, size)
        return self.cp(
            self.acc.at[loc, self.x, self.y, span], self.rz.at[loc, 1, span], k, 5, 6,
            place(self.z - 1, self.x, self.y, self.c),
        )

    def add(self, loc, xp, yp, span, src):
        value = self.acc[loc, xp, yp, span, :].astype(f32) + src.astype(f32)
        self.acc[loc, xp, yp, span, :] = value.astype(bf16)

    def ok(self, k):
        return (k >= 0) & (k < self.steps)

    def guard(self, k, act):
        if isinstance(k, int):
            if 0 <= k < self.steps:
                act()
        else:
            pl.when(self.ok(k))(act)

    def neighbours(self, act):
        z, x, y, c = self.z, self.x, self.y, self.c
        for device in (self.to_x, self.to_y, self.to_c):
            act(device)
        pl.when(z > 0)(lambda: act(place(z - 1, x, y, c)))
        pl.when(z < self.zn - 1)(lambda: act(place(z + 1, x, y, c)))

    def stage_core(self, k):
        def act():
            if self.static:
                if self.opens(k) and self.table[k][0] + self.room < self.zn:
                    self.claim(k)
            else:
                pl.when(k >= self.room)(lambda: self.claim(k))
            self.from_source(k, lambda src: self.core(k, src).start())
            self.from_source(k, lambda src: self.load(k, src).start())

        self.guard(k, act)

    def claim(self, k):
        z = self.z
        zp, loc, chunk = self.at(k)
        pl.semaphore_wait(
            self.free.at[loc],
            3 + (z > 0).astype(jnp.int32) + (z < self.zn - 1).astype(jnp.int32),
        )

    def retire(self, k):
        def act():
            zp, loc, chunk = self.at(k)
            for item in (
                self.core(k), self.far_x(k), self.far_y(k), self.then_x(k), self.then_y(k)
            ):
                item.wait_send()
            pl.when(zp > self.z)(lambda: self.right(k).wait_send())
            pl.when(zp < self.z)(lambda: self.left(k).wait_send())

            def tell():
                self.neighbours(
                    lambda d: pl.semaphore_signal(
                        self.free.at[loc], inc=1, device_id=d, device_id_type=MESH
                    )
                )

            if self.static:
                if self.ends(k) and zp >= self.room:
                    tell()
            else:
                pl.when(zp >= self.room)(tell)

        self.guard(k, act)

    def stage_one(self, k):
        def act():
            zp, loc, chunk = self.at(k)
            over_x, over_y = self.spans(k)
            x, y = self.x, self.y
            self.core(k).wait_recv()
            self.load(k).wait()

            def add(xp, yp, span):
                self.add(loc, xp, yp, span, self.rc[loc, xp, yp, span, :])

            add(1 - x, 0, over_x)
            add(1 - x, 1, over_x)
            self.far_x(k).start()
            add(0, 1 - y, over_y)
            add(1, 1 - y, over_y)
            self.far_y(k).start()
            add(x, 0, over_x)
            add(x, 1, over_x)
            add(0, y, over_y)
            add(1, y, over_y)

        self.guard(k, act)

    def stage_two(self, k):
        def act():
            zp, loc, chunk = self.at(k)
            over_x, over_y = self.spans(k)
            x, y = self.x, self.y

            def add(xp, yp, span, row):
                self.add(loc, xp, yp, span, self.first[loc, row, span, :])

            self.far_x(k).wait_recv()
            add(x, 1 - y, over_x, 1 - y)
            self.then_y(k).start()
            self.far_y(k).wait_recv()
            add(1 - x, y, over_y, 1 - x)
            self.then_x(k).start()
            add(x, y, over_x, y)
            add(x, y, over_y, x)

        self.guard(k, act)

    def stage_three(self, k):
        def act():
            zp, loc, (base, size, cut) = self.at(k)
            span = pl.ds(base, size)
            z, x, y = self.z, self.x, self.y
            self.then_y(k).wait_recv()
            self.then_x(k).wait_recv()

            @pl.when(zp == z)
            def _():
                self.fin[span, :] = self.acc[loc, x, y, span, :].astype(f32) + self.second[
                    loc, span, :
                ].astype(f32)

            @pl.when(zp != z)
            def _():
                self.add(loc, x, y, span, self.second[loc, span, :])

            pl.when((zp > z) & (z == 0))(lambda: self.right(k).start())
            pl.when((zp < z) & (z == self.zn - 1))(lambda: self.left(k).start())

        self.guard(k, act)

    def stage_hop(self, k, z, rightward):
        def act():
            zp, loc, (base, size, cut) = self.at(k)
            span = pl.ds(base, size)
            x, y = self.x, self.y
            item = self.right(k) if rightward else self.left(k)
            part = self.rz.at[loc, 0 if rightward else 1, span]

            onward = (zp > z) if rightward else (zp < z)

            @when(onward)
            def _():
                item.wait_recv()
                self.add(loc, x, y, span, part[...])
                item.start()

            @when(zp == z)
            def _():
                item.wait_recv()
                self.fin[span, :] = self.fin[span, :] + part[...].astype(f32)

        self.guard(k, act)

    def stage_four(self, u):
        z, last = self.z, self.zn - 1
        if not self.static:
            @pl.when(z > 0)
            def _():
                self.stage_hop(self.step_at(u - self.hop - (z - 1)), z, True)

            @pl.when(z < last)
            def _():
                self.stage_hop(self.step_at(u - self.hop - (last - z - 1)), z, False)

            return
        for place_z in range(self.zn):
            steps = []
            if place_z > 0:
                k = self.step_at(u - self.hop - (place_z - 1))
                if 0 <= k < self.steps and self.at(k)[0] >= place_z:
                    steps.append((k, True))
            if place_z < last:
                k = self.step_at(u - self.hop - (last - place_z - 1))
                if 0 <= k < self.steps and self.at(k)[0] <= place_z:
                    steps.append((k, False))
            if steps:

                @pl.when(z == place_z)
                def _(steps=steps, place_z=place_z):
                    for k, rightward in steps:
                        self.stage_hop(k, place_z, rightward)

    def begin(self):
        for k in range(min(self.ahead, self.steps)):
            self.stage_core(k)

    def turn(self, u):
        self.retire(self.step_at(u - self.retired))
        if self.static:
            for j in range(self.ahead, self.steps):
                if self.starts_at(j) == u:
                    self.stage_core(j)
        else:
            k = self.step_at(u + self.ahead)
            pl.when(k >= self.ahead)(lambda: self.stage_core(k))
        self.stage_one(self.step_at(u))
        self.stage_two(self.step_at(u - self.two))
        self.stage_three(self.step_at(u - self.three))
        self.stage_four(u)

    def pump(self, low, high):
        if self.static:
            for k in range(low, high):
                self.turn(k)
        elif high > low:

            def one(k, carry):
                self.turn(k)
                return carry

            lax.fori_loop(low, high, one, 0)


def stage_last(
    e2, r1, r2, gains, hidden, q, ctx, b_low, units, cos, sin, gains_one, master, one, two,
    slots_one, p, both, kv, w_gu, w_down, w_out, w_qkv, zn, rows_slot, share,
):
    rows = e2.shape[0]
    cols = kv.shape[0]
    ndev = zn * 8
    per_layer = ndev // 2
    half_zn = zn // 2
    step = chunk_rows(rows_slot)
    turns = rows_slot // step
    middle = split_slot(share)
    static, room, table = Reduce.plan(zn, rows_slot)
    steps = len(table)

    def body(
        e2_ref, r1_ref, r2_ref, g_ref, c_ref, s_ref, g1_ref, b_ref,
        s1_any, p_any, both_any, kv_any, gu_any, dn_any, wo_any, wq_any,
        h_any, q_any, ctx_any, units_any, m_any, one_any, two_any,
        ig_ref, nm_ref, n1_ref, n2_ref, nw_ref, gn_ref, gg_ref, s0_any,
        p_ref, both_ref, kv_ref, gu_ref, dn_ref, wo_ref, wq_ref,
        h_ref, q_ref, ctx_ref, units_ref, m_ref, one_ref, two_ref, load_sem,
        eboth_ref, ef_ref, ea_ref, ectx_ref, eq_ref, ekv_ref, lin_ref,
        flat, ring, stage, esem,
        acc, rc, first_buf, second_buf, rz, fin, sq, sqs,
        send, recv, lsem, ssem, rsem, free,
        dkv_ref, from_c, pair, from_y, ksend, krecv,
    ):
        z, x, y, c = coords()
        me = ((z * 2 + x) * 2 + y) * 2 + c
        bar = pltpu.get_barrier_semaphore()

        def peer(d):
            tgt = lax.rem(me + d, ndev)
            return {"dp": lax.div(tgt, 4), "sp": lax.rem(tgt, 4)}

        def hello(d, carry):
            pl.semaphore_signal(bar, inc=1, device_id=peer(d), device_id_type=MESH)
            return carry

        lax.fori_loop(1, ndev, hello, 0)
        loads = Loads(
            [
                (gu_any, gu_ref), (dn_any, dn_ref), (both_any, both_ref), (wo_any, wo_ref),
                (kv_any, kv_ref), (p_any, p_ref), (wq_any, wq_ref),
                (units_any, units_ref), (q_any, q_ref), (ctx_any, ctx_ref), (h_any, h_ref),
                (m_any, m_ref), (one_any, one_ref), (two_any, two_ref),
            ],
            load_sem,
        )
        bufs = (acc, rc, first_buf, second_buf, rz)
        stream = Reduce(s0_any, s1_any, bufs, fin, send, recv, lsem, free, zn, rows_slot)
        total = KeySum(dkv_ref, ekv_ref, from_c, pair, from_y, ksend, krecv)
        pl.semaphore_wait(bar, ndev - 1)
        stream.begin()
        done = [0]

        def pump(until):
            if until > done[0]:
                stream.pump(done[0], until)
                done[0] = until

        first_limit = stream.limit(half_zn - 1)
        second_limit = stream.limit((middle + 7) // 8 - 1)

        def ahead(part):
            pump(min(int(first_limit * part), first_limit))

        r2 = r2_ref[...]
        er2, gain2 = norm_back(e2_ref[...], r2, norm_factor(r2), g_ref[1:2, :])
        sq[12:16, :] = gain2.reshape(4, LANES)
        sq[16:24, :] = g1_ref[...].reshape(8, LANES)
        ef_ref[...] = er2.astype(bf16)
        loads.wait(0, 1, 2)
        ahead(0.1)
        e_first = er2 + feed_back(ef_ref[...], gu_ref, dn_ref, both_ref, eboth_ref)
        ahead(0.25)
        r1 = r1_ref[...]
        er1, gain1 = norm_back(e_first, r1, norm_factor(r1), g_ref[0:1, :])
        sq[8:12, :] = gain1.reshape(4, LANES)
        ig_ref[...] = er1
        ea_ref[...] = er1.astype(bf16)
        for t in range(TILES):
            grad_gate_up(flat, ring, t, b_ref[...], eboth_ref)
            if t % 3 == 2:
                ahead(0.25 + 0.15 * (t // 3 + 1))
        loads.wait(7)
        grad_down(flat, units_ref[...], ef_ref[...])
        grad_gains(flat, gain1, gain2)
        ahead(0.8)
        emit_slots(flat, BASE_GU, stage, s0_any, esem, rows_slot, share, middle, per_layer)
        loads.wait(3, 4, 5, 8)
        ectx_ref[...] = mm_nt(ea_ref[...], wo_ref[...]).astype(bf16)
        pump(first_limit)
        pairs = HEADS // 2
        for i in range(pairs):
            attend_back(i, q_ref, kv_ref, p_ref, ectx_ref, eq_ref, dkv_ref)
            total.start(i)
            if i >= 1:
                total.middle(i - 1)
            pump(first_limit + (second_limit - first_limit) * (i + 1) // (2 * pairs))
        total.middle(pairs - 1)
        carry_edge(flat, rows_slot)
        loads.wait(9, 10)
        grad_out(flat, ctx_ref[...], ea_ref[...])
        for i in range(pairs):
            total.end(i)
        pump(first_limit + (second_limit - first_limit) * 3 // 4)
        lin_grads(eq_ref, ekv_ref, c_ref, s_ref, lin_ref)
        grad_qkv(flat, h_ref[...], lin_ref)
        emit_slots(flat, 0, stage, s0_any, esem, rows_slot, share, 0, middle)
        pump(second_limit + 2)
        loads.wait(6, 11, 12, 13)
        ig_ref[...] = ig_ref[...] + mm_nt(lin_ref[...], wq_ref[...])
        pump(stream.turns)

        fin[pl.ds(rows_slot, 8), :] = jnp.zeros((8, LANES), f32)
        shift = lax.rem(share * me, LANES)
        back = lax.rem(LANES - shift, LANES)
        lane = lax.broadcasted_iota(jnp.int32, (step, LANES), 1)
        row = lax.broadcasted_iota(jnp.int32, (step, LANES), 0)

        def realign(i, carry):
            now = pltpu.roll(fin[pl.ds(i * step, step), :], back, 1)
            after = pltpu.roll(fin[pl.ds(i * step + 1, step), :], back, 1)
            value = jnp.where(lane < LANES - shift, now, after)
            value = jnp.where((row + i * step) * LANES + lane < share, value, 0.0)
            n1_ref[pl.ds(i * step, step), :] = value
            square = value * value
            return carry + jnp.sum(square.reshape(step // 8, 8, LANES), axis=0)

        sq[0:8, :] = lax.fori_loop(0, turns, realign, jnp.zeros((8, LANES), f32))

        def tell(d, carry):
            remote(sq, sqs.at[me], ssem, rsem, peer(d)).start()
            return carry

        lax.fori_loop(1, ndev, tell, 0)
        sqs[me] = sq[...]
        total.sent()
        part = sqs.at[pl.ds(0, ndev - 1)]
        both = remote(part, part, ssem, rsem, stream.to_c)
        both.wait_send()
        both.wait_recv()
        sums = lax.fori_loop(1, ndev, lambda i, s: s + sqs[i], sqs[0])
        gg_ref[...] = sums[8:24, :]
        squares = sums[0:8, :]
        norm = jnp.sqrt(jnp.sum(squares, keepdims=True))
        gn_ref[...] = jnp.broadcast_to(norm, (8, LANES))
        scale = jnp.minimum(1.0, 1.0 / norm)
        correction = 1.0 - 0.5**STEP

        def update(i, carry):
            span = pl.ds(pl.multiple_of(i * step, 16), step)
            clipped = n1_ref[span, :] * scale
            new_one = 0.5 * one_ref[span, :] + 0.5 * clipped
            new_two = 0.5 * two_ref[span, :] + 0.5 * clipped * clipped
            n1_ref[span, :] = new_one
            n2_ref[span, :] = new_two
            new_master = m_ref[pl.ds(8 + i * step, step), :] * (
                1.0 - LEARN_RATE * DECAY_RATE
            ) - LEARN_RATE * (new_one / correction) / (jnp.sqrt(new_two / correction) + ADAM_EPS)
            nm_ref[span, :] = new_master
            nw_ref[span, :] = new_master.astype(bf16)
            return carry

        lax.fori_loop(0, turns, update, 0)

    slot_flat = ((rows_slot, LANES), f32)
    outs = [
        ((rows, D), f32),
        slot_flat,
        slot_flat,
        slot_flat,
        ((rows_slot, LANES), bf16),
        ((8, LANES), f32),
        ((16, LANES), f32),
        ((per_layer // 8, 2, 2, 2, rows_slot, LANES), bf16),
    ]
    small = [e2, r1, r2, gains, cos, sin, gains_one, b_low]
    late = [hidden, q, ctx, units, master, one, two]
    large = [slots_one, p, both, kv, w_gu, w_down, w_out, w_qkv] + late
    act = pltpu.VMEM((rows, D), bf16)
    return pl.pallas_call(
        body,
        out_shape=[jax.ShapeDtypeStruct(s, d) for s, d in outs],
        in_specs=[vmem_spec()] * len(small) + [any_spec()] * len(large),
        out_specs=[vmem_spec()] * 7 + [any_spec()],
        scratch_shapes=[
            pltpu.VMEM(p.shape, bf16),
            pltpu.VMEM(both.shape, f32),
            pltpu.VMEM(kv.shape, bf16),
            pltpu.VMEM(w_gu.shape, bf16),
            pltpu.VMEM(w_down.shape, bf16),
            pltpu.VMEM(w_out.shape, bf16),
            pltpu.VMEM(w_qkv.shape, bf16),
        ]
        + [pltpu.VMEM(v.shape, v.dtype) for v in late]
        + [
            pltpu.SemaphoreType.DMA((14,)),
            pltpu.VMEM((rows, 2 * FFP), bf16),
            act,
            act,
            act,
            act,
            pltpu.VMEM((rows, 2 * D), bf16),
            pltpu.VMEM((rows, 3 * D), bf16),
            pltpu.VMEM((flat_rows(rows_slot), LANES), f32),
            pltpu.VMEM((6, D, LANES), f32),
            pltpu.VMEM((2, rows_slot, LANES), bf16),
            pltpu.SemaphoreType.DMA((2,)),
            pltpu.VMEM((room, 2, 2, rows_slot, LANES), bf16),
            pltpu.VMEM((room, 2, 2, rows_slot, LANES), bf16),
            pltpu.VMEM((room, 2, rows_slot, LANES), bf16),
            pltpu.VMEM((room, rows_slot, LANES), bf16),
            pltpu.VMEM((room, 2, rows_slot, LANES), bf16),
            pltpu.VMEM((rows_slot + 8, LANES), f32),
            pltpu.VMEM((24, LANES), f32),
            pltpu.VMEM((ndev, 24, LANES), f32),
            pltpu.SemaphoreType.DMA((steps, 6)),
            pltpu.SemaphoreType.DMA((steps, 7)),
            pltpu.SemaphoreType.DMA((steps,)),
            pltpu.SemaphoreType.DMA,
            pltpu.SemaphoreType.DMA,
            pltpu.SemaphoreType.REGULAR((room,)),
        ]
        + key_sum_scratch(rows),
        compiler_params=pltpu.CompilerParams(
            collective_id=4, has_side_effects=True, vmem_limit_bytes=63 * MIB
        ),
    )(*small, *large)


def rope_rows(rows):
    frequency = jnp.exp(
        -jnp.log(10000.0) * jnp.arange(HEAD_DIM // 2).astype(f32) * 2.0 / HEAD_DIM
    )
    positions = lax.axis_index("sp") * rows + jnp.arange(rows)
    angles = positions.astype(f32)[:, None] * jnp.tile(frequency, 4)[None, :]
    first = lax.rem(jnp.arange(LANES), HEAD_DIM) < HEAD_DIM // 2
    sin = jnp.sin(angles)
    return jnp.cos(angles), jnp.where(first[None, :], -sin, sin)


def step_shard(dp_size, sp_size, hidden_in, cotangent, lengths, master, moment_one, moment_two):
    share = master.shape[0]
    zn = dp_size // 2
    per_layer = dp_size * sp_size // 2
    rows = -(-(-(-share // LANES) + 1) // 32) * 32
    seqs, tokens, width = hidden_in.shape

    def pad(flat, lead):
        return jnp.pad(flat, (lead * LANES, rows * LANES - share)).reshape(rows + lead, LANES)

    master_pad = pad(master, 8)
    cos, sin = rope_rows(tokens)
    hidden = hidden_in.reshape(tokens, width)

    (
        g0, g1, q0, ctx0, r1, b0, units0, r2, second, a1, q1,
        wq0, wo0, wg0, wd0, wq1, wo1, wg1, wd1, kv0, kv1, p0, both0,
    ) = stage_head(lengths, master_pad, hidden, cos, sin, zn, rows, share)
    output, e2, gains_one, slots_one = stage_second(
        lengths, cotangent.reshape(tokens, width), second, q1, kv1, wo1, wg1, wd1, wq1, g1, a1,
        cos, sin, share, rows,
    )
    input_grad, new_master, new_one, new_two, new_weights, norm, gains, _ = stage_last(
        e2, r1, r2, g0, hidden, q0, ctx0, b0, units0, cos, sin, gains_one,
        master_pad, pad(moment_one, 0), pad(moment_two, 0),
        slots_one, p0, both0, kv0, wg0, wd0, wo0, wq0, zn, rows, share,
    )

    def flat(value):
        return value.reshape(-1)[:share]

    return (
        output.reshape(hidden_in.shape),
        input_grad.reshape(hidden_in.shape),
        flat(new_master),
        flat(new_one),
        flat(new_two),
        flat(new_weights),
        norm[0, 0],
        gains.reshape(2, 2, width),
    )


def solution(mesh):
    in_specs = (
        P("dp", "sp", None),
        P("dp", "sp", None),
        P("dp"),
        P(("dp", "sp")),
        P(("dp", "sp")),
        P(("dp", "sp")),
    )
    out_specs = (
        P("dp", "sp", None),
        P("dp", "sp", None),
        P(("dp", "sp")),
        P(("dp", "sp")),
        P(("dp", "sp")),
        P(("dp", "sp")),
        P(),
        P(),
    )
    body = functools.partial(step_shard, mesh.shape["dp"], mesh.shape["sp"])
    return jax.shard_map(body, mesh=mesh, in_specs=in_specs, out_specs=out_specs, check_vma=False)
```
